32 devices in a mesh: dp: 8 (over y, x, core), tensor: 4 (over z).
Axes of the slice: x: 2, y: 2, z: 4, core: 2. Of those that a mesh axis runs over, the one named last changes fastest.
Arguments:
- tokens: bfloat16 [2, 8, 1024, 1024], P(None, 'dp', 'tensor'), may hold values from -6 to 6
- block_ids: int32 [2, 8, 1024], P(None, 'dp'), may hold values from 0 to 7, never falling along the last dimension, each value on 1 to 256 neighbouring positions
- routes: int32 [2, 8, 1024, 1], P(None, 'dp'), may hold values from 0 to 31; in each aligned block of 1024 rows (0 to 1023, 1024 to 2047, ..., all dimensions but the last counted through in order) at most 48 rows name the same one
- cotangent: bfloat16 [2, 8, 1024, 1024], P(None, 'dp', 'tensor'), may hold values from -6 to 6
- ln1_gain: float32 [1024], replicated, may hold values from 0.5 to 1.5
- ln1_bias: float32 [1024], replicated, may hold values from -0.6 to 0.6
- w_qkv: bfloat16 [1024, 3, 1024], P('dp', None, 'tensor'), may hold values from -0.25 to 0.25
- w_out: bfloat16 [1024, 1024], P('tensor', 'dp'), may hold values from -0.75 to 0.75
- ln2_gain: float32 [1024], replicated, may hold values from 0.5 to 1.5
- ln2_bias: float32 [1024], replicated, may hold values from -0.6 to 0.6
- router: bfloat16 [1024, 32], replicated, may hold values from -0.125 to 0.125
- w_up: bfloat16 [32, 1024, 4096], P('dp', None, 'tensor'), may hold values from -0.1875 to 0.1875
- w_down: bfloat16 [32, 4096, 1024], P('dp', 'tensor'), may hold values from -6 to 6
Outputs:
- out: bfloat16 [2, 8, 1024, 1024], P(None, 'dp', 'tensor')
- grad_tokens: float32 [2, 8, 1024, 1024], P(None, 'dp', 'tensor')
- grad_ln1_gain: float32 [1024], replicated
- grad_ln1_bias: float32 [1024], replicated
- grad_qkv: float32 [1024, 3, 1024], P('dp', None, 'tensor')
- grad_out: float32 [1024, 1024], P('tensor', 'dp')
- grad_ln2_gain: float32 [1024], replicated
- grad_ln2_bias: float32 [1024], replicated
- grad_router: float32 [1024, 32], replicated
- grad_up: float32 [32, 1024, 4096], P('dp', None, 'tensor')
- grad_down: float32 [32, 4096, 1024], P('dp', 'tensor')
The draws below stay inside these ranges and needn't reach their ends.
Inputs may be any that keep to these rules, and one draw needn't show every extreme that they name: `routes`: within one sequence at most 48 tokens name the same expert, and in every draw some expert is named by exactly 48 tokens of some sequence. `block_ids`: within each sequence the ids never fall; each id covers 1 to 256 consecutive positions, and some id covers exactly 256.
All inputs are finite; a program needn't handle non-finite values.
Results may differ from the reference program's by a relative error of at most 0.024.
Values may be sent and summed in bfloat16 or wider, within the bound.
A program may use at most 256 MiB of HBM per device.

```python
import math
import jax
import jax.numpy as jnp
import numpy as np
from jax import lax

MODEL_DIMENSION = 1024
HEADS = 16
HEAD_DIM = 64
FFN = 4096
SEQUENCE_TOKENS = 1024
BLOCK = 256
MICRO = 2
SEQS = 8
EXPERTS = 32
CAP = 48


def level_of(rng, shape, pieces, smallest, top_value):
    factor_of = 1.0
    for dim, parts in pieces:
        heights = jax.random.uniform(jax.random.fold_in(jax.random.fold_in(rng, 6), dim), (parts,), jnp.float32, smallest / len(pieces), top_value / len(pieces))
        factor_of = factor_of * jnp.repeat(jnp.exp(heights), shape[dim] // parts).reshape((-1,) + (1,) * (len(shape) - 1 - dim))
    return factor_of


def split_up(number_of, total, most, slope):
    weights = [(1 << 20) // math.isqrt(grade ** slope) + 1 for grade in range(2, number_of + 1)]
    spare, counts = total - most - (number_of - 1), [1] * (number_of - 1)
    while spare > 0:
        free = [i for i in range(number_of - 1) if counts[i] < most]
        whole, left = sum([weights[i] for i in free]), spare
        for i in free:
            addition = min(most - counts[i], max(1, left * weights[i] // whole), spare)
            counts[i] = counts[i] + addition
            spare = spare - addition
    return np.array([most] + counts)


def uneven(key, count, total, bound, lean):
    if count == 2:
        one = jax.random.randint(key, (), max(1, total - bound), min(bound, total - 1) + 1)
        return jnp.stack([one, total - one])
    sizes = jnp.asarray(split_up(count, total, bound, lean), jnp.int32)
    couples = (count - 1) // 2
    source_of, receiver = sizes[1:1 + 2 * couples:2], sizes[2:2 + 2 * couples:2]
    room = jnp.minimum(source_of - 1, bound - receiver)
    shifted = jax.random.randint(jax.random.fold_in(key, 1), (couples,), 0, 1 << 20) % (room + 1)
    sizes = sizes.at[1:1 + 2 * couples:2].set(source_of - shifted).at[2:2 + 2 * couples:2].set(receiver + shifted)
    return sizes[jax.random.permutation(jax.random.fold_in(key, 2), count)]


def shared_out(own_key, own, number, rows, amount, top, reach, skew):
    order = jax.random.permutation(own_key, amount)
    crowded, usual = shares(amount, rows * top, reach, skew, True), shares(amount, rows * top, reach, skew, False)
    places = jnp.arange(amount)

    def named(tallies, rotation):
        used = int((tallies > 0).sum())
        fixed = max(1, used // 4)
        passed = fixed + (places - fixed + rotation * (used - fixed)) % max(1, amount - fixed)
        return jnp.zeros((amount,), jnp.int32).at[order[jnp.where(places < fixed, places, passed)]].set(jnp.asarray(tallies, jnp.int32))

    tallies = jnp.where(number % 4 == 0, named(crowded, number // 4), named(usual, number - number // 4 - 1))
    mixed = jax.random.permutation(jax.random.fold_in(own, 3), amount)
    giver, taker = mixed[0:amount // 2 * 2:2], mixed[1:amount // 2 * 2:2]
    room = jnp.minimum(tallies[giver] - 1, reach - tallies[taker]) // 2
    room = jnp.where((giver == order[0]) | (taker == order[0]) | (tallies[taker] == 0), 0, jnp.maximum(room, 0))
    passed = jax.random.randint(jax.random.fold_in(own, 4), (amount // 2,), 0, 1 << 20) % (room + 1)
    tallies = tallies.at[giver].add(-passed).at[taker].add(passed)
    members = jnp.searchsorted(jnp.cumsum(tallies), jnp.arange(rows * top), side="right").astype(jnp.int32)
    grid = members.reshape(top, rows).T
    grid = grid[jax.random.permutation(jax.random.fold_in(own, 1), rows)]
    rotation = jax.random.randint(jax.random.fold_in(own, 2), (rows, 1), 0, top)
    return jnp.take_along_axis(grid, (jnp.arange(top)[None, :] + rotation) % top, axis=1)


def shares(amount, total, limit, skew, full):
    portions = [(1 << 20) // math.isqrt(standing ** skew) + 1 for standing in range(1, amount + 1)]
    largest = limit if full else min(limit, max(-(-total // amount), total * portions[0] // sum(portions)))
    least = 1 if total - largest >= amount - 1 else 0
    holding, surplus = [largest] + [least] * (amount - 1), total - largest - least * (amount - 1)
    while surplus > 0:
        free = [i for i in range(1, amount) if holding[i] < largest] or [i for i in range(1, amount) if holding[i] < limit]
        pool, budget = sum([portions[i] for i in free]), surplus
        for i in free:
            more = min(limit - holding[i], max(1, budget * portions[i] // pool), surplus)
            holding[i] = holding[i] + more
            surplus = surplus - more
    return np.array(holding)


def normal_values(rng, dims, deviation, most, cuts=(), kind=jnp.bfloat16):
    factor_of = level_of(rng, dims, cuts, -0.22, 0.18) if cuts else 1.0
    values = jax.random.normal(rng, dims, jnp.float32) * deviation * factor_of
    return jnp.minimum(jnp.maximum(values, -most), most).astype(kind)


def setup_inputs(seed: int = 0) -> dict:
    keys = jax.random.split(jax.random.key(seed), 14)
    tokens = normal_values(keys[0], (MICRO, SEQS, SEQUENCE_TOKENS, MODEL_DIMENSION), 1.0, 6.0, ((1, 8), (2, 4)))
    block_ids = jax.vmap(lambda own: jnp.searchsorted(jnp.cumsum(uneven(own, 2 * SEQUENCE_TOKENS // BLOCK, SEQUENCE_TOKENS, BLOCK, 2)), jnp.arange(SEQUENCE_TOKENS), side="right"))(jax.random.split(keys[1], MICRO * SEQS)).reshape((MICRO, SEQS, SEQUENCE_TOKENS)).astype(jnp.int32)
    routes_keys = jax.random.split(jax.random.fold_in(keys[2], 1), MICRO * SEQS * SEQUENCE_TOKENS // SEQUENCE_TOKENS)
    routes_turns = jax.random.permutation(jax.random.fold_in(keys[2], 3), MICRO * SEQS * SEQUENCE_TOKENS // SEQUENCE_TOKENS)
    routes = jax.vmap(lambda own, number: shared_out(jax.random.fold_in(keys[2], 2), own, number, SEQUENCE_TOKENS, EXPERTS, 1, CAP, 2))(routes_keys, routes_turns).reshape((MICRO, SEQS, SEQUENCE_TOKENS, 1))
    cotangent = normal_values(keys[3], (MICRO, SEQS, SEQUENCE_TOKENS, MODEL_DIMENSION), 1.0, 6.0, ((1, 8), (2, 4)))
    ln1_gain = jnp.clip(1.0 + 0.1 * jax.random.normal(keys[4], (MODEL_DIMENSION,), jnp.float32), 0.5, 1.5)
    ln1_bias = normal_values(keys[5], (MODEL_DIMENSION,), 0.1, 0.6, (), jnp.float32)
    w_qkv = normal_values(keys[6], (MODEL_DIMENSION, 3, MODEL_DIMENSION), (MODEL_DIMENSION // 2) ** -0.5, 0.25, ((0, 8), (2, 4)))
    w_out = normal_values(keys[7], (MODEL_DIMENSION, MODEL_DIMENSION), (MODEL_DIMENSION // 16) ** -0.5, 0.75, ((0, 4), (1, 8)))
    ln2_gain = jnp.clip(1.0 + 0.1 * jax.random.normal(keys[8], (MODEL_DIMENSION,), jnp.float32), 0.5, 1.5)
    ln2_bias = normal_values(keys[9], (MODEL_DIMENSION,), 0.1, 0.6, (), jnp.float32)
    router = normal_values(keys[10], (MODEL_DIMENSION, EXPERTS), (2 * MODEL_DIMENSION) ** -0.5, 0.125)
    w_up = normal_values(keys[11], (EXPERTS, MODEL_DIMENSION, FFN), MODEL_DIMENSION ** -0.5, 0.1875, ((0, 8), (2, 4)))
    w_down = normal_values(keys[12], (EXPERTS, FFN, MODEL_DIMENSION), 1 ** -0.5, 6.0, ((0, 8), (1, 4)))
    return {"tokens": tokens, "block_ids": block_ids, "routes": routes, "cotangent": cotangent, "ln1_gain": ln1_gain, "ln1_bias": ln1_bias, "w_qkv": w_qkv, "w_out": w_out, "ln2_gain": ln2_gain, "ln2_bias": ln2_bias, "router": router, "w_up": w_up, "w_down": w_down}


EPSILON = 1e-05
MASKED_SCORE = -1e+30
EXACT_PRECISION = lax.Precision.HIGHEST

@jax.custom_vjp
def low(v):
    return lax.optimization_barrier(v.astype(jnp.bfloat16)).astype(jnp.float32)

@jax.custom_vjp
def reduced_backward(v):
    return v

def low_keep(v):
    return (low(v), None)

def low_pass(kept, grad):
    return (grad,)

def back_keep(v):
    return (v, None)

def back_low(kept, grad):
    return (low(grad),)
low.defvjp(low_keep, low_pass)
reduced_backward.defvjp(back_keep, back_low)

def reduced_everywhere(values_in):
    return reduced_backward(low(values_in))

def layer_norm(stream, gain_vec, bias_vec):
    centre = stream - lax.optimization_barrier(jnp.mean(stream, -1, keepdims=True))
    variance = lax.optimization_barrier(jnp.mean(centre * centre, -1, keepdims=True))
    return centre * lax.rsqrt(variance + EPSILON) * gain_vec + bias_vec

def attend_block(query_block, segment_block, key_rows, value_rows, segments):
    scores = reduced_backward(jnp.einsum('qhd,khd->hqk', query_block, key_rows, precision=EXACT_PRECISION) * HEAD_DIM ** (-0.5))
    visible = segments[None, None, :] <= segment_block[None, :, None]
    scores = jnp.where(visible, scores, MASKED_SCORE)
    row_max = lax.optimization_barrier(jnp.max(scores, -1, keepdims=True))
    weights_exp = jnp.exp(scores - row_max)
    prob_rows = low(weights_exp / lax.optimization_barrier(jnp.sum(weights_exp, -1, keepdims=True)))
    return reduced_everywhere(jnp.einsum('hqk,khd->qhd', prob_rows, value_rows, precision=EXACT_PRECISION))

def attend_sequence(queries, key_rows, value_rows, segments):
    length = queries.shape[0]
    block_rows = min(512, length)
    block_count = length // block_rows
    checked = jax.checkpoint(attend_block)
    mixture_output = lax.map(lambda element: checked(element[0], element[1], key_rows, value_rows, segments), (queries.reshape(block_count, block_rows, HEADS, HEAD_DIM), segments.reshape(block_count, block_rows)))
    return mixture_output.reshape(length, HEADS, HEAD_DIM)

def expert_apply(slot_token, up_weight, down_weight, row_data):
    picked = jnp.take(row_data, slot_token, axis=0, mode='fill', fill_value=0.0)
    up_act = reduced_backward(jnp.dot(picked, up_weight, precision=EXACT_PRECISION))
    hidden = low(jax.nn.gelu(up_act, approximate=True))
    return jnp.dot(hidden, down_weight, precision=EXACT_PRECISION)

def reference(tokens, block_ids, routes, cotangent, ln1_gain, ln1_bias, w_qkv, w_out, ln2_gain, ln2_bias, router, w_up, w_down):
    sequence_count = MICRO * SEQS
    segments = block_ids.reshape(sequence_count, SEQUENCE_TOKENS)
    expert_ids = routes.reshape(sequence_count, SEQUENCE_TOKENS)
    onehot = (expert_ids[:, :, None] == jnp.arange(EXPERTS, dtype=jnp.int32)[None, None, :]).astype(jnp.int32)
    slot_pos = lax.optimization_barrier(jnp.sum((jnp.cumsum(onehot, 1) - onehot) * onehot, 2))
    seq_index = jnp.arange(sequence_count, dtype=jnp.int32)[:, None]
    dest_index = (expert_ids * (sequence_count * CAP) + seq_index * CAP + slot_pos).reshape(-1)
    token_index = (seq_index * SEQUENCE_TOKENS + jnp.arange(SEQUENCE_TOKENS, dtype=jnp.int32)[None, :]).reshape(-1)
    slot_token = jnp.full((EXPERTS * sequence_count * CAP,), sequence_count * SEQUENCE_TOKENS, jnp.int32).at[dest_index].set(token_index)
    slot_token = slot_token.reshape(EXPERTS, sequence_count * CAP)
    pick_table = onehot.astype(jnp.float32)

    def forward(stream, gain_one, bias_one, query_key_value_weight, output_matrix, gain_two, bias_two, router_matrix, up_weights, down_weights):
        stream = stream.reshape(sequence_count, SEQUENCE_TOKENS, MODEL_DIMENSION)
        first_normalized = low(layer_norm(stream, gain_one, bias_one))
        query_key_value_rows = reduced_everywhere(jnp.einsum('ome,enq->omnq', first_normalized, query_key_value_weight, precision=EXACT_PRECISION))
        queries = query_key_value_rows[:, :, 0].reshape(sequence_count, SEQUENCE_TOKENS, HEADS, HEAD_DIM)
        key_rows = query_key_value_rows[:, :, 1].reshape(sequence_count, SEQUENCE_TOKENS, HEADS, HEAD_DIM)
        value_rows = query_key_value_rows[:, :, 2].reshape(sequence_count, SEQUENCE_TOKENS, HEADS, HEAD_DIM)
        mixture_output = lax.map(lambda element: attend_sequence(element[0], element[1], element[2], element[3]), (queries, key_rows, value_rows, segments))
        attention_result = reduced_backward(jnp.einsum('ajk,kq->ajq', mixture_output.reshape(sequence_count, SEQUENCE_TOKENS, MODEL_DIMENSION), output_matrix, precision=EXACT_PRECISION))
        stream_one = stream + attention_result
        second_normalized = low(layer_norm(stream_one, gain_two, bias_two))
        router_scores = reduced_backward(jnp.einsum('mza,aq->mzq', second_normalized, router_matrix, precision=EXACT_PRECISION))
        row_max = lax.optimization_barrier(jnp.max(router_scores, -1, keepdims=True))
        weights_exp = jnp.exp(router_scores - row_max)
        probs_router = weights_exp / lax.optimization_barrier(jnp.sum(weights_exp, -1, keepdims=True))
        gate_val = lax.optimization_barrier(jnp.sum(probs_router * pick_table, -1))
        row_data = second_normalized.reshape(sequence_count * SEQUENCE_TOKENS, MODEL_DIMENSION)
        checked = jax.checkpoint(expert_apply)
        results = lax.map(lambda element: checked(element[0], element[1], element[2], row_data), (slot_token, up_weights, down_weights))
        expert_out = reduced_backward(jnp.take(results.reshape(-1, MODEL_DIMENSION), dest_index, axis=0).reshape(sequence_count, SEQUENCE_TOKENS, MODEL_DIMENSION))
        final = stream_one + gate_val[:, :, None] * expert_out
        return final.reshape(MICRO, SEQS, SEQUENCE_TOKENS, MODEL_DIMENSION)
    primals = (tokens.astype(jnp.float32), ln1_gain.astype(jnp.float32), ln1_bias.astype(jnp.float32), w_qkv.astype(jnp.float32), w_out.astype(jnp.float32), ln2_gain.astype(jnp.float32), ln2_bias.astype(jnp.float32), router.astype(jnp.float32), w_up.astype(jnp.float32), w_down.astype(jnp.float32))
    final, pullback = jax.vjp(forward, *primals)
    grads = pullback(cotangent.astype(jnp.float32))
    return (final.astype(jnp.bfloat16), grads[0], grads[1], grads[2], grads[3], grads[4], grads[5], grads[6], grads[7], grads[8], grads[9])
```

```python
import functools

import jax
import jax.numpy as jnp
from jax import lax
from jax.experimental import pallas as pl
from jax.experimental.pallas import tpu as pltpu
from jax.sharding import PartitionSpec as P

HEAD_DIM = 64
LANES = 128
BLOCK = 256
EPSILON = 1e-05
MASKED_SCORE = -1e30
F32 = jnp.float32
BF16 = jnp.bfloat16
NT = (((1,), (1,)), ((), ()))
TN = (((0,), (0,)), ((), ()))
VMEM_LIMIT = 60 * 1024 * 1024


def norm_parts(stream):
    centre = stream - jnp.mean(stream, -1, keepdims=True)
    inv_std = lax.rsqrt(jnp.mean(centre * centre, -1, keepdims=True) + EPSILON)
    return centre * inv_std, inv_std


def norm_backward(grad_normed, normed, inv_std, gain_vec):
    grad_hat = grad_normed * gain_vec
    mean_grad = jnp.mean(grad_hat, -1, keepdims=True)
    mean_cross = jnp.mean(grad_hat * normed, -1, keepdims=True)
    return inv_std * (grad_hat - mean_grad - normed * mean_cross)


def dot32(a, b):
    return jnp.dot(a, b, preferred_element_type=F32)


def head_masks(rows):
    lane = lax.broadcasted_iota(jnp.int32, (rows, LANES), 1)
    return [(lane // HEAD_DIM) == h for h in range(LANES // HEAD_DIM)]


def exp_rows(scores):
    row_max = jnp.max(scores, -1, keepdims=True)
    return jnp.exp(scores - row_max)


def attend_kernel(seg_col, seg_row, q_ref, k_ref, v_ref, o_ref, *, length, scaling):
    masks = head_masks(BLOCK)
    for i in range(length // BLOCK):
        lo, hi = i * BLOCK, min(length, (i + 2) * BLOCK)
        rows = pl.ds(lo, BLOCK)
        visible = seg_row[:, lo:hi] <= seg_col[rows, :]
        q = q_ref[rows, :]
        outs = []
        for mask in masks:
            qm = jnp.where(mask, q * scaling, 0).astype(BF16)
            near = lax.dot_general(qm, k_ref[lo:hi, :], NT, preferred_element_type=F32)
            near = jnp.where(visible, near, MASKED_SCORE)
            top = jnp.max(near, -1, keepdims=True)
            if i:
                far = lax.dot_general(qm, k_ref[0:lo, :], NT, preferred_element_type=F32)
                top = jnp.maximum(top, jnp.max(far, -1, keepdims=True))
            near = jnp.exp(near - top)
            total = jnp.sum(near, -1, keepdims=True)
            if i:
                far = jnp.exp(far - top)
                total = total + jnp.sum(far, -1, keepdims=True)
            inv = 1.0 / total
            out = dot32((near * inv).astype(BF16), v_ref[lo:hi, :])
            if i:
                out = out + dot32((far * inv).astype(BF16), v_ref[0:lo, :])
            outs.append(out)
        acc = outs[0]
        for mask, out in zip(masks[1:], outs[1:]):
            acc = jnp.where(mask, out, acc)
        o_ref[rows, :] = acc.astype(BF16)


def attend(qkv, seg_col, seg_row, scaling):
    length, width = qkv.shape[0], qkv.shape[1] // 3
    pairs = width // LANES

    def part(c):
        return pl.BlockSpec((length, LANES), lambda j, c=c: (0, c * pairs + j))

    return pl.pallas_call(
        functools.partial(attend_kernel, length=length, scaling=scaling),
        grid=(pairs,),
        out_shape=jax.ShapeDtypeStruct((length, width), BF16),
        in_specs=[
            pl.BlockSpec((length, 1), lambda j: (0, 0)),
            pl.BlockSpec((1, length), lambda j: (0, 0)),
            part(0),
            part(1),
            part(2),
        ],
        out_specs=pl.BlockSpec((length, LANES), lambda j: (0, j)),
        compiler_params=pltpu.CompilerParams(vmem_limit_bytes=VMEM_LIMIT),
        cost_estimate=pl.CostEstimate(
            flops=8 * length * length * width, bytes_accessed=8 * length * width, transcendentals=0
        ),
        name="attend",
    )(seg_col, seg_row, qkv, qkv, qkv)


def attend_back_kernel(
    seg_col, seg_row, q_ref, k_ref, v_ref, g_ref, o_ref, dk_ref, dv_ref, *, length, scaling, width
):
    pair = pl.program_id(0)
    masks = head_masks(BLOCK)
    key_t = jnp.transpose(k_ref[...])
    dk_ref[...] = jnp.zeros_like(dk_ref)
    dv_ref[...] = jnp.zeros_like(dv_ref)
    half = lax.broadcasted_iota(jnp.int32, (LANES, BLOCK), 0) // HEAD_DIM
    for i in range(length // BLOCK):
        lo, hi = i * BLOCK, min(length, (i + 2) * BLOCK)
        rows = pl.ds(lo, BLOCK)
        visible = seg_col[lo:hi, :] <= seg_row[:, rows]
        q, g = q_ref[rows, :], g_ref[rows, :]
        dq_t = None
        for h, mask in enumerate(masks):
            qm = jnp.where(mask, q * scaling, 0).astype(BF16)
            gm = jnp.where(mask, g, 0).astype(BF16)
            near = lax.dot_general(k_ref[lo:hi, :], qm, NT, preferred_element_type=F32)
            near = jnp.where(visible, near, MASKED_SCORE)
            top = jnp.max(near, 0, keepdims=True)
            if i:
                far = lax.dot_general(k_ref[0:lo, :], qm, NT, preferred_element_type=F32)
                top = jnp.maximum(top, jnp.max(far, 0, keepdims=True))
            near = jnp.exp(near - top)
            total = jnp.sum(near, 0, keepdims=True)
            if i:
                far = jnp.exp(far - top)
                total = total + jnp.sum(far, 0, keepdims=True)
            inv = 1.0 / total
            near = near * inv
            near_g = lax.dot_general(v_ref[lo:hi, :], gm, NT, preferred_element_type=F32)
            inner = jnp.sum(near * near_g, 0, keepdims=True)
            if i:
                far = far * inv
                far_g = lax.dot_general(v_ref[0:lo, :], gm, NT, preferred_element_type=F32)
                inner = inner + jnp.sum(far * far_g, 0, keepdims=True)
            near_s = (near * (near_g - inner)).astype(BF16)
            dv_ref[lo:hi, :] += dot32(near.astype(BF16), gm)
            dk_ref[lo:hi, :] += dot32(near_s, qm)
            dq = dot32(key_t[:, lo:hi], near_s)
            if i:
                far_s = (far * (far_g - inner)).astype(BF16)
                dv_ref[0:lo, :] += dot32(far.astype(BF16), gm)
                dk_ref[0:lo, :] += dot32(far_s, qm)
                dq = dq + dot32(key_t[:, 0:lo], far_s)
            dq_t = dq if dq_t is None else jnp.where(half == h, dq, dq_t)
        lanes = pl.ds(pl.multiple_of(pair * LANES, LANES), LANES)
        o_ref[rows, lanes] = (jnp.transpose(dq_t) * scaling).astype(BF16)
    for c, ref in ((1, dk_ref), (2, dv_ref)):
        lanes = pl.ds(pl.multiple_of(c * width + pair * LANES, LANES), LANES)
        o_ref[:, lanes] = ref[...].astype(BF16)


def attend_back(qkv, seg_col, seg_row, grad_mixed, scaling):
    length, width = qkv.shape[0], qkv.shape[1] // 3
    pairs = width // LANES

    def part(c):
        return pl.BlockSpec((length, LANES), lambda j, c=c: (0, c * pairs + j))

    return pl.pallas_call(
        functools.partial(attend_back_kernel, length=length, scaling=scaling, width=width),
        grid=(pairs,),
        out_shape=jax.ShapeDtypeStruct((length, 3 * width), BF16),
        in_specs=[
            pl.BlockSpec((length, 1), lambda j: (0, 0)),
            pl.BlockSpec((1, length), lambda j: (0, 0)),
            part(0),
            part(1),
            part(2),
            pl.BlockSpec((length, LANES), lambda j: (0, j)),
        ],
        out_specs=pl.BlockSpec((length, 3 * width), lambda j: (0, 0)),
        scratch_shapes=[pltpu.VMEM((length, LANES), F32)] * 2,
        compiler_params=pltpu.CompilerParams(vmem_limit_bytes=VMEM_LIMIT),
        cost_estimate=pl.CostEstimate(
            flops=20 * length * length * width, bytes_accessed=16 * length * width, transcendentals=0
        ),
        name="attend_back",
    )(seg_col, seg_row, qkv, qkv, qkv, grad_mixed)


def residual_kernel(m_ref, w_ref, t_ref, g_ref, b_ref, s_ref, n_ref, *, groups):
    acc = t_ref[...].astype(F32)
    depth = m_ref.shape[2]
    for t in range(groups):
        acc = acc + dot32(m_ref[t], w_ref[t * depth : (t + 1) * depth, :])
    s_ref[...] = acc
    hat, unused = norm_parts(acc)
    n_ref[...] = (hat * g_ref[...] + b_ref[...]).astype(BF16)


def residual_norm(mixed_all, weight, tokens_all, gain, bias):
    groups, length, depth = mixed_all.shape
    width = weight.shape[1]
    rows = BLOCK
    return pl.pallas_call(
        functools.partial(residual_kernel, groups=groups),
        grid=(length // rows,),
        out_shape=(
            jax.ShapeDtypeStruct((length, width), F32),
            jax.ShapeDtypeStruct((length, width), BF16),
        ),
        in_specs=[
            pl.BlockSpec((groups, rows, depth), lambda i: (0, i, 0)),
            pl.BlockSpec((groups * depth, width), lambda i: (0, 0)),
            pl.BlockSpec((rows, width), lambda i: (i, 0)),
            pl.BlockSpec((1, width), lambda i: (0, 0)),
            pl.BlockSpec((1, width), lambda i: (0, 0)),
        ],
        out_specs=(
            pl.BlockSpec((rows, width), lambda i: (i, 0)),
            pl.BlockSpec((rows, width), lambda i: (i, 0)),
        ),
        compiler_params=pltpu.CompilerParams(vmem_limit_bytes=VMEM_LIMIT),
        cost_estimate=pl.CostEstimate(
            flops=2 * length * width * width, bytes_accessed=12 * length * width, transcendentals=0
        ),
        name="residual_norm",
    )(mixed_all, weight, tokens_all, gain[None], bias[None])


def spread_kernel(d_ref, x_ref, o_ref):
    rows = o_ref.shape[0]
    slot = lax.broadcasted_iota(jnp.int32, (rows, d_ref.shape[1]), 0) + pl.program_id(0) * rows
    pick = jnp.where(slot == d_ref[...], 1.0, 0.0).astype(BF16)
    o_ref[...] = dot32(pick, x_ref[...]).astype(BF16)


def spread(dest_row, rows_in, slots):
    length, width = rows_in.shape
    block = 2 * BLOCK
    return pl.pallas_call(
        spread_kernel,
        grid=(slots // block,),
        out_shape=jax.ShapeDtypeStruct((slots, width), BF16),
        in_specs=[
            pl.BlockSpec((1, length), lambda i: (0, 0)),
            pl.BlockSpec((length, width), lambda i: (0, 0)),
        ],
        out_specs=pl.BlockSpec((block, width), lambda i: (i, 0)),
        compiler_params=pltpu.CompilerParams(vmem_limit_bytes=VMEM_LIMIT),
        cost_estimate=pl.CostEstimate(
            flops=2 * slots * length * width, bytes_accessed=2 * (length + slots) * width, transcendentals=0
        ),
        name="spread",
    )(dest_row, rows_in)


def pick_kernel(d_ref, x_ref, o_ref):
    rows, slots = o_ref.shape[0], x_ref.shape[0]
    slot = lax.broadcasted_iota(jnp.int32, (rows, slots), 1)
    pick = jnp.where(slot == d_ref[...], 1.0, 0.0).astype(BF16)
    o_ref[...] = dot32(pick, x_ref[...]).astype(BF16)


def pick_rows(dest_col, rows_in, length):
    slots, width = rows_in.shape
    return pl.pallas_call(
        pick_kernel,
        grid=(length // BLOCK,),
        out_shape=jax.ShapeDtypeStruct((length, width), BF16),
        in_specs=[
            pl.BlockSpec((BLOCK, 1), lambda i: (i, 0)),
            pl.BlockSpec((slots, width), lambda i: (0, 0)),
        ],
        out_specs=pl.BlockSpec((BLOCK, width), lambda i: (i, 0)),
        compiler_params=pltpu.CompilerParams(vmem_limit_bytes=VMEM_LIMIT),
        cost_estimate=pl.CostEstimate(
            flops=2 * slots * length * width, bytes_accessed=2 * (length + slots) * width, transcendentals=0
        ),
        name="pick_rows",
    )(dest_col, rows_in)


ROOT = 0.7978845608028654
CUBE = 0.044715


def expert_kernel(x_ref, u_ref, w_ref, o_ref, h_ref, s_ref, *, chunk):
    x = x_ref[...].reshape(-1, x_ref.shape[-1])
    rows, ffn = x.shape[0], u_ref.shape[2]
    acc = None
    for c in range(ffn // chunk):
        part = slice(c * chunk, (c + 1) * chunk)
        up = dot32(x, u_ref[0, :, part])
        square = up * up
        tanh = jnp.tanh(ROOT * (up + CUBE * (square * up)))
        half = 0.5 * (1.0 + tanh)
        hidden = (up * half).astype(BF16)
        slope = half + (0.5 * ROOT) * up * (1.0 - tanh * tanh) * (1.0 + (3.0 * CUBE) * square)
        h_ref[0, :, part] = hidden
        s_ref[0, :, part] = slope.astype(BF16)
        out = dot32(hidden, w_ref[0, part, :])
        acc = out if acc is None else acc + out
    o_ref[...] = acc.astype(BF16).reshape(o_ref.shape)


def expert_forward(received, w_up, w_down):
    sources, experts, capacity, width = received.shape
    rows, ffn = sources * capacity, w_up.shape[2]
    tile = pl.BlockSpec((sources, 1, capacity, width), lambda e: (0, e, 0, 0))
    flat = pl.BlockSpec((1, rows, ffn), lambda e: (e, 0, 0))
    return pl.pallas_call(
        functools.partial(expert_kernel, chunk=256),
        grid=(experts,),
        out_shape=(
            jax.ShapeDtypeStruct(received.shape, BF16),
            jax.ShapeDtypeStruct((experts, rows, ffn), BF16),
            jax.ShapeDtypeStruct((experts, rows, ffn), BF16),
        ),
        in_specs=[
            tile,
            pl.BlockSpec((1, width, ffn), lambda e: (e, 0, 0)),
            pl.BlockSpec((1, ffn, width), lambda e: (e, 0, 0)),
        ],
        out_specs=(tile, flat, flat),
        compiler_params=pltpu.CompilerParams(vmem_limit_bytes=VMEM_LIMIT),
        cost_estimate=pl.CostEstimate(
            flops=4 * experts * rows * ffn * width,
            bytes_accessed=4 * experts * (ffn * width + 2 * rows * width),
            transcendentals=0,
        ),
        name="expert_forward",
    )(received, w_up, w_down)


def expert_back_kernel(x_ref, c_ref, r_ref, u_ref, w_ref, s_ref, o_ref, g_ref, e_ref, *, chunk, experts):
    first = lax.axis_index("dp") * experts + pl.program_id(0)
    x = x_ref[...].reshape(-1, x_ref.shape[-1])
    logits = dot32(x, r_ref[...])
    weights = exp_rows(logits)
    lane = lax.broadcasted_iota(jnp.int32, logits.shape, 1)
    chosen = jnp.sum(jnp.where(lane == first, weights, 0.0), -1, keepdims=True)
    gate = chosen / jnp.sum(weights, -1, keepdims=True)
    grad = (c_ref[...].reshape(x.shape).astype(F32) * gate).astype(BF16)
    e_ref[0] = grad
    acc = None
    for c in range(u_ref.shape[2] // chunk):
        part = slice(c * chunk, (c + 1) * chunk)
        hidden = lax.dot_general(grad, w_ref[0, part, :], NT, preferred_element_type=F32)
        upact = (hidden * s_ref[0, :, part].astype(F32)).astype(BF16)
        g_ref[0, :, part] = upact
        out = lax.dot_general(upact, u_ref[0, :, part], NT, preferred_element_type=F32)
        acc = out if acc is None else acc + out
    o_ref[...] = acc.astype(BF16).reshape(o_ref.shape)


def expert_backward(received, cot_received, router, w_up, w_down, slope):
    sources, experts, capacity, width = received.shape
    rows, ffn = sources * capacity, w_up.shape[2]
    tile = pl.BlockSpec((sources, 1, capacity, width), lambda e: (0, e, 0, 0))
    flat = pl.BlockSpec((1, rows, ffn), lambda e: (e, 0, 0))
    return pl.pallas_call(
        functools.partial(expert_back_kernel, chunk=256, experts=experts),
        grid=(experts,),
        out_shape=(
            jax.ShapeDtypeStruct(received.shape, BF16),
            jax.ShapeDtypeStruct((experts, rows, ffn), BF16),
            jax.ShapeDtypeStruct((experts, rows, width), BF16),
        ),
        in_specs=[
            tile,
            tile,
            pl.BlockSpec(router.shape, lambda e: (0, 0)),
            pl.BlockSpec((1, width, ffn), lambda e: (e, 0, 0)),
            pl.BlockSpec((1, ffn, width), lambda e: (e, 0, 0)),
            flat,
        ],
        out_specs=(tile, flat, pl.BlockSpec((1, rows, width), lambda e: (e, 0, 0))),
        compiler_params=pltpu.CompilerParams(vmem_limit_bytes=VMEM_LIMIT),
        cost_estimate=pl.CostEstimate(
            flops=4 * experts * rows * ffn * width,
            bytes_accessed=4 * experts * (ffn * width + 3 * rows * width),
            transcendentals=0,
        ),
        name="expert_backward",
    )(received, cot_received, router, w_up, w_down, slope)


def weight_grad_kernel(*refs, count, chunk):
    lefts, rights, o_ref = refs[:count], refs[count : 2 * count], refs[2 * count]
    outs = o_ref.shape[1]

    @pl.loop(0, outs // chunk)
    def _(c):
        part = pl.ds(pl.multiple_of(c * chunk, chunk), chunk)
        acc = None
        for a_ref, b_ref in zip(lefts, rights):
            if len(a_ref.shape) == 4:
                a = a_ref[:, :, :, part].reshape(-1, chunk)
            else:
                a = a_ref[0, :, part]
            out = lax.dot_general(a, b_ref[0], TN, preferred_element_type=F32)
            acc = out if acc is None else acc + out
        o_ref[0, part, :] = acc


def weight_grads(lefts, rights):
    experts, rows, ncols = rights[0].shape
    mrows = lefts[0].shape[-1]

    def spec(a):
        if a.ndim == 4:
            return pl.BlockSpec((a.shape[0], 1, a.shape[2], a.shape[3]), lambda e: (0, e, 0, 0))
        return pl.BlockSpec((1,) + a.shape[1:], lambda e: (e, 0, 0))

    return pl.pallas_call(
        functools.partial(weight_grad_kernel, count=len(lefts), chunk=256),
        grid=(experts,),
        out_shape=jax.ShapeDtypeStruct((experts, mrows, ncols), F32),
        in_specs=[spec(a) for a in lefts] + [spec(b) for b in rights],
        out_specs=pl.BlockSpec((1, mrows, ncols), lambda e: (e, 0, 0)),
        compiler_params=pltpu.CompilerParams(vmem_limit_bytes=VMEM_LIMIT),
        cost_estimate=pl.CostEstimate(
            flops=2 * len(lefts) * experts * rows * mrows * ncols,
            bytes_accessed=experts * (4 * mrows * ncols + 2 * len(lefts) * rows * (mrows + ncols)),
            transcendentals=0,
        ),
        name="weight_grads",
    )(*lefts, *rights)


class Chain:
    def __init__(self):
        self.last = None

    def run(self, step, operand, *more):
        if self.last is not None:
            more = more + (self.last,)
        if more:
            operand, unused = lax.optimization_barrier((operand, more))
        self.last = step(operand)
        return self.last


def z_gather(rows):
    return lax.all_gather(rows, "tensor", axis=0, tiled=True)


def z_stack(rows):
    return lax.all_gather(rows, "tensor", axis=0, tiled=False)


def z_scatter(rows):
    return lax.psum_scatter(rows, "tensor", scatter_dimension=0, tiled=True)


def exchange(blocks, axis):
    return lax.all_to_all(blocks, axis, split_axis=0, concat_axis=0, tiled=True)


def dp_exchange(blocks):
    return exchange(blocks, "dp")


def gather_by_exchange(piece, axis):
    return exchange(jnp.broadcast_to(piece[None], (lax.axis_size(axis),) + piece.shape), axis)


def mesh_copy(src, dst, send, recv, axis, peer):
    return pltpu.make_async_remote_copy(
        src_ref=src,
        dst_ref=dst,
        send_sem=send,
        recv_sem=recv,
        device_id={axis: peer},
        device_id_type=pl.DeviceIdType.MESH,
    )


def greet(peers):
    barrier = pltpu.get_barrier_semaphore()
    for axis, peer in peers:
        pl.semaphore_signal(
            barrier, inc=1, device_id={axis: peer}, device_id_type=pl.DeviceIdType.MESH
        )
    pl.semaphore_wait(barrier, len(peers))


def other_peers(axis, count):
    me = lax.axis_index(axis)
    return [lax.rem(me + k, count) for k in range(1, count)]


def z_swap_kernel(x_ref, o_ref, send, recv, *, count):
    me = lax.axis_index("tensor")
    peers = other_peers("tensor", count)
    greet([("tensor", p) for p in peers])
    copies = [
        mesh_copy(x_ref.at[p], o_ref.at[me], send.at[k], recv.at[k], "tensor", p)
        for k, p in enumerate(peers)
    ]
    for copy in copies:
        copy.start()
    o_ref[me] = x_ref[me]
    for copy in copies:
        copy.wait()


def z_swap(blocks, number=1):
    count = blocks.shape[0]
    whole = pl.BlockSpec(memory_space=pltpu.VMEM)
    return pl.pallas_call(
        functools.partial(z_swap_kernel, count=count),
        out_shape=jax.ShapeDtypeStruct(blocks.shape, blocks.dtype),
        in_specs=[whole],
        out_specs=whole,
        scratch_shapes=[pltpu.SemaphoreType.DMA((count - 1,))] * 2,
        compiler_params=pltpu.CompilerParams(collective_id=number, has_side_effects=True),
        cost_estimate=pl.CostEstimate(flops=0, bytes_accessed=40_000_000, transcendentals=0),
        name="z_swap",
    )(blocks)


def out_swap(blocks):
    return z_swap(blocks, 4)


def tree_sum(ref, count):
    total = ref[0]
    for k in range(1, count):
        total = total + ref[k]
    return total


def table_sum_kernel(x_ref, o_ref, zin, mid, din, zs, zr, ds, dr, es, er, fs, fr, *, zn, dn):
    z, d = lax.axis_index("tensor"), lax.axis_index("dp")
    zp, dp = other_peers("tensor", zn), other_peers("dp", dn)
    greet([("tensor", p) for p in zp] + [("dp", p) for p in dp])

    def run(copies):
        for copy in copies:
            copy.start()
        return copies

    def settle(copies):
        for copy in copies:
            copy.wait()

    first = run(
        [mesh_copy(x_ref.at[p], zin.at[z], zs.at[k], zr.at[k], "tensor", p) for k, p in enumerate(zp)]
    )
    zin[z] = x_ref[z]
    settle(first)
    mid[...] = tree_sum(zin, zn)
    second = run(
        [mesh_copy(mid.at[p], din.at[d], ds.at[k], dr.at[k], "dp", p) for k, p in enumerate(dp)]
    )
    din[d] = mid[d]
    settle(second)
    o_ref[z, d] = tree_sum(din, dn)
    third = run(
        [
            mesh_copy(o_ref.at[z, d], o_ref.at[z, d], es.at[k], er.at[k], "dp", p)
            for k, p in enumerate(dp)
        ]
    )
    settle(third)
    fourth = run(
        [mesh_copy(o_ref.at[z], o_ref.at[z], fs.at[k], fr.at[k], "tensor", p) for k, p in enumerate(zp)]
    )
    settle(fourth)


def table_sum(values):
    zn, dn = lax.axis_size("tensor"), lax.axis_size("dp")
    shape = (zn, dn, values.size // (zn * dn * LANES), LANES)
    whole = pl.BlockSpec(memory_space=pltpu.VMEM)
    sems = [pltpu.SemaphoreType.DMA((n - 1,)) for n in (zn, zn, dn, dn, dn, dn, zn, zn)]
    return pl.pallas_call(
        functools.partial(table_sum_kernel, zn=zn, dn=dn),
        out_shape=jax.ShapeDtypeStruct(shape, F32),
        in_specs=[whole],
        out_specs=whole,
        scratch_shapes=[
            pltpu.VMEM(shape, F32),
            pltpu.VMEM(shape[1:], F32),
            pltpu.VMEM(shape[1:], F32),
        ]
        + sems,
        compiler_params=pltpu.CompilerParams(collective_id=2, has_side_effects=True),
        cost_estimate=pl.CostEstimate(flops=0, bytes_accessed=40_000_000, transcendentals=0),
        name="table_sum",
    )(values.reshape(shape)).reshape(values.shape)


def vector_sum_kernel(x_ref, o_ref, zin, mid, din, zs, zr, ds, dr, *, zn, dn):
    z, d = lax.axis_index("tensor"), lax.axis_index("dp")
    zp, dp = other_peers("tensor", zn), other_peers("dp", dn)
    greet([("tensor", p) for p in zp] + [("dp", p) for p in dp])
    first = [
        mesh_copy(x_ref, zin.at[z], zs.at[k], zr.at[k], "tensor", p) for k, p in enumerate(zp)
    ]
    for copy in first:
        copy.start()
    zin[z] = x_ref[...]
    for copy in first:
        copy.wait()
    total = tree_sum(zin, zn)
    mid[...] = total
    second = [mesh_copy(mid, din.at[d], ds.at[k], dr.at[k], "dp", p) for k, p in enumerate(dp)]
    for copy in second:
        copy.start()
    din[d] = total
    for copy in second:
        copy.wait()
    o_ref[...] = tree_sum(din, dn)


def vector_sum(values):
    zn, dn = lax.axis_size("tensor"), lax.axis_size("dp")
    shape = (values.size // LANES, LANES)
    whole = pl.BlockSpec(memory_space=pltpu.VMEM)
    sems = [pltpu.SemaphoreType.DMA((n - 1,)) for n in (zn, zn, dn, dn)]
    return pl.pallas_call(
        functools.partial(vector_sum_kernel, zn=zn, dn=dn),
        out_shape=jax.ShapeDtypeStruct(shape, F32),
        in_specs=[whole],
        out_specs=whole,
        scratch_shapes=[
            pltpu.VMEM((zn,) + shape, F32),
            pltpu.VMEM(shape, F32),
            pltpu.VMEM((dn,) + shape, F32),
        ]
        + sems,
        compiler_params=pltpu.CompilerParams(collective_id=3, has_side_effects=True),
        cost_estimate=pl.CostEstimate(flops=0, bytes_accessed=30_000_000, transcendentals=0),
        name="vector_sum",
    )(values.reshape(shape)).reshape(values.shape)


def shards(
    tokens,
    block_ids,
    routes,
    cotangent,
    ln1_gain,
    ln1_bias,
    w_qkv,
    w_out,
    ln2_gain,
    ln2_bias,
    router,
    w_up,
    w_down,
):
    micro_count, unused, rows_dev, model_width = tokens.shape
    length = routes.shape[2]
    local_experts = w_up.shape[0]
    experts_all = router.shape[1]
    dp_count = lax.axis_size("dp")
    tensor_count = lax.axis_size("tensor")
    capacity = -(-(3 * length // (2 * experts_all)) // 16) * 16
    slots = experts_all * capacity
    scaling = HEAD_DIM ** (-0.5)
    local_width = w_qkv.shape[2]
    first_row = lax.axis_index("tensor") * rows_dev
    expert_range = jnp.arange(experts_all, dtype=jnp.int32)
    micros = range(micro_count)

    def own(rows):
        return lax.dynamic_slice_in_dim(rows, first_row, rows_dev)

    zc, tc, xc = Chain(), Chain(), Chain()
    qkv_flat = gather_by_exchange(w_qkv.reshape(-1, 3 * local_width), "dp")
    qkv_flat = qkv_flat.reshape(model_width, 3 * local_width)
    out_parts = gather_by_exchange(gather_by_exchange(w_out, "tensor"), "dp")
    out_matrix = out_parts.transpose(1, 2, 0, 3).reshape(model_width, model_width)

    dest_rows, dest_cols, seg_rows, seg_cols = [], [], [], []
    before = (
        jnp.arange(length, dtype=jnp.int32)[:, None] > jnp.arange(length, dtype=jnp.int32)[None, :]
    ).astype(BF16)
    for m in micros:
        ids = routes[m, 0]
        onehot = (ids == expert_range[None, :]).astype(BF16)
        place = jnp.sum(dot32(before, onehot) * onehot.astype(F32), 1).astype(jnp.int32)
        dest = ids[:, 0] * capacity + place
        dest_rows.append(dest[None, :])
        dest_cols.append(dest[:, None])
        seg_rows.append(block_ids[m])
        seg_cols.append(block_ids[m, 0][:, None])

    def to_blocks(rows):
        return rows.reshape(dp_count, local_experts, capacity, model_width)

    tokens_all, cot_all, whole_one, qkv, mixed = {}, {}, {}, {}, {}
    mixed_all, stream_all, whole_two = {}, {}, {}
    cot_received, received, hidden, slope, upact, grad_expert = {}, {}, {}, {}, {}, {}
    returned, grad_back, expert_out, grad_two = {}, {}, {}, {}
    partial, grad_in = {}, {}
    grad_stream, grad_mixed, grad_one, final_rows, grad_rows = {}, {}, {}, {}, {}
    routers, gain_two, outs_acc, qkv_acc, gain_acc = {}, {}, {}, {}, {}

    def attention(m):
        def step(rows):
            whole = (norm_parts(rows.astype(F32))[0] * ln1_gain + ln1_bias).astype(BF16)
            act = dot32(whole, qkv_flat).astype(BF16)
            return attend(act, seg_cols[m], seg_rows[m], scaling), whole, act

        mixed[m], whole_one[m], qkv[m] = tc.run(step, tokens_all[m])

    def send_cotangent(m):
        blocks = tc.run(lambda v: to_blocks(spread(dest_rows[m], v, slots)), cot_all[m])
        cot_received[m] = xc.run(dp_exchange, blocks)

    def send_tokens(m):
        def step(v):
            stream, whole = residual_norm(v, out_matrix, tokens_all[m], ln2_gain, ln2_bias)
            return to_blocks(spread(dest_rows[m], whole, slots)), stream, whole

        blocks, stream_all[m], whole_two[m] = tc.run(step, mixed_all[m])
        received[m] = xc.run(dp_exchange, blocks)

    def experts_forward(m):
        partial[m], hidden[m], slope[m] = tc.run(
            lambda v: expert_forward(v, w_up, w_down), received[m]
        )

    def experts_backward(m):
        grad_in[m], upact[m], grad_expert[m] = tc.run(
            lambda v: expert_backward(v[0], v[1], router, w_up, w_down, v[2]),
            (received[m], cot_received[m], slope[m]),
        )

    def send_back(m, source, target):
        target[m] = xc.run(dp_exchange, source[m]).reshape(slots, model_width)

    def combine(m, source):
        return tc.run(lambda v: pick_rows(dest_cols[m], v, length), source[m])

    def middle(m):
        def step(v):
            eo, gt, stream, whole, mix = v
            stream_one = own(stream)
            hat_two, inv_two = norm_parts(stream_one)
            normed_two = own(whole)
            logits = dot32(normed_two, router)
            weights = exp_rows(logits)
            probs = weights / jnp.sum(weights, -1, keepdims=True)
            pick_table = (own(routes[m, 0]) == expert_range[None, :]).astype(F32)
            gate = jnp.sum(probs * pick_table, -1, keepdims=True)
            eo, gt = eo.astype(F32), gt.astype(F32)
            final = (stream_one + gate * eo).astype(BF16)
            grad_final = cotangent[m, 0].astype(F32)
            grad_gate = jnp.sum(grad_final * eo, -1, keepdims=True)
            grad_logits = (gate * grad_gate * (pick_table - probs)).astype(BF16)
            gt = gt + lax.dot_general(grad_logits, router, NT, preferred_element_type=F32)
            grad_router = lax.dot_general(grad_logits, normed_two, TN, preferred_element_type=F32)
            gains = jnp.stack([jnp.sum(gt * hat_two, 0), jnp.sum(gt, 0)])
            grad = grad_final + norm_backward(gt, hat_two, inv_two, ln2_gain)
            grad_attn = grad.astype(BF16)
            mixed_own = lax.dynamic_slice_in_dim(mix, first_row, rows_dev, axis=1)
            out_acc = jnp.einsum("trf,rd->tfd", mixed_own, grad_attn, preferred_element_type=F32)
            gm = lax.dot_general(grad_attn, out_matrix, NT, preferred_element_type=F32).astype(BF16)
            gm = gm.reshape(rows_dev, tensor_count, local_width).transpose(1, 0, 2)
            return gm, final, grad_router, gains, grad, out_acc

        gm, final_rows[m], routers[m], gain_two[m], grad_stream[m], outs_acc[m] = tc.run(
            step, (expert_out[m], grad_two[m], stream_all[m], whole_two[m], mixed_all[m])
        )
        grad_mixed[m] = tc.run(z_swap, gm).reshape(length, local_width)

    def attention_back(m):
        def step(v):
            act = attend_back(qkv[m], seg_cols[m], seg_rows[m], v, scaling)
            part = lax.dot_general(act, qkv_flat, NT, preferred_element_type=F32).astype(BF16)
            return part, act

        part, act = tc.run(step, grad_mixed[m])
        qkv_acc[m] = lax.dot_general(whole_one[m], act, TN, preferred_element_type=F32)
        return part

    def finish(m):
        grad = grad_one[m].astype(F32)
        hat_one, inv_one = norm_parts(tokens[m, 0].astype(F32))
        gain_acc[m] = jnp.stack([jnp.sum(grad * hat_one, 0), jnp.sum(grad, 0)])
        grad_rows[m] = grad_stream[m] + norm_backward(grad, hat_one, inv_one, ln1_gain)

    tokens_all[0] = zc.run(z_gather, tokens[0, 0])
    cot_all[0] = zc.run(z_gather, cotangent[0, 0], qkv_flat)
    attention(0)
    mixed_all[0] = zc.run(z_stack, mixed[0], out_matrix)
    send_cotangent(0)
    cot_all[1] = zc.run(z_gather, cotangent[1, 0])
    send_tokens(0)
    tokens_all[1] = zc.run(z_gather, tokens[1, 0])
    send_cotangent(1)
    experts_forward(0)
    send_back(0, partial, returned)
    experts_backward(0)
    send_back(0, grad_in, grad_back)
    attention(1)
    mixed_all[1] = zc.run(z_stack, mixed[1])
    expert_out[0] = zc.run(z_scatter, combine(0, returned))
    send_tokens(1)
    grad_two[0] = zc.run(z_scatter, combine(0, grad_back))
    experts_forward(1)
    send_back(1, partial, returned)
    experts_backward(1)
    send_back(1, grad_in, grad_back)
    middle(0)
    expert_out[1] = zc.run(z_scatter, combine(1, returned))
    part = attention_back(0)
    acc_up = tc.run(
        lambda v: weight_grads([v[0], v[1]], [v[2], v[3]]),
        (received[0], received[1], upact[0], upact[1]),
    )
    grad_two[1] = zc.run(z_scatter, combine(1, grad_back))
    grad_one[0] = zc.run(z_scatter, part)
    acc_down = tc.run(
        lambda v: weight_grads([v[0], v[1]], [v[2], v[3]]),
        (hidden[0], hidden[1], grad_expert[0], grad_expert[1]),
    )
    middle(1)
    acc_out = (outs_acc[0] + outs_acc[1]).astype(BF16)
    acc_out = acc_out.reshape(model_width, dp_count, -1).transpose(1, 0, 2)
    acc_out = xc.run(dp_exchange, acc_out)
    finish(0)
    part = attention_back(1)
    grad_one[1] = zc.run(z_scatter, part)
    acc_qkv = (qkv_acc[0] + qkv_acc[1]).astype(BF16)
    acc_qkv = xc.run(dp_exchange, acc_qkv.reshape(dp_count, -1, 3 * local_width))
    router_sum = tc.run(table_sum, routers[0] + routers[1])
    acc_out = tc.run(
        lambda v: jnp.sum(v.astype(F32), 0).astype(BF16).reshape((tensor_count,) + w_out.shape),
        acc_out,
    )
    grad_out_shard = jnp.sum(tc.run(out_swap, acc_out).astype(F32), 0)
    grad_qkv_shard = jnp.sum(acc_qkv.astype(F32), 0).reshape(w_qkv.shape)
    finish(1)
    gain_sum = tc.run(
        vector_sum, jnp.concatenate([gain_two[0] + gain_two[1], gain_acc[0] + gain_acc[1]])
    )
    return (
        jnp.stack([final_rows[m] for m in micros])[:, None],
        jnp.stack([grad_rows[m] for m in micros])[:, None],
        gain_sum[2],
        gain_sum[3],
        grad_qkv_shard,
        grad_out_shard,
        gain_sum[0],
        gain_sum[1],
        router_sum.T,
        acc_up,
        acc_down,
    )


def solution(mesh):
    return jax.shard_map(
        shards,
        mesh=mesh,
        in_specs=(
            P(None, "dp", "tensor", None),
            P(None, "dp", None),
            P(None, "dp", None, None),
            P(None, "dp", "tensor", None),
            P(),
            P(),
            P("dp", None, "tensor"),
            P("tensor", "dp"),
            P(),
            P(),
            P(),
            P("dp", None, "tensor"),
            P("dp", "tensor", None),
        ),
        out_specs=(
            P(None, "dp", "tensor", None),
            P(None, "dp", "tensor", None),
            P(),
            P(),
            P("dp", None, "tensor"),
            P("tensor", "dp"),
            P(),
            P(),
            P(),
            P("dp", None, "tensor"),
            P("dp", "tensor", None),
        ),
        check_vma=False,
    )
```

```python
import functools

import jax
import jax.numpy as jnp
from jax import lax
from jax.experimental import pallas as pl
from jax.experimental.pallas import tpu as pltpu
from jax.sharding import PartitionSpec as P

HEAD_DIM = 64
LANES = 128
BLOCK = 256
EPSILON = 1e-05
MASKED_SCORE = -1e30
F32 = jnp.float32
BF16 = jnp.bfloat16
NT = (((1,), (1,)), ((), ()))
TN = (((0,), (0,)), ((), ()))
VMEM_LIMIT = 60 * 1024 * 1024


def norm_parts(stream):
    centre = stream - jnp.mean(stream, -1, keepdims=True)
    inv_std = lax.rsqrt(jnp.mean(centre * centre, -1, keepdims=True) + EPSILON)
    return centre * inv_std, inv_std


def norm_backward(grad_normed, normed, inv_std, gain_vec):
    grad_hat = grad_normed * gain_vec
    mean_grad = jnp.mean(grad_hat, -1, keepdims=True)
    mean_cross = jnp.mean(grad_hat * normed, -1, keepdims=True)
    return inv_std * (grad_hat - mean_grad - normed * mean_cross)


def dot32(a, b):
    return jnp.dot(a, b, preferred_element_type=F32)


def head_masks(rows):
    lane = lax.broadcasted_iota(jnp.int32, (rows, LANES), 1)
    return [(lane // HEAD_DIM) == h for h in range(LANES // HEAD_DIM)]


def exp_rows(scores):
    row_max = jnp.max(scores, -1, keepdims=True)
    return jnp.exp(scores - row_max)


def attend_kernel(seg_col, seg_row, q_ref, k_ref, v_ref, o_ref, *, length, scaling):
    masks = head_masks(BLOCK)
    for i in range(length // BLOCK):
        lo, hi = i * BLOCK, min(length, (i + 2) * BLOCK)
        rows = pl.ds(lo, BLOCK)
        visible = seg_row[:, lo:hi] <= seg_col[rows, :]
        q = q_ref[rows, :]
        outs = []
        for mask in masks:
            qm = jnp.where(mask, q * scaling, 0).astype(BF16)
            near = lax.dot_general(qm, k_ref[lo:hi, :], NT, preferred_element_type=F32)
            near = jnp.where(visible, near, MASKED_SCORE)
            top = jnp.max(near, -1, keepdims=True)
            if i:
                far = lax.dot_general(qm, k_ref[0:lo, :], NT, preferred_element_type=F32)
                top = jnp.maximum(top, jnp.max(far, -1, keepdims=True))
            near = jnp.exp(near - top)
            total = jnp.sum(near, -1, keepdims=True)
            if i:
                far = jnp.exp(far - top)
                total = total + jnp.sum(far, -1, keepdims=True)
            inv = 1.0 / total
            out = dot32((near * inv).astype(BF16), v_ref[lo:hi, :])
            if i:
                out = out + dot32((far * inv).astype(BF16), v_ref[0:lo, :])
            outs.append(out)
        acc = outs[0]
        for mask, out in zip(masks[1:], outs[1:]):
            acc = jnp.where(mask, out, acc)
        o_ref[rows, :] = acc.astype(BF16)


def attend(qkv, seg_col, seg_row, scaling):
    length, width = qkv.shape[0], qkv.shape[1] // 3
    pairs = width // LANES

    def part(c):
        return pl.BlockSpec((length, LANES), lambda j, c=c: (0, c * pairs + j))

    return pl.pallas_call(
        functools.partial(attend_kernel, length=length, scaling=scaling),
        grid=(pairs,),
        out_shape=jax.ShapeDtypeStruct((length, width), BF16),
        in_specs=[
            pl.BlockSpec((length, 1), lambda j: (0, 0)),
            pl.BlockSpec((1, length), lambda j: (0, 0)),
            part(0),
            part(1),
            part(2),
        ],
        out_specs=pl.BlockSpec((length, LANES), lambda j: (0, j)),
        compiler_params=pltpu.CompilerParams(vmem_limit_bytes=VMEM_LIMIT),
        cost_estimate=pl.CostEstimate(
            flops=8 * length * length * width, bytes_accessed=8 * length * width, transcendentals=0
        ),
        name="attend",
    )(seg_col, seg_row, qkv, qkv, qkv)


def attend_back_kernel(
    seg_col, seg_row, q_ref, k_ref, v_ref, g_ref, o_ref, dk_ref, dv_ref, *, length, scaling, width
):
    pair = pl.program_id(0)
    masks = head_masks(BLOCK)
    key_t = jnp.transpose(k_ref[...])
    dk_ref[...] = jnp.zeros_like(dk_ref)
    dv_ref[...] = jnp.zeros_like(dv_ref)
    half = lax.broadcasted_iota(jnp.int32, (LANES, BLOCK), 0) // HEAD_DIM
    for i in range(length // BLOCK):
        lo, hi = i * BLOCK, min(length, (i + 2) * BLOCK)
        rows = pl.ds(lo, BLOCK)
        visible = seg_col[lo:hi, :] <= seg_row[:, rows]
        q, g = q_ref[rows, :], g_ref[rows, :]
        dq_t = None
        for h, mask in enumerate(masks):
            qm = jnp.where(mask, q * scaling, 0).astype(BF16)
            gm = jnp.where(mask, g, 0).astype(BF16)
            near = lax.dot_general(k_ref[lo:hi, :], qm, NT, preferred_element_type=F32)
            near = jnp.where(visible, near, MASKED_SCORE)
            top = jnp.max(near, 0, keepdims=True)
            if i:
                far = lax.dot_general(k_ref[0:lo, :], qm, NT, preferred_element_type=F32)
                top = jnp.maximum(top, jnp.max(far, 0, keepdims=True))
            near = jnp.exp(near - top)
            total = jnp.sum(near, 0, keepdims=True)
            if i:
                far = jnp.exp(far - top)
                total = total + jnp.sum(far, 0, keepdims=True)
            inv = 1.0 / total
            near = near * inv
            near_g = lax.dot_general(v_ref[lo:hi, :], gm, NT, preferred_element_type=F32)
            inner = jnp.sum(near * near_g, 0, keepdims=True)
            if i:
                far = far * inv
                far_g = lax.dot_general(v_ref[0:lo, :], gm, NT, preferred_element_type=F32)
                inner = inner + jnp.sum(far * far_g, 0, keepdims=True)
            near_s = (near * (near_g - inner)).astype(BF16)
            dv_ref[lo:hi, :] += dot32(near.astype(BF16), gm)
            dk_ref[lo:hi, :] += dot32(near_s, qm)
            dq = dot32(key_t[:, lo:hi], near_s)
            if i:
                far_s = (far * (far_g - inner)).astype(BF16)
                dv_ref[0:lo, :] += dot32(far.astype(BF16), gm)
                dk_ref[0:lo, :] += dot32(far_s, qm)
                dq = dq + dot32(key_t[:, 0:lo], far_s)
            dq_t = dq if dq_t is None else jnp.where(half == h, dq, dq_t)
        lanes = pl.ds(pl.multiple_of(pair * LANES, LANES), LANES)
        o_ref[rows, lanes] = (jnp.transpose(dq_t) * scaling).astype(BF16)
    for c, ref in ((1, dk_ref), (2, dv_ref)):
        lanes = pl.ds(pl.multiple_of(c * width + pair * LANES, LANES), LANES)
        o_ref[:, lanes] = ref[...].astype(BF16)


def attend_back(qkv, seg_col, seg_row, grad_mixed, scaling):
    length, width = qkv.shape[0], qkv.shape[1] // 3
    pairs = width // LANES

    def part(c):
        return pl.BlockSpec((length, LANES), lambda j, c=c: (0, c * pairs + j))

    return pl.pallas_call(
        functools.partial(attend_back_kernel, length=length, scaling=scaling, width=width),
        grid=(pairs,),
        out_shape=jax.ShapeDtypeStruct((length, 3 * width), BF16),
        in_specs=[
            pl.BlockSpec((length, 1), lambda j: (0, 0)),
            pl.BlockSpec((1, length), lambda j: (0, 0)),
            part(0),
            part(1),
            part(2),
            pl.BlockSpec((length, LANES), lambda j: (0, j)),
        ],
        out_specs=pl.BlockSpec((length, 3 * width), lambda j: (0, 0)),
        scratch_shapes=[pltpu.VMEM((length, LANES), F32)] * 2,
        compiler_params=pltpu.CompilerParams(vmem_limit_bytes=VMEM_LIMIT),
        cost_estimate=pl.CostEstimate(
            flops=20 * length * length * width, bytes_accessed=16 * length * width, transcendentals=0
        ),
        name="attend_back",
    )(seg_col, seg_row, qkv, qkv, qkv, grad_mixed)


def residual_kernel(m_ref, w_ref, t_ref, g_ref, b_ref, s_ref, n_ref, *, groups):
    acc = t_ref[...].astype(F32)
    depth = m_ref.shape[2]
    for t in range(groups):
        acc = acc + dot32(m_ref[t], w_ref[t * depth : (t + 1) * depth, :])
    s_ref[...] = acc
    hat, unused = norm_parts(acc)
    n_ref[...] = (hat * g_ref[...] + b_ref[...]).astype(BF16)


def residual_norm(mixed_all, weight, tokens_all, gain, bias):
    groups, length, depth = mixed_all.shape
    width = weight.shape[1]
    rows = BLOCK
    return pl.pallas_call(
        functools.partial(residual_kernel, groups=groups),
        grid=(length // rows,),
        out_shape=(
            jax.ShapeDtypeStruct((length, width), F32),
            jax.ShapeDtypeStruct((length, width), BF16),
        ),
        in_specs=[
            pl.BlockSpec((groups, rows, depth), lambda i: (0, i, 0)),
            pl.BlockSpec((groups * depth, width), lambda i: (0, 0)),
            pl.BlockSpec((rows, width), lambda i: (i, 0)),
            pl.BlockSpec((1, width), lambda i: (0, 0)),
            pl.BlockSpec((1, width), lambda i: (0, 0)),
        ],
        out_specs=(
            pl.BlockSpec((rows, width), lambda i: (i, 0)),
            pl.BlockSpec((rows, width), lambda i: (i, 0)),
        ),
        compiler_params=pltpu.CompilerParams(vmem_limit_bytes=VMEM_LIMIT),
        cost_estimate=pl.CostEstimate(
            flops=2 * length * width * width, bytes_accessed=12 * length * width, transcendentals=0
        ),
        name="residual_norm",
    )(mixed_all, weight, tokens_all, gain[None], bias[None])


def spread_kernel(d_ref, x_ref, o_ref):
    rows = o_ref.shape[0]
    slot = lax.broadcasted_iota(jnp.int32, (rows, d_ref.shape[1]), 0) + pl.program_id(0) * rows
    pick = jnp.where(slot == d_ref[...], 1.0, 0.0).astype(BF16)
    o_ref[...] = dot32(pick, x_ref[...]).astype(BF16)


def spread(dest_row, rows_in, slots):
    length, width = rows_in.shape
    block = 2 * BLOCK
    return pl.pallas_call(
        spread_kernel,
        grid=(slots // block,),
        out_shape=jax.ShapeDtypeStruct((slots, width), BF16),
        in_specs=[
            pl.BlockSpec((1, length), lambda i: (0, 0)),
            pl.BlockSpec((length, width), lambda i: (0, 0)),
        ],
        out_specs=pl.BlockSpec((block, width), lambda i: (i, 0)),
        compiler_params=pltpu.CompilerParams(vmem_limit_bytes=VMEM_LIMIT),
        cost_estimate=pl.CostEstimate(
            flops=2 * slots * length * width, bytes_accessed=2 * (length + slots) * width, transcendentals=0
        ),
        name="spread",
    )(dest_row, rows_in)


def pick_kernel(d_ref, x_ref, o_ref):
    rows, slots = o_ref.shape[0], x_ref.shape[0]
    slot = lax.broadcasted_iota(jnp.int32, (rows, slots), 1)
    pick = jnp.where(slot == d_ref[...], 1.0, 0.0).astype(BF16)
    o_ref[...] = dot32(pick, x_ref[...]).astype(BF16)


def pick_rows(dest_col, rows_in, length):
    slots, width = rows_in.shape
    return pl.pallas_call(
        pick_kernel,
        grid=(length // BLOCK,),
        out_shape=jax.ShapeDtypeStruct((length, width), BF16),
        in_specs=[
            pl.BlockSpec((BLOCK, 1), lambda i: (i, 0)),
            pl.BlockSpec((slots, width), lambda i: (0, 0)),
        ],
        out_specs=pl.BlockSpec((BLOCK, width), lambda i: (i, 0)),
        compiler_params=pltpu.CompilerParams(vmem_limit_bytes=VMEM_LIMIT),
        cost_estimate=pl.CostEstimate(
            flops=2 * slots * length * width, bytes_accessed=2 * (length + slots) * width, transcendentals=0
        ),
        name="pick_rows",
    )(dest_col, rows_in)


ROOT = 0.7978845608028654
CUBE = 0.044715


def expert_kernel(x_ref, u_ref, w_ref, o_ref, h_ref, s_ref, *, chunk):
    x = x_ref[...].reshape(-1, x_ref.shape[-1])
    rows, ffn = x.shape[0], u_ref.shape[2]
    acc = None
    for c in range(ffn // chunk):
        part = slice(c * chunk, (c + 1) * chunk)
        up = dot32(x, u_ref[0, :, part])
        square = up * up
        tanh = jnp.tanh(ROOT * (up + CUBE * (square * up)))
        half = 0.5 * (1.0 + tanh)
        hidden = (up * half).astype(BF16)
        slope = half + (0.5 * ROOT) * up * (1.0 - tanh * tanh) * (1.0 + (3.0 * CUBE) * square)
        h_ref[0, :, part] = hidden
        s_ref[0, :, part] = slope.astype(BF16)
        out = dot32(hidden, w_ref[0, part, :])
        acc = out if acc is None else acc + out
    o_ref[...] = acc.astype(BF16).reshape(o_ref.shape)


def expert_forward(received, w_up, w_down):
    sources, experts, capacity, width = received.shape
    rows, ffn = sources * capacity, w_up.shape[2]
    tile = pl.BlockSpec((sources, 1, capacity, width), lambda e: (0, e, 0, 0))
    flat = pl.BlockSpec((1, rows, ffn), lambda e: (e, 0, 0))
    return pl.pallas_call(
        functools.partial(expert_kernel, chunk=256),
        grid=(experts,),
        out_shape=(
            jax.ShapeDtypeStruct(received.shape, BF16),
            jax.ShapeDtypeStruct((experts, rows, ffn), BF16),
            jax.ShapeDtypeStruct((experts, rows, ffn), BF16),
        ),
        in_specs=[
            tile,
            pl.BlockSpec((1, width, ffn), lambda e: (e, 0, 0)),
            pl.BlockSpec((1, ffn, width), lambda e: (e, 0, 0)),
        ],
        out_specs=(tile, flat, flat),
        compiler_params=pltpu.CompilerParams(vmem_limit_bytes=VMEM_LIMIT),
        cost_estimate=pl.CostEstimate(
            flops=4 * experts * rows * ffn * width,
            bytes_accessed=4 * experts * (ffn * width + 2 * rows * width),
            transcendentals=0,
        ),
        name="expert_forward",
    )(received, w_up, w_down)


def expert_back_kernel(x_ref, c_ref, r_ref, u_ref, w_ref, s_ref, o_ref, g_ref, e_ref, *, chunk, experts):
    first = lax.axis_index("dp") * experts + pl.program_id(0)
    x = x_ref[...].reshape(-1, x_ref.shape[-1])
    logits = dot32(x, r_ref[...])
    weights = exp_rows(logits)
    lane = lax.broadcasted_iota(jnp.int32, logits.shape, 1)
    chosen = jnp.sum(jnp.where(lane == first, weights, 0.0), -1, keepdims=True)
    gate = chosen / jnp.sum(weights, -1, keepdims=True)
    grad = (c_ref[...].reshape(x.shape).astype(F32) * gate).astype(BF16)
    e_ref[0] = grad
    acc = None
    for c in range(u_ref.shape[2] // chunk):
        part = slice(c * chunk, (c + 1) * chunk)
        hidden = lax.dot_general(grad, w_ref[0, part, :], NT, preferred_element_type=F32)
        upact = (hidden * s_ref[0, :, part].astype(F32)).astype(BF16)
        g_ref[0, :, part] = upact
        out = lax.dot_general(upact, u_ref[0, :, part], NT, preferred_element_type=F32)
        acc = out if acc is None else acc + out
    o_ref[...] = acc.astype(BF16).reshape(o_ref.shape)


def expert_backward(received, cot_received, router, w_up, w_down, slope):
    sources, experts, capacity, width = received.shape
    rows, ffn = sources * capacity, w_up.shape[2]
    tile = pl.BlockSpec((sources, 1, capacity, width), lambda e: (0, e, 0, 0))
    flat = pl.BlockSpec((1, rows, ffn), lambda e: (e, 0, 0))
    return pl.pallas_call(
        functools.partial(expert_back_kernel, chunk=256, experts=experts),
        grid=(experts,),
        out_shape=(
            jax.ShapeDtypeStruct(received.shape, BF16),
            jax.ShapeDtypeStruct((experts, rows, ffn), BF16),
            jax.ShapeDtypeStruct((experts, rows, width), BF16),
        ),
        in_specs=[
            tile,
            tile,
            pl.BlockSpec(router.shape, lambda e: (0, 0)),
            pl.BlockSpec((1, width, ffn), lambda e: (e, 0, 0)),
            pl.BlockSpec((1, ffn, width), lambda e: (e, 0, 0)),
            flat,
        ],
        out_specs=(tile, flat, pl.BlockSpec((1, rows, width), lambda e: (e, 0, 0))),
        compiler_params=pltpu.CompilerParams(vmem_limit_bytes=VMEM_LIMIT),
        cost_estimate=pl.CostEstimate(
            flops=4 * experts * rows * ffn * width,
            bytes_accessed=4 * experts * (ffn * width + 3 * rows * width),
            transcendentals=0,
        ),
        name="expert_backward",
    )(received, cot_received, router, w_up, w_down, slope)


def weight_grad_kernel(*refs, count, chunk):
    lefts, rights, o_ref = refs[:count], refs[count : 2 * count], refs[2 * count]
    outs = o_ref.shape[1]

    @pl.loop(0, outs // chunk)
    def _(c):
        part = pl.ds(pl.multiple_of(c * chunk, chunk), chunk)
        acc = None
        for a_ref, b_ref in zip(lefts, rights):
            if len(a_ref.shape) == 4:
                a = a_ref[:, :, :, part].reshape(-1, chunk)
            else:
                a = a_ref[0, :, part]
            out = lax.dot_general(a, b_ref[0], TN, preferred_element_type=F32)
            acc = out if acc is None else acc + out
        o_ref[0, part, :] = acc


def weight_grads(lefts, rights):
    experts, rows, ncols = rights[0].shape
    mrows = lefts[0].shape[-1]

    def spec(a):
        if a.ndim == 4:
            return pl.BlockSpec((a.shape[0], 1, a.shape[2], a.shape[3]), lambda e: (0, e, 0, 0))
        return pl.BlockSpec((1,) + a.shape[1:], lambda e: (e, 0, 0))

    return pl.pallas_call(
        functools.partial(weight_grad_kernel, count=len(lefts), chunk=256),
        grid=(experts,),
        out_shape=jax.ShapeDtypeStruct((experts, mrows, ncols), F32),
        in_specs=[spec(a) for a in lefts] + [spec(b) for b in rights],
        out_specs=pl.BlockSpec((1, mrows, ncols), lambda e: (e, 0, 0)),
        compiler_params=pltpu.CompilerParams(vmem_limit_bytes=VMEM_LIMIT),
        cost_estimate=pl.CostEstimate(
            flops=2 * len(lefts) * experts * rows * mrows * ncols,
            bytes_accessed=experts * (4 * mrows * ncols + 2 * len(lefts) * rows * (mrows + ncols)),
            transcendentals=0,
        ),
        name="weight_grads",
    )(*lefts, *rights)


class Chain:
    def __init__(self):
        self.last = None

    def run(self, step, operand, *more):
        if self.last is not None:
            more = more + (self.last,)
        if more:
            operand, unused = lax.optimization_barrier((operand, more))
        self.last = step(operand)
        return self.last


def z_gather(rows):
    return lax.all_gather(rows, "tensor", axis=0, tiled=True)


def z_stack(rows):
    return lax.all_gather(rows, "tensor", axis=0, tiled=False)


def z_scatter(rows):
    return lax.psum_scatter(rows, "tensor", scatter_dimension=0, tiled=True)


def exchange(blocks, axis):
    return lax.all_to_all(blocks, axis, split_axis=0, concat_axis=0, tiled=True)


def dp_exchange(blocks):
    return exchange(blocks, "dp")


def gather_by_exchange(piece, axis):
    return exchange(jnp.broadcast_to(piece[None], (lax.axis_size(axis),) + piece.shape), axis)


def mesh_copy(src, dst, send, recv, axis, peer):
    return pltpu.make_async_remote_copy(
        src_ref=src,
        dst_ref=dst,
        send_sem=send,
        recv_sem=recv,
        device_id={axis: peer},
        device_id_type=pl.DeviceIdType.MESH,
    )


def greet(peers):
    barrier = pltpu.get_barrier_semaphore()
    for axis, peer in peers:
        pl.semaphore_signal(
            barrier, inc=1, device_id={axis: peer}, device_id_type=pl.DeviceIdType.MESH
        )
    pl.semaphore_wait(barrier, len(peers))


def other_peers(axis, count):
    me = lax.axis_index(axis)
    return [lax.rem(me + k, count) for k in range(1, count)]


def z_swap_kernel(x_ref, o_ref, send, recv, *, count):
    me = lax.axis_index("tensor")
    peers = other_peers("tensor", count)
    greet([("tensor", p) for p in peers])
    copies = [
        mesh_copy(x_ref.at[p], o_ref.at[me], send.at[k], recv.at[k], "tensor", p)
        for k, p in enumerate(peers)
    ]
    for copy in copies:
        copy.start()
    o_ref[me] = x_ref[me]
    for copy in copies:
        copy.wait()


def z_swap(blocks, number=1):
    count = blocks.shape[0]
    whole = pl.BlockSpec(memory_space=pltpu.VMEM)
    return pl.pallas_call(
        functools.partial(z_swap_kernel, count=count),
        out_shape=jax.ShapeDtypeStruct(blocks.shape, blocks.dtype),
        in_specs=[whole],
        out_specs=whole,
        scratch_shapes=[pltpu.SemaphoreType.DMA((count - 1,))] * 2,
        compiler_params=pltpu.CompilerParams(collective_id=number, has_side_effects=True),
        cost_estimate=pl.CostEstimate(flops=0, bytes_accessed=40_000_000, transcendentals=0),
        name="z_swap",
    )(blocks)


def out_swap(blocks):
    return z_swap(blocks, 4)


def tree_sum(ref, count):
    total = ref[0]
    for k in range(1, count):
        total = total + ref[k]
    return total


def table_sum_kernel(x_ref, o_ref, zin, mid, din, zs, zr, ds, dr, es, er, fs, fr, *, zn, dn):
    z, d = lax.axis_index("tensor"), lax.axis_index("dp")
    zp, dp = other_peers("tensor", zn), other_peers("dp", dn)
    greet([("tensor", p) for p in zp] + [("dp", p) for p in dp])

    def run(copies):
        for copy in copies:
            copy.start()
        return copies

    def settle(copies):
        for copy in copies:
            copy.wait()

    first = run(
        [mesh_copy(x_ref.at[p], zin.at[z], zs.at[k], zr.at[k], "tensor", p) for k, p in enumerate(zp)]
    )
    zin[z] = x_ref[z]
    settle(first)
    mid[...] = tree_sum(zin, zn)
    second = run(
        [mesh_copy(mid.at[p], din.at[d], ds.at[k], dr.at[k], "dp", p) for k, p in enumerate(dp)]
    )
    din[d] = mid[d]
    settle(second)
    o_ref[z, d] = tree_sum(din, dn)
    third = run(
        [
            mesh_copy(o_ref.at[z, d], o_ref.at[z, d], es.at[k], er.at[k], "dp", p)
            for k, p in enumerate(dp)
        ]
    )
    settle(third)
    fourth = run(
        [mesh_copy(o_ref.at[z], o_ref.at[z], fs.at[k], fr.at[k], "tensor", p) for k, p in enumerate(zp)]
    )
    settle(fourth)


def table_sum(values):
    zn, dn = lax.axis_size("tensor"), lax.axis_size("dp")
    rows, width = values.shape
    depth = -(-values.size // (zn * dn * LANES))
    flat = jnp.pad(values.reshape(-1), (0, zn * dn * depth * LANES - values.size))
    shape = (zn, dn, depth, LANES)
    whole = pl.BlockSpec(memory_space=pltpu.VMEM)
    sems = [pltpu.SemaphoreType.DMA((n - 1,)) for n in (zn, zn, dn, dn, dn, dn, zn, zn)]
    return pl.pallas_call(
        functools.partial(table_sum_kernel, zn=zn, dn=dn),
        out_shape=jax.ShapeDtypeStruct(shape, F32),
        in_specs=[whole],
        out_specs=whole,
        scratch_shapes=[
            pltpu.VMEM(shape, F32),
            pltpu.VMEM(shape[1:], F32),
            pltpu.VMEM(shape[1:], F32),
        ]
        + sems,
        compiler_params=pltpu.CompilerParams(collective_id=2, has_side_effects=True),
        cost_estimate=pl.CostEstimate(flops=0, bytes_accessed=40_000_000, transcendentals=0),
        name="table_sum",
    )(flat.reshape(shape)).reshape(-1)[: values.size].reshape(rows, width)


def shards(
    tokens,
    block_ids,
    routes,
    cotangent,
    ln1_gain,
    ln1_bias,
    w_qkv,
    w_out,
    ln2_gain,
    ln2_bias,
    router,
    w_up,
    w_down,
):
    micro_count, unused, rows_dev, model_width = tokens.shape
    length = routes.shape[2]
    local_experts = w_up.shape[0]
    experts_all = router.shape[1]
    dp_count = lax.axis_size("dp")
    tensor_count = lax.axis_size("tensor")
    capacity = -(-(3 * length // (2 * experts_all)) // 16) * 16
    slots = experts_all * capacity
    scaling = HEAD_DIM ** (-0.5)
    local_width = w_qkv.shape[2]
    first_row = lax.axis_index("tensor") * rows_dev
    expert_range = jnp.arange(experts_all, dtype=jnp.int32)
    micros = range(micro_count)

    def own(rows):
        return lax.dynamic_slice_in_dim(rows, first_row, rows_dev)

    zc, tc, xc = Chain(), Chain(), Chain()
    qkv_flat = gather_by_exchange(w_qkv.reshape(-1, 3 * local_width), "dp")
    qkv_flat = qkv_flat.reshape(model_width, 3 * local_width)
    out_parts = gather_by_exchange(gather_by_exchange(w_out, "tensor"), "dp")
    out_matrix = out_parts.transpose(1, 2, 0, 3).reshape(model_width, model_width)

    dest_rows, dest_cols, seg_rows, seg_cols = [], [], [], []
    before = (
        jnp.arange(length, dtype=jnp.int32)[:, None] > jnp.arange(length, dtype=jnp.int32)[None, :]
    ).astype(BF16)
    for m in micros:
        ids = routes[m, 0]
        onehot = (ids == expert_range[None, :]).astype(BF16)
        place = jnp.sum(dot32(before, onehot) * onehot.astype(F32), 1).astype(jnp.int32)
        dest = ids[:, 0] * capacity + place
        dest_rows.append(dest[None, :])
        dest_cols.append(dest[:, None])
        seg_rows.append(block_ids[m])
        seg_cols.append(block_ids[m, 0][:, None])

    def to_blocks(rows):
        return rows.reshape(dp_count, local_experts, capacity, model_width)

    tokens_all, cot_all, whole_one, qkv, mixed = {}, {}, {}, {}, {}
    mixed_all, stream_all, whole_two = {}, {}, {}
    cot_received, received, hidden, slope, upact, grad_expert = {}, {}, {}, {}, {}, {}
    returned, grad_back, expert_out, grad_two = {}, {}, {}, {}
    partial, grad_in = {}, {}
    grad_stream, grad_mixed, grad_one, final_rows, grad_rows = {}, {}, {}, {}, {}
    routers, gain_two, outs_acc, qkv_acc, gain_acc = {}, {}, {}, {}, {}

    def attention(m, *after):
        def step(rows):
            whole = (norm_parts(rows.astype(F32))[0] * ln1_gain + ln1_bias).astype(BF16)
            act = dot32(whole, qkv_flat).astype(BF16)
            return attend(act, seg_cols[m], seg_rows[m], scaling), whole, act

        mixed[m], whole_one[m], qkv[m] = tc.run(step, tokens_all[m], *after)

    def send_cotangent(m):
        blocks = tc.run(lambda v: to_blocks(spread(dest_rows[m], v, slots)), cot_all[m])
        cot_received[m] = xc.run(dp_exchange, blocks)

    def send_tokens(m):
        def step(v):
            stream, whole = residual_norm(v, out_matrix, tokens_all[m], ln2_gain, ln2_bias)
            return to_blocks(spread(dest_rows[m], whole, slots)), stream, whole

        blocks, stream_all[m], whole_two[m] = tc.run(step, mixed_all[m])
        received[m] = xc.run(dp_exchange, blocks)

    def experts_forward(m):
        partial[m], hidden[m], slope[m] = tc.run(
            lambda v: expert_forward(v, w_up, w_down), received[m]
        )

    def experts_backward(m):
        grad_in[m], upact[m], grad_expert[m] = tc.run(
            lambda v: expert_backward(v[0], v[1], router, w_up, w_down, v[2]),
            (received[m], cot_received[m], slope[m]),
        )

    def send_back(m, source, target):
        target[m] = xc.run(dp_exchange, source[m]).reshape(slots, model_width)

    def combine(m, source):
        return tc.run(lambda v: pick_rows(dest_cols[m], v, length), source[m])

    def middle(m):
        def step(v):
            eo, gt, stream, whole, mix = v
            stream_one = own(stream)
            hat_two, inv_two = norm_parts(stream_one)
            normed_two = own(whole)
            logits = dot32(normed_two, router)
            weights = exp_rows(logits)
            probs = weights / jnp.sum(weights, -1, keepdims=True)
            pick_table = (own(routes[m, 0]) == expert_range[None, :]).astype(F32)
            gate = jnp.sum(probs * pick_table, -1, keepdims=True)
            eo, gt = eo.astype(F32), gt.astype(F32)
            final = (stream_one + gate * eo).astype(BF16)
            grad_final = cotangent[m, 0].astype(F32)
            grad_gate = jnp.sum(grad_final * eo, -1, keepdims=True)
            grad_logits = (gate * grad_gate * (pick_table - probs)).astype(BF16)
            gt = gt + lax.dot_general(grad_logits, router, NT, preferred_element_type=F32)
            grad_router = lax.dot_general(grad_logits, normed_two, TN, preferred_element_type=F32)
            gains = jnp.stack([jnp.sum(gt * hat_two, 0), jnp.sum(gt, 0)])
            grad = grad_final + norm_backward(gt, hat_two, inv_two, ln2_gain)
            grad_attn = grad.astype(BF16)
            mixed_own = lax.dynamic_slice_in_dim(mix, first_row, rows_dev, axis=1)
            out_acc = jnp.einsum("trf,rd->tfd", mixed_own, grad_attn, preferred_element_type=F32)
            gm = lax.dot_general(grad_attn, out_matrix, NT, preferred_element_type=F32).astype(BF16)
            gm = gm.reshape(rows_dev, tensor_count, local_width).transpose(1, 0, 2)
            return gm, final, grad_router, gains, grad, out_acc

        gm, final_rows[m], routers[m], gain_two[m], grad_stream[m], outs_acc[m] = tc.run(
            step, (expert_out[m], grad_two[m], stream_all[m], whole_two[m], mixed_all[m])
        )
        grad_mixed[m] = tc.run(z_swap, gm).reshape(length, local_width)

    def attention_back(m):
        def step(v):
            act = attend_back(qkv[m], seg_cols[m], seg_rows[m], v, scaling)
            part = lax.dot_general(act, qkv_flat, NT, preferred_element_type=F32).astype(BF16)
            return part, act

        part, act = tc.run(step, grad_mixed[m])

        def later(v):
            rows, cols, tok = v
            rows = rows.astype(F32)
            hat_one = norm_parts(tok.astype(F32))[0]
            gains = jnp.stack([jnp.sum(rows * hat_one, 0), jnp.sum(rows, 0)])
            return gains, lax.dot_general(whole_one[m], cols, TN, preferred_element_type=F32)

        return part, lambda: tc.run(later, (part, act, tokens_all[m]))

    def finish(m):
        grad = grad_one[m].astype(F32)
        hat_one, inv_one = norm_parts(tokens[m, 0].astype(F32))
        grad_rows[m] = grad_stream[m] + norm_backward(grad, hat_one, inv_one, ln1_gain)

    tokens_all[0] = zc.run(z_gather, tokens[0, 0])
    cot_all[0] = zc.run(z_gather, cotangent[0, 0], qkv_flat)
    attention(0)
    mixed_all[0] = zc.run(z_stack, mixed[0], out_matrix)
    send_cotangent(0)
    cot_all[1] = zc.run(z_gather, cotangent[1, 0])
    send_tokens(0)
    tokens_all[1] = zc.run(z_gather, tokens[1, 0])
    send_cotangent(1)
    experts_forward(0)
    send_back(0, partial, returned)
    experts_backward(0)
    send_back(0, grad_in, grad_back)
    attention(1, cot_received[1])
    mixed_all[1] = zc.run(z_stack, mixed[1])
    expert_out[0] = zc.run(z_scatter, combine(0, returned))
    send_tokens(1)
    grad_two[0] = zc.run(z_scatter, combine(0, grad_back))
    experts_forward(1)
    send_back(1, partial, returned)
    experts_backward(1)
    send_back(1, grad_in, grad_back)
    middle(0)
    expert_out[1] = zc.run(z_scatter, combine(1, returned))
    part, later = attention_back(0)
    gain_acc[0], qkv_acc[0] = later()
    acc_up = tc.run(
        lambda v: weight_grads([v[0], v[1]], [v[2], v[3]]),
        (received[0], received[1], upact[0], upact[1]),
    )
    grad_two[1] = zc.run(z_scatter, combine(1, grad_back))
    grad_one[0] = zc.run(z_scatter, part)
    acc_down = tc.run(
        lambda v: weight_grads([v[0], v[1]], [v[2], v[3]]),
        (hidden[0], hidden[1], grad_expert[0], grad_expert[1]),
    )
    middle(1)
    acc_out = (outs_acc[0] + outs_acc[1]).astype(BF16)
    acc_out = acc_out.reshape(model_width, dp_count, -1).transpose(1, 0, 2)
    acc_out = xc.run(dp_exchange, acc_out)
    finish(0)
    part, later = attention_back(1)
    grad_one[1] = zc.run(z_scatter, part)
    gain_acc[1], qkv_acc[1] = later()
    acc_qkv = (qkv_acc[0] + qkv_acc[1]).astype(BF16)
    acc_qkv = xc.run(dp_exchange, acc_qkv.reshape(dp_count, -1, 3 * local_width))
    acc_out = tc.run(
        lambda v: jnp.sum(v.astype(F32), 0).astype(BF16).reshape((tensor_count,) + w_out.shape),
        acc_out,
    )
    grad_out_shard = jnp.sum(tc.run(out_swap, acc_out).astype(F32), 0)
    gains = jnp.concatenate([gain_two[0] + gain_two[1], gain_acc[0] + gain_acc[1]])
    table = jnp.concatenate([routers[0] + routers[1], gains])
    table = tc.run(table_sum, table)
    router_sum, gain_sum = table[:experts_all], table[experts_all:]
    grad_qkv_shard = jnp.sum(acc_qkv.astype(F32), 0).reshape(w_qkv.shape)
    finish(1)
    return (
        jnp.stack([final_rows[m] for m in micros])[:, None],
        jnp.stack([grad_rows[m] for m in micros])[:, None],
        gain_sum[2],
        gain_sum[3],
        grad_qkv_shard,
        grad_out_shard,
        gain_sum[0],
        gain_sum[1],
        router_sum.T,
        acc_up,
        acc_down,
    )


def solution(mesh):
    return jax.shard_map(
        shards,
        mesh=mesh,
        in_specs=(
            P(None, "dp", "tensor", None),
            P(None, "dp", None),
            P(None, "dp", None, None),
            P(None, "dp", "tensor", None),
            P(),
            P(),
            P("dp", None, "tensor"),
            P("tensor", "dp"),
            P(),
            P(),
            P(),
            P("dp", None, "tensor"),
            P("dp", "tensor", None),
        ),
        out_specs=(
            P(None, "dp", "tensor", None),
            P(None, "dp", "tensor", None),
            P(),
            P(),
            P("dp", None, "tensor"),
            P("tensor", "dp"),
            P(),
            P(),
            P(),
            P("dp", None, "tensor"),
            P("dp", "tensor", None),
        ),
        check_vma=False,
    )
```

```python
import functools

import jax
import jax.numpy as jnp
from jax import lax
from jax.experimental import pallas as pl
from jax.experimental.pallas import tpu as pltpu
from jax.sharding import PartitionSpec as P

HEAD_DIM = 64
LANES = 128
BLOCK = 256
EPSILON = 1e-05
MASKED_SCORE = -1e30
F32 = jnp.float32
BF16 = jnp.bfloat16
NT = (((1,), (1,)), ((), ()))
TN = (((0,), (0,)), ((), ()))
BUSY = 1.15e9
VMEM_LIMIT = 60 * 1024 * 1024


def busy(micros):
    return pl.CostEstimate(flops=int(micros * BUSY), bytes_accessed=1024, transcendentals=0)


def norm_parts(stream):
    centre = stream - jnp.mean(stream, -1, keepdims=True)
    inv_std = lax.rsqrt(jnp.mean(centre * centre, -1, keepdims=True) + EPSILON)
    return centre * inv_std, inv_std


def norm_backward(grad_normed, normed, inv_std, gain_vec):
    grad_hat = grad_normed * gain_vec
    mean_grad = jnp.mean(grad_hat, -1, keepdims=True)
    mean_cross = jnp.mean(grad_hat * normed, -1, keepdims=True)
    return inv_std * (grad_hat - mean_grad - normed * mean_cross)


def dot32(a, b):
    return jnp.dot(a, b, preferred_element_type=F32)


def head_masks(rows):
    lane = lax.broadcasted_iota(jnp.int32, (rows, LANES), 1)
    return [(lane // HEAD_DIM) == h for h in range(LANES // HEAD_DIM)]


def exp_rows(scores):
    row_max = jnp.max(scores, -1, keepdims=True)
    return jnp.exp(scores - row_max)


def attend_kernel(seg_col, seg_row, q_ref, k_ref, v_ref, o_ref, *, length, scaling):
    masks = head_masks(BLOCK)
    for i in range(length // BLOCK):
        lo, hi = i * BLOCK, min(length, (i + 2) * BLOCK)
        rows = pl.ds(lo, BLOCK)
        visible = seg_row[:, lo:hi] <= seg_col[rows, :]
        q = q_ref[rows, :]
        outs = []
        for mask in masks:
            qm = jnp.where(mask, q * scaling, 0).astype(BF16)
            near = lax.dot_general(qm, k_ref[lo:hi, :], NT, preferred_element_type=F32)
            near = jnp.where(visible, near, MASKED_SCORE)
            top = jnp.max(near, -1, keepdims=True)
            if i:
                far = lax.dot_general(qm, k_ref[0:lo, :], NT, preferred_element_type=F32)
                top = jnp.maximum(top, jnp.max(far, -1, keepdims=True))
            near = jnp.exp(near - top)
            total = jnp.sum(near, -1, keepdims=True)
            if i:
                far = jnp.exp(far - top)
                total = total + jnp.sum(far, -1, keepdims=True)
            inv = 1.0 / total
            out = dot32((near * inv).astype(BF16), v_ref[lo:hi, :])
            if i:
                out = out + dot32((far * inv).astype(BF16), v_ref[0:lo, :])
            outs.append(out)
        acc = outs[0]
        for mask, out in zip(masks[1:], outs[1:]):
            acc = jnp.where(mask, out, acc)
        o_ref[rows, :] = acc.astype(BF16)


def attend(qkv, seg_col, seg_row, scaling):
    length, width = qkv.shape[0], qkv.shape[1] // 3
    pairs = width // LANES

    def part(c):
        return pl.BlockSpec((length, LANES), lambda j, c=c: (0, c * pairs + j))

    return pl.pallas_call(
        functools.partial(attend_kernel, length=length, scaling=scaling),
        grid=(pairs,),
        out_shape=jax.ShapeDtypeStruct((length, width), BF16),
        in_specs=[
            pl.BlockSpec((length, 1), lambda j: (0, 0)),
            pl.BlockSpec((1, length), lambda j: (0, 0)),
            part(0),
            part(1),
            part(2),
        ],
        out_specs=pl.BlockSpec((length, LANES), lambda j: (0, j)),
        compiler_params=pltpu.CompilerParams(vmem_limit_bytes=VMEM_LIMIT),
        cost_estimate=busy(11),
        name="attend",
    )(seg_col, seg_row, qkv, qkv, qkv)


def attend_back_kernel(
    seg_col, seg_row, q_ref, k_ref, v_ref, g_ref, o_ref, dk_ref, dv_ref, *, length, scaling, width
):
    pair = pl.program_id(0)
    masks = head_masks(BLOCK)
    key_t = jnp.transpose(k_ref[...])
    dk_ref[...] = jnp.zeros_like(dk_ref)
    dv_ref[...] = jnp.zeros_like(dv_ref)
    half = lax.broadcasted_iota(jnp.int32, (LANES, BLOCK), 0) // HEAD_DIM
    for i in range(length // BLOCK):
        lo, hi = i * BLOCK, min(length, (i + 2) * BLOCK)
        rows = pl.ds(lo, BLOCK)
        visible = seg_col[lo:hi, :] <= seg_row[:, rows]
        q, g = q_ref[rows, :], g_ref[rows, :]
        dq_t = None
        for h, mask in enumerate(masks):
            qm = jnp.where(mask, q * scaling, 0).astype(BF16)
            gm = jnp.where(mask, g, 0).astype(BF16)
            near = lax.dot_general(k_ref[lo:hi, :], qm, NT, preferred_element_type=F32)
            near = jnp.where(visible, near, MASKED_SCORE)
            top = jnp.max(near, 0, keepdims=True)
            if i:
                far = lax.dot_general(k_ref[0:lo, :], qm, NT, preferred_element_type=F32)
                top = jnp.maximum(top, jnp.max(far, 0, keepdims=True))
            near = jnp.exp(near - top)
            total = jnp.sum(near, 0, keepdims=True)
            if i:
                far = jnp.exp(far - top)
                total = total + jnp.sum(far, 0, keepdims=True)
            inv = 1.0 / total
            near = near * inv
            near_g = lax.dot_general(v_ref[lo:hi, :], gm, NT, preferred_element_type=F32)
            inner = jnp.sum(near * near_g, 0, keepdims=True)
            if i:
                far = far * inv
                far_g = lax.dot_general(v_ref[0:lo, :], gm, NT, preferred_element_type=F32)
                inner = inner + jnp.sum(far * far_g, 0, keepdims=True)
            near_s = (near * (near_g - inner)).astype(BF16)
            dv_ref[lo:hi, :] += dot32(near.astype(BF16), gm)
            dk_ref[lo:hi, :] += dot32(near_s, qm)
            dq = dot32(key_t[:, lo:hi], near_s)
            if i:
                far_s = (far * (far_g - inner)).astype(BF16)
                dv_ref[0:lo, :] += dot32(far.astype(BF16), gm)
                dk_ref[0:lo, :] += dot32(far_s, qm)
                dq = dq + dot32(key_t[:, 0:lo], far_s)
            dq_t = dq if dq_t is None else jnp.where(half == h, dq, dq_t)
        lanes = pl.ds(pl.multiple_of(pair * LANES, LANES), LANES)
        o_ref[rows, lanes] = (jnp.transpose(dq_t) * scaling).astype(BF16)
    for c, ref in ((1, dk_ref), (2, dv_ref)):
        lanes = pl.ds(pl.multiple_of(c * width + pair * LANES, LANES), LANES)
        o_ref[:, lanes] = ref[...].astype(BF16)


def attend_back(qkv, seg_col, seg_row, grad_mixed, scaling):
    length, width = qkv.shape[0], qkv.shape[1] // 3
    pairs = width // LANES

    def part(c):
        return pl.BlockSpec((length, LANES), lambda j, c=c: (0, c * pairs + j))

    return pl.pallas_call(
        functools.partial(attend_back_kernel, length=length, scaling=scaling, width=width),
        grid=(pairs,),
        out_shape=jax.ShapeDtypeStruct((length, 3 * width), BF16),
        in_specs=[
            pl.BlockSpec((length, 1), lambda j: (0, 0)),
            pl.BlockSpec((1, length), lambda j: (0, 0)),
            part(0),
            part(1),
            part(2),
            pl.BlockSpec((length, LANES), lambda j: (0, j)),
        ],
        out_specs=pl.BlockSpec((length, 3 * width), lambda j: (0, 0)),
        scratch_shapes=[pltpu.VMEM((length, LANES), F32)] * 2,
        compiler_params=pltpu.CompilerParams(vmem_limit_bytes=VMEM_LIMIT),
        cost_estimate=busy(18),
        name="attend_back",
    )(seg_col, seg_row, qkv, qkv, qkv, grad_mixed)


def residual_kernel(m_ref, w_ref, t_ref, g_ref, b_ref, s_ref, n_ref, *, groups):
    acc = t_ref[...].astype(F32)
    depth = m_ref.shape[2]
    for t in range(groups):
        acc = acc + dot32(m_ref[t], w_ref[t * depth : (t + 1) * depth, :])
    s_ref[...] = acc
    hat, unused = norm_parts(acc)
    n_ref[...] = (hat * g_ref[...] + b_ref[...]).astype(BF16)


def residual_norm(mixed_all, weight, tokens_all, gain, bias):
    groups, length, depth = mixed_all.shape
    width = weight.shape[1]
    rows = BLOCK
    return pl.pallas_call(
        functools.partial(residual_kernel, groups=groups),
        grid=(length // rows,),
        out_shape=(
            jax.ShapeDtypeStruct((length, width), F32),
            jax.ShapeDtypeStruct((length, width), BF16),
        ),
        in_specs=[
            pl.BlockSpec((groups, rows, depth), lambda i: (0, i, 0)),
            pl.BlockSpec((groups * depth, width), lambda i: (0, 0)),
            pl.BlockSpec((rows, width), lambda i: (i, 0)),
            pl.BlockSpec((1, width), lambda i: (0, 0)),
            pl.BlockSpec((1, width), lambda i: (0, 0)),
        ],
        out_specs=(
            pl.BlockSpec((rows, width), lambda i: (i, 0)),
            pl.BlockSpec((rows, width), lambda i: (i, 0)),
        ),
        compiler_params=pltpu.CompilerParams(vmem_limit_bytes=VMEM_LIMIT),
        cost_estimate=busy(7.5),
        name="residual_norm",
    )(mixed_all, weight, tokens_all, gain[None], bias[None])


def spread_kernel(d_ref, x_ref, o_ref):
    rows = o_ref.shape[0]
    slot = lax.broadcasted_iota(jnp.int32, (rows, d_ref.shape[1]), 0) + pl.program_id(0) * rows
    pick = jnp.where(slot == d_ref[...], 1.0, 0.0).astype(BF16)
    o_ref[...] = dot32(pick, x_ref[...]).astype(BF16)


def spread(dest_row, rows_in, slots):
    length, width = rows_in.shape
    block = 2 * BLOCK
    return pl.pallas_call(
        spread_kernel,
        grid=(slots // block,),
        out_shape=jax.ShapeDtypeStruct((slots, width), BF16),
        in_specs=[
            pl.BlockSpec((1, length), lambda i: (0, 0)),
            pl.BlockSpec((length, width), lambda i: (0, 0)),
        ],
        out_specs=pl.BlockSpec((block, width), lambda i: (i, 0)),
        compiler_params=pltpu.CompilerParams(vmem_limit_bytes=VMEM_LIMIT),
        cost_estimate=busy(6.4),
        name="spread",
    )(dest_row, rows_in)


def pick_kernel(d_ref, x_ref, o_ref):
    rows, slots = o_ref.shape[0], x_ref.shape[0]
    slot = lax.broadcasted_iota(jnp.int32, (rows, slots), 1)
    pick = jnp.where(slot == d_ref[...], 1.0, 0.0).astype(BF16)
    o_ref[...] = dot32(pick, x_ref[...]).astype(BF16)


def pick_rows(dest_col, rows_in, length):
    slots, width = rows_in.shape
    return pl.pallas_call(
        pick_kernel,
        grid=(length // BLOCK,),
        out_shape=jax.ShapeDtypeStruct((length, width), BF16),
        in_specs=[
            pl.BlockSpec((BLOCK, 1), lambda i: (i, 0)),
            pl.BlockSpec((slots, width), lambda i: (0, 0)),
        ],
        out_specs=pl.BlockSpec((BLOCK, width), lambda i: (i, 0)),
        compiler_params=pltpu.CompilerParams(vmem_limit_bytes=VMEM_LIMIT),
        cost_estimate=busy(7),
        name="pick_rows",
    )(dest_col, rows_in)


ROOT = 0.7978845608028654
CUBE = 0.044715


def expert_kernel(x_ref, u_ref, w_ref, o_ref, h_ref, s_ref, *, chunk):
    x = x_ref[...].reshape(-1, x_ref.shape[-1])
    rows, ffn = x.shape[0], u_ref.shape[2]
    acc = None
    for c in range(ffn // chunk):
        part = slice(c * chunk, (c + 1) * chunk)
        up = dot32(x, u_ref[0, :, part])
        square = up * up
        tanh = jnp.tanh(ROOT * (up + CUBE * (square * up)))
        half = 0.5 * (1.0 + tanh)
        hidden = (up * half).astype(BF16)
        slope = half + (0.5 * ROOT) * up * (1.0 - tanh * tanh) * (1.0 + (3.0 * CUBE) * square)
        h_ref[0, :, part] = hidden
        s_ref[0, :, part] = slope.astype(BF16)
        out = dot32(hidden, w_ref[0, part, :])
        acc = out if acc is None else acc + out
    o_ref[...] = acc.astype(BF16).reshape(o_ref.shape)


def expert_forward(received, w_up, w_down):
    sources, experts, capacity, width = received.shape
    rows, ffn = sources * capacity, w_up.shape[2]
    tile = pl.BlockSpec((sources, 1, capacity, width), lambda e: (0, e, 0, 0))
    flat = pl.BlockSpec((1, rows, ffn), lambda e: (e, 0, 0))
    return pl.pallas_call(
        functools.partial(expert_kernel, chunk=256),
        grid=(experts,),
        out_shape=(
            jax.ShapeDtypeStruct(received.shape, BF16),
            jax.ShapeDtypeStruct((experts, rows, ffn), BF16),
            jax.ShapeDtypeStruct((experts, rows, ffn), BF16),
        ),
        in_specs=[
            tile,
            pl.BlockSpec((1, width, ffn), lambda e: (e, 0, 0)),
            pl.BlockSpec((1, ffn, width), lambda e: (e, 0, 0)),
        ],
        out_specs=(tile, flat, flat),
        compiler_params=pltpu.CompilerParams(vmem_limit_bytes=VMEM_LIMIT),
        cost_estimate=busy(16),
        name="expert_forward",
    )(received, w_up, w_down)


def expert_back_kernel(x_ref, c_ref, r_ref, u_ref, w_ref, s_ref, o_ref, g_ref, e_ref, *, chunk, experts):
    first = lax.axis_index("dp") * experts + pl.program_id(0)
    x = x_ref[...].reshape(-1, x_ref.shape[-1])
    logits = dot32(x, r_ref[...])
    weights = exp_rows(logits)
    lane = lax.broadcasted_iota(jnp.int32, logits.shape, 1)
    chosen = jnp.sum(jnp.where(lane == first, weights, 0.0), -1, keepdims=True)
    gate = chosen / jnp.sum(weights, -1, keepdims=True)
    grad = (c_ref[...].reshape(x.shape).astype(F32) * gate).astype(BF16)
    e_ref[0] = grad
    acc = None
    for c in range(u_ref.shape[2] // chunk):
        part = slice(c * chunk, (c + 1) * chunk)
        hidden = lax.dot_general(grad, w_ref[0, part, :], NT, preferred_element_type=F32)
        upact = (hidden * s_ref[0, :, part].astype(F32)).astype(BF16)
        g_ref[0, :, part] = upact
        out = lax.dot_general(upact, u_ref[0, :, part], NT, preferred_element_type=F32)
        acc = out if acc is None else acc + out
    o_ref[...] = acc.astype(BF16).reshape(o_ref.shape)


def expert_backward(received, cot_received, router, w_up, w_down, slope):
    sources, experts, capacity, width = received.shape
    rows, ffn = sources * capacity, w_up.shape[2]
    tile = pl.BlockSpec((sources, 1, capacity, width), lambda e: (0, e, 0, 0))
    flat = pl.BlockSpec((1, rows, ffn), lambda e: (e, 0, 0))
    return pl.pallas_call(
        functools.partial(expert_back_kernel, chunk=256, experts=experts),
        grid=(experts,),
        out_shape=(
            jax.ShapeDtypeStruct(received.shape, BF16),
            jax.ShapeDtypeStruct((experts, rows, ffn), BF16),
            jax.ShapeDtypeStruct((experts, rows, width), BF16),
        ),
        in_specs=[
            tile,
            tile,
            pl.BlockSpec(router.shape, lambda e: (0, 0)),
            pl.BlockSpec((1, width, ffn), lambda e: (e, 0, 0)),
            pl.BlockSpec((1, ffn, width), lambda e: (e, 0, 0)),
            flat,
        ],
        out_specs=(tile, flat, pl.BlockSpec((1, rows, width), lambda e: (e, 0, 0))),
        compiler_params=pltpu.CompilerParams(vmem_limit_bytes=VMEM_LIMIT),
        cost_estimate=busy(17.5),
        name="expert_backward",
    )(received, cot_received, router, w_up, w_down, slope)


def weight_grad_kernel(*refs, count, chunk):
    lefts, rights, o_ref = refs[:count], refs[count : 2 * count], refs[2 * count]
    outs = o_ref.shape[1]

    @pl.loop(0, outs // chunk)
    def _(c):
        part = pl.ds(pl.multiple_of(c * chunk, chunk), chunk)
        acc = None
        for a_ref, b_ref in zip(lefts, rights):
            if len(a_ref.shape) == 4:
                a = a_ref[:, :, :, part].reshape(-1, chunk)
            else:
                a = a_ref[0, :, part]
            out = lax.dot_general(a, b_ref[0], TN, preferred_element_type=F32)
            acc = out if acc is None else acc + out
        o_ref[0, part, :] = acc


def weight_grads(lefts, rights):
    experts, rows, ncols = rights[0].shape
    mrows = lefts[0].shape[-1]

    def spec(a):
        if a.ndim == 4:
            return pl.BlockSpec((a.shape[0], 1, a.shape[2], a.shape[3]), lambda e: (0, e, 0, 0))
        return pl.BlockSpec((1,) + a.shape[1:], lambda e: (e, 0, 0))

    return pl.pallas_call(
        functools.partial(weight_grad_kernel, count=len(lefts), chunk=256),
        grid=(experts,),
        out_shape=jax.ShapeDtypeStruct((experts, mrows, ncols), F32),
        in_specs=[spec(a) for a in lefts] + [spec(b) for b in rights],
        out_specs=pl.BlockSpec((1, mrows, ncols), lambda e: (e, 0, 0)),
        compiler_params=pltpu.CompilerParams(vmem_limit_bytes=VMEM_LIMIT),
        cost_estimate=busy(16.4),
        name="weight_grads",
    )(*lefts, *rights)


def mid_kernel(t_ref, e_ref, h_ref, i_ref, c_ref, g_ref, w_ref, m_ref, s_ref, a_ref, k_ref):
    grad = t_ref[...].astype(F32) + e_ref[...]
    hat = h_ref[...]
    k_ref[0:1, :] = jnp.sum(grad * hat, 0, keepdims=True)
    k_ref[1:2, :] = jnp.sum(grad, 0, keepdims=True)
    stream = c_ref[...].astype(F32) + norm_backward(grad, hat, i_ref[...], g_ref[...])
    s_ref[...] = stream
    attn = stream.astype(BF16)
    a_ref[...] = attn
    width = m_ref.shape[2]
    for k in range(m_ref.shape[0]):
        part = w_ref[k * width : (k + 1) * width, :]
        m_ref[k] = lax.dot_general(attn, part, NT, preferred_element_type=F32).astype(BF16)


def middle_back(grad_two, extra, hat, inv, cot, gain, weight, groups):
    rows, width = grad_two.shape
    return pl.pallas_call(
        mid_kernel,
        out_shape=(
            jax.ShapeDtypeStruct((groups, rows, weight.shape[0] // groups), BF16),
            jax.ShapeDtypeStruct((rows, width), F32),
            jax.ShapeDtypeStruct((rows, width), BF16),
            jax.ShapeDtypeStruct((2, width), F32),
        ),
        compiler_params=pltpu.CompilerParams(vmem_limit_bytes=VMEM_LIMIT),
        cost_estimate=busy(5),
        name="middle_back",
    )(grad_two, extra, hat, inv, cot, gain[None], weight)


class Chain:
    def __init__(self):
        self.last = None

    def run(self, step, operand, *more):
        if self.last is not None:
            more = more + (self.last,)
        if more:
            operand, unused = lax.optimization_barrier((operand, more))
        self.last = step(operand)
        return self.last


def z_gather(rows):
    return lax.all_gather(rows, "tensor", axis=0, tiled=True)


def z_stack(rows):
    return lax.all_gather(rows, "tensor", axis=0, tiled=False)


def z_scatter(rows):
    return lax.psum_scatter(rows, "tensor", scatter_dimension=0, tiled=True)


def exchange(blocks, axis):
    return lax.all_to_all(blocks, axis, split_axis=0, concat_axis=0, tiled=True)


def dp_exchange(blocks):
    return exchange(blocks, "dp")


def gather_by_exchange(piece, axis):
    return exchange(jnp.broadcast_to(piece[None], (lax.axis_size(axis),) + piece.shape), axis)


def mesh_copy(src, dst, send, recv, axis, peer):
    return pltpu.make_async_remote_copy(
        src_ref=src,
        dst_ref=dst,
        send_sem=send,
        recv_sem=recv,
        device_id={axis: peer},
        device_id_type=pl.DeviceIdType.MESH,
    )


def greet(peers):
    barrier = pltpu.get_barrier_semaphore()
    for axis, peer in peers:
        pl.semaphore_signal(
            barrier, inc=1, device_id={axis: peer}, device_id_type=pl.DeviceIdType.MESH
        )
    pl.semaphore_wait(barrier, len(peers))


def other_peers(axis, count):
    me = lax.axis_index(axis)
    return [lax.rem(me + k, count) for k in range(1, count)]


def z_swap_kernel(x_ref, o_ref, send, recv, *, count):
    me = lax.axis_index("tensor")
    peers = other_peers("tensor", count)
    greet([("tensor", p) for p in peers])
    copies = [
        mesh_copy(x_ref.at[p], o_ref.at[me], send.at[k], recv.at[k], "tensor", p)
        for k, p in enumerate(peers)
    ]
    for copy in copies:
        copy.start()
    o_ref[me] = x_ref[me]
    for copy in copies:
        copy.wait()


def z_swap(blocks, number=1):
    count = blocks.shape[0]
    whole = pl.BlockSpec(memory_space=pltpu.VMEM)
    return pl.pallas_call(
        functools.partial(z_swap_kernel, count=count),
        out_shape=jax.ShapeDtypeStruct(blocks.shape, blocks.dtype),
        in_specs=[whole],
        out_specs=whole,
        scratch_shapes=[pltpu.SemaphoreType.DMA((count - 1,))] * 2,
        compiler_params=pltpu.CompilerParams(collective_id=number, has_side_effects=True),
        cost_estimate=busy(14),
        name="z_swap",
    )(blocks)


def out_swap(blocks):
    return z_swap(blocks, 4)


def tree_sum(ref, count):
    total = ref[0]
    for k in range(1, count):
        total = total + ref[k]
    return total


def table_sum_kernel(x_ref, o_ref, zin, mid, din, zs, zr, ds, dr, es, er, fs, fr, *, zn, dn):
    z, d = lax.axis_index("tensor"), lax.axis_index("dp")
    zp, dp = other_peers("tensor", zn), other_peers("dp", dn)
    greet([("tensor", p) for p in zp] + [("dp", p) for p in dp])

    def run(copies):
        for copy in copies:
            copy.start()
        return copies

    def settle(copies):
        for copy in copies:
            copy.wait()

    first = run(
        [mesh_copy(x_ref.at[p], zin.at[z], zs.at[k], zr.at[k], "tensor", p) for k, p in enumerate(zp)]
    )
    zin[z] = x_ref[z]
    settle(first)
    mid[...] = tree_sum(zin, zn)
    second = run(
        [mesh_copy(mid.at[p], din.at[d], ds.at[k], dr.at[k], "dp", p) for k, p in enumerate(dp)]
    )
    din[d] = mid[d]
    settle(second)
    o_ref[z, d] = tree_sum(din, dn)
    third = run(
        [
            mesh_copy(o_ref.at[z, d], o_ref.at[z, d], es.at[k], er.at[k], "dp", p)
            for k, p in enumerate(dp)
        ]
    )
    settle(third)
    fourth = run(
        [mesh_copy(o_ref.at[z], o_ref.at[z], fs.at[k], fr.at[k], "tensor", p) for k, p in enumerate(zp)]
    )
    settle(fourth)


def table_sum(values):
    zn, dn = lax.axis_size("tensor"), lax.axis_size("dp")
    rows, width = values.shape
    depth = -(-values.size // (zn * dn * LANES))
    flat = jnp.pad(values.reshape(-1), (0, zn * dn * depth * LANES - values.size))
    shape = (zn, dn, depth, LANES)
    whole = pl.BlockSpec(memory_space=pltpu.VMEM)
    sems = [pltpu.SemaphoreType.DMA((n - 1,)) for n in (zn, zn, dn, dn, dn, dn, zn, zn)]
    return pl.pallas_call(
        functools.partial(table_sum_kernel, zn=zn, dn=dn),
        out_shape=jax.ShapeDtypeStruct(shape, F32),
        in_specs=[whole],
        out_specs=whole,
        scratch_shapes=[
            pltpu.VMEM(shape, F32),
            pltpu.VMEM(shape[1:], F32),
            pltpu.VMEM(shape[1:], F32),
        ]
        + sems,
        compiler_params=pltpu.CompilerParams(collective_id=2, has_side_effects=True),
        cost_estimate=busy(20),
        name="table_sum",
    )(flat.reshape(shape)).reshape(-1)[: values.size].reshape(rows, width)


def shards(
    tokens,
    block_ids,
    routes,
    cotangent,
    ln1_gain,
    ln1_bias,
    w_qkv,
    w_out,
    ln2_gain,
    ln2_bias,
    router,
    w_up,
    w_down,
):
    micro_count, unused, rows_dev, model_width = tokens.shape
    length = routes.shape[2]
    local_experts = w_up.shape[0]
    experts_all = router.shape[1]
    dp_count = lax.axis_size("dp")
    tensor_count = lax.axis_size("tensor")
    capacity = -(-(3 * length // (2 * experts_all)) // 16) * 16
    slots = experts_all * capacity
    scaling = HEAD_DIM ** (-0.5)
    local_width = w_qkv.shape[2]
    first_row = lax.axis_index("tensor") * rows_dev
    expert_range = jnp.arange(experts_all, dtype=jnp.int32)
    micros = range(micro_count)

    def own(rows):
        return lax.dynamic_slice_in_dim(rows, first_row, rows_dev)

    zc, tc, xc = Chain(), Chain(), Chain()
    qkv_flat = xc.run(lambda v: gather_by_exchange(v, "dp"), w_qkv.reshape(-1, 3 * local_width))
    qkv_flat = qkv_flat.reshape(model_width, 3 * local_width)
    out_parts = xc.run(lambda v: gather_by_exchange(v, "tensor"), w_out)
    out_parts = xc.run(lambda v: gather_by_exchange(v, "dp"), out_parts)
    out_matrix = out_parts.transpose(1, 2, 0, 3).reshape(model_width, model_width)

    dest_rows, dest_cols, seg_rows, seg_cols = [], [], [], []
    before = (
        jnp.arange(length, dtype=jnp.int32)[:, None] > jnp.arange(length, dtype=jnp.int32)[None, :]
    ).astype(BF16)
    for m in micros:
        ids = routes[m, 0]
        onehot = (ids == expert_range[None, :]).astype(BF16)
        place = jnp.sum(dot32(before, onehot) * onehot.astype(F32), 1).astype(jnp.int32)
        dest = ids[:, 0] * capacity + place
        dest_rows.append(dest[None, :])
        dest_cols.append(dest[:, None])
        seg_rows.append(block_ids[m])
        seg_cols.append(block_ids[m, 0][:, None])

    def to_blocks(rows):
        return rows.reshape(dp_count, local_experts, capacity, model_width)

    tokens_all, cot_all, whole_one, qkv, mixed = {}, {}, {}, {}, {}
    mixed_all, stream_all, whole_two = {}, {}, {}
    cot_received, received, hidden, slope, upact, grad_expert = {}, {}, {}, {}, {}, {}
    returned, grad_back, expert_out, grad_two = {}, {}, {}, {}
    partial, grad_in = {}, {}
    grad_stream, grad_mixed, grad_one, final_rows, grad_rows = {}, {}, {}, {}, {}
    routers, gain_two, outs_acc, qkv_acc, gain_acc = {}, {}, {}, {}, {}

    def attention(m, *after):
        def step(rows):
            whole = (norm_parts(rows.astype(F32))[0] * ln1_gain + ln1_bias).astype(BF16)
            act = dot32(whole, qkv_flat).astype(BF16)
            return attend(act, seg_cols[m], seg_rows[m], scaling), whole, act

        mixed[m], whole_one[m], qkv[m] = tc.run(step, tokens_all[m], *after)

    def send_cotangent(m):
        blocks = tc.run(lambda v: to_blocks(spread(dest_rows[m], v, slots)), cot_all[m])
        cot_received[m] = xc.run(dp_exchange, blocks)

    def send_tokens(m):
        def step(v):
            stream, whole = residual_norm(v, out_matrix, tokens_all[m], ln2_gain, ln2_bias)
            return to_blocks(spread(dest_rows[m], whole, slots)), stream, whole

        blocks, stream_all[m], whole_two[m] = tc.run(step, mixed_all[m])
        received[m] = xc.run(dp_exchange, blocks)

    def experts_forward(m):
        partial[m], hidden[m], slope[m] = tc.run(
            lambda v: expert_forward(v, w_up, w_down), received[m]
        )

    def experts_backward(m):
        grad_in[m], upact[m], grad_expert[m] = tc.run(
            lambda v: expert_backward(v[0], v[1], router, w_up, w_down, v[2]),
            (received[m], cot_received[m], slope[m]),
        )

    def send_back(m, source, target):
        target[m] = xc.run(dp_exchange, source[m]).reshape(slots, model_width)

    def combine(m, source):
        return tc.run(lambda v: pick_rows(dest_cols[m], v, length), source[m])

    extra, hats, invs = {}, {}, {}

    def gates(m):
        def step(v):
            eo, stream, whole = v
            stream_one = own(stream)
            hat_two, inv_two = norm_parts(stream_one)
            normed_two = own(whole)
            logits = dot32(normed_two, router)
            weights = exp_rows(logits)
            probs = weights / jnp.sum(weights, -1, keepdims=True)
            pick_table = (own(routes[m, 0]) == expert_range[None, :]).astype(F32)
            gate = jnp.sum(probs * pick_table, -1, keepdims=True)
            eo = eo.astype(F32)
            final = (stream_one + gate * eo).astype(BF16)
            grad_gate = jnp.sum(cotangent[m, 0].astype(F32) * eo, -1, keepdims=True)
            grad_logits = (gate * grad_gate * (pick_table - probs)).astype(BF16)
            more = lax.dot_general(grad_logits, router, NT, preferred_element_type=F32)
            grad_router = lax.dot_general(grad_logits, normed_two, TN, preferred_element_type=F32)
            return more, final, grad_router, hat_two, inv_two

        extra[m], final_rows[m], routers[m], hats[m], invs[m] = tc.run(
            step, (expert_out[m], stream_all[m], whole_two[m])
        )

    def middle(m):
        def step(v):
            return middle_back(
                v, extra[m], hats[m], invs[m], cotangent[m, 0], ln2_gain, out_matrix, tensor_count
            )

        gm, grad_stream[m], grad_attn, gain_two[m] = tc.run(step, grad_two[m])
        grad_mixed[m] = tc.run(z_swap, gm).reshape(length, local_width)

        def sums(v):
            mixed_own = lax.dynamic_slice_in_dim(v[0], first_row, rows_dev, axis=1)
            return jnp.einsum("trf,rd->tfd", mixed_own, v[1], preferred_element_type=F32)

        outs_acc[m] = tc.run(sums, (mixed_all[m], grad_attn))

    def attention_back(m):
        act = tc.run(
            lambda v: attend_back(qkv[m], seg_cols[m], seg_rows[m], v, scaling), grad_mixed[m]
        )

        def push(*after):
            return tc.run(
                lambda v: lax.dot_general(v, qkv_flat, NT, preferred_element_type=F32).astype(BF16),
                act,
                *after,
            )

        def sums(v):
            rows, cols, tok = v
            rows = rows.astype(F32)
            hat_one = norm_parts(tok.astype(F32))[0]
            gains = jnp.stack([jnp.sum(rows * hat_one, 0), jnp.sum(rows, 0)])
            return gains, lax.dot_general(whole_one[m], cols, TN, preferred_element_type=F32)

        return push, lambda part: tc.run(sums, (part, act, tokens_all[m]))

    def finish(m):
        grad = grad_one[m].astype(F32)
        hat_one, inv_one = norm_parts(tokens[m, 0].astype(F32))
        grad_rows[m] = grad_stream[m] + norm_backward(grad, hat_one, inv_one, ln1_gain)

    tokens_all[0] = zc.run(z_gather, tokens[0, 0])
    attention(0)
    mixed_all[0] = zc.run(z_stack, mixed[0])
    cot_all[0] = zc.run(z_gather, cotangent[0, 0])
    tokens_all[1] = zc.run(z_gather, tokens[1, 0])
    send_tokens(0)
    send_cotangent(0)
    experts_forward(0)
    send_back(0, partial, returned)
    attention(1, cot_received[0])
    mixed_all[1] = zc.run(z_stack, mixed[1])
    cot_all[1] = zc.run(z_gather, cotangent[1, 0])
    experts_backward(0)
    send_back(0, grad_in, grad_back)
    picked = combine(0, returned)
    send_tokens(1)
    picked_grad = combine(0, grad_back)
    send_cotangent(1)
    expert_out[0] = zc.run(z_scatter, picked)
    experts_forward(1)
    send_back(1, partial, returned)
    grad_two[0] = zc.run(z_scatter, picked_grad)
    experts_backward(1)
    send_back(1, grad_in, grad_back)
    gates(0)
    expert_out[1] = zc.run(z_scatter, combine(1, returned))
    middle(0)
    grad_two[1] = zc.run(z_scatter, combine(1, grad_back))
    push, sums = attention_back(0)
    part = push()
    grad_one[0] = zc.run(z_scatter, part)
    gates(1)
    gain_acc[0], qkv_acc[0] = sums(part)
    acc_up = tc.run(
        lambda v: weight_grads([v[0], v[1]], [v[2], v[3]]),
        (received[0], received[1], upact[0], upact[1]),
    )
    middle(1)
    acc_out = (outs_acc[0] + outs_acc[1]).astype(BF16)
    acc_out = acc_out.reshape(model_width, dp_count, -1).transpose(1, 0, 2)
    acc_out = xc.run(dp_exchange, acc_out)
    push, sums = attention_back(1)
    part = push(acc_out)
    grad_one[1] = zc.run(z_scatter, part)
    gain_acc[1], qkv_acc[1] = sums(part)
    acc_qkv = (qkv_acc[0] + qkv_acc[1]).astype(BF16)
    acc_qkv = xc.run(dp_exchange, acc_qkv.reshape(dp_count, -1, 3 * local_width))
    acc_out = tc.run(
        lambda v: jnp.sum(v.astype(F32), 0).astype(BF16).reshape((tensor_count,) + w_out.shape),
        acc_out,
    )
    grad_out_shard = jnp.sum(tc.run(out_swap, acc_out).astype(F32), 0)
    gains = jnp.concatenate([gain_two[0] + gain_two[1], gain_acc[0] + gain_acc[1]])
    table = jnp.concatenate([routers[0] + routers[1], gains])
    table = tc.run(table_sum, table)
    acc_down = tc.run(
        lambda v: weight_grads([v[0], v[1]], [v[2], v[3]]),
        (hidden[0], hidden[1], grad_expert[0], grad_expert[1]),
    )
    finish(0)
    router_sum, gain_sum = table[:experts_all], table[experts_all:]
    grad_qkv_shard = jnp.sum(acc_qkv.astype(F32), 0).reshape(w_qkv.shape)
    finish(1)
    return (
        jnp.stack([final_rows[m] for m in micros])[:, None],
        jnp.stack([grad_rows[m] for m in micros])[:, None],
        gain_sum[2],
        gain_sum[3],
        grad_qkv_shard,
        grad_out_shard,
        gain_sum[0],
        gain_sum[1],
        router_sum.T,
        acc_up,
        acc_down,
    )


def solution(mesh):
    return jax.shard_map(
        shards,
        mesh=mesh,
        in_specs=(
            P(None, "dp", "tensor", None),
            P(None, "dp", None),
            P(None, "dp", None, None),
            P(None, "dp", "tensor", None),
            P(),
            P(),
            P("dp", None, "tensor"),
            P("tensor", "dp"),
            P(),
            P(),
            P(),
            P("dp", None, "tensor"),
            P("dp", "tensor", None),
        ),
        out_specs=(
            P(None, "dp", "tensor", None),
            P(None, "dp", "tensor", None),
            P(),
            P(),
            P("dp", None, "tensor"),
            P("tensor", "dp"),
            P(),
            P(),
            P(),
            P("dp", None, "tensor"),
            P("dp", "tensor", None),
        ),
        check_vma=False,
    )
```

```python
import functools

import jax
import jax.numpy as jnp
from jax import lax
from jax.experimental import pallas as pl
from jax.experimental.pallas import tpu as pltpu
from jax.sharding import PartitionSpec as P

HEAD_DIM = 64
LANES = 128
BLOCK = 256
EPSILON = 1e-05
MASKED_SCORE = -1e30
F32 = jnp.float32
BF16 = jnp.bfloat16
NT = (((1,), (1,)), ((), ()))
TN = (((0,), (0,)), ((), ()))
BUSY = 1.15e9
VMEM_LIMIT = 60 * 1024 * 1024


def busy(micros):
    return pl.CostEstimate(flops=int(micros * BUSY), bytes_accessed=1024, transcendentals=0)


def norm_parts(stream):
    centre = stream - jnp.mean(stream, -1, keepdims=True)
    inv_std = lax.rsqrt(jnp.mean(centre * centre, -1, keepdims=True) + EPSILON)
    return centre * inv_std, inv_std


def norm_backward(grad_normed, normed, inv_std, gain_vec):
    grad_hat = grad_normed * gain_vec
    mean_grad = jnp.mean(grad_hat, -1, keepdims=True)
    mean_cross = jnp.mean(grad_hat * normed, -1, keepdims=True)
    return inv_std * (grad_hat - mean_grad - normed * mean_cross)


def dot32(a, b):
    return jnp.dot(a, b, preferred_element_type=F32)


def head_masks(rows):
    lane = lax.broadcasted_iota(jnp.int32, (rows, LANES), 1)
    return [(lane // HEAD_DIM) == h for h in range(LANES // HEAD_DIM)]


def exp_rows(scores):
    row_max = jnp.max(scores, -1, keepdims=True)
    return jnp.exp(scores - row_max)


def attend_kernel(seg_col, seg_row, q_ref, k_ref, v_ref, o_ref, *, length, scaling):
    masks = head_masks(BLOCK)
    for i in range(length // BLOCK):
        lo, hi = i * BLOCK, min(length, (i + 2) * BLOCK)
        rows = pl.ds(lo, BLOCK)
        visible = seg_row[:, lo:hi] <= seg_col[rows, :]
        q = q_ref[rows, :]
        outs = []
        for mask in masks:
            qm = jnp.where(mask, q * scaling, 0).astype(BF16)
            near = lax.dot_general(qm, k_ref[lo:hi, :], NT, preferred_element_type=F32)
            near = jnp.where(visible, near, MASKED_SCORE)
            top = jnp.max(near, -1, keepdims=True)
            if i:
                far = lax.dot_general(qm, k_ref[0:lo, :], NT, preferred_element_type=F32)
                top = jnp.maximum(top, jnp.max(far, -1, keepdims=True))
            near = jnp.exp(near - top)
            total = jnp.sum(near, -1, keepdims=True)
            if i:
                far = jnp.exp(far - top)
                total = total + jnp.sum(far, -1, keepdims=True)
            inv = 1.0 / total
            out = dot32((near * inv).astype(BF16), v_ref[lo:hi, :])
            if i:
                out = out + dot32((far * inv).astype(BF16), v_ref[0:lo, :])
            outs.append(out)
        acc = outs[0]
        for mask, out in zip(masks[1:], outs[1:]):
            acc = jnp.where(mask, out, acc)
        o_ref[rows, :] = acc.astype(BF16)


def attend(qkv, seg_col, seg_row, scaling):
    length, width = qkv.shape[0], qkv.shape[1] // 3
    pairs = width // LANES

    def part(c):
        return pl.BlockSpec((length, LANES), lambda j, c=c: (0, c * pairs + j))

    return pl.pallas_call(
        functools.partial(attend_kernel, length=length, scaling=scaling),
        grid=(pairs,),
        out_shape=jax.ShapeDtypeStruct((length, width), BF16),
        in_specs=[
            pl.BlockSpec((length, 1), lambda j: (0, 0)),
            pl.BlockSpec((1, length), lambda j: (0, 0)),
            part(0),
            part(1),
            part(2),
        ],
        out_specs=pl.BlockSpec((length, LANES), lambda j: (0, j)),
        compiler_params=pltpu.CompilerParams(vmem_limit_bytes=VMEM_LIMIT),
        cost_estimate=busy(11),
        name="attend",
    )(seg_col, seg_row, qkv, qkv, qkv)


def attend_back_kernel(
    seg_col, seg_row, q_ref, k_ref, v_ref, g_ref, o_ref, dk_ref, dv_ref, *, length, scaling, width
):
    pair = pl.program_id(0)
    masks = head_masks(BLOCK)
    key_t = jnp.transpose(k_ref[...])
    dk_ref[...] = jnp.zeros_like(dk_ref)
    dv_ref[...] = jnp.zeros_like(dv_ref)
    half = lax.broadcasted_iota(jnp.int32, (LANES, BLOCK), 0) // HEAD_DIM
    for i in range(length // BLOCK):
        lo, hi = i * BLOCK, min(length, (i + 2) * BLOCK)
        rows = pl.ds(lo, BLOCK)
        visible = seg_col[lo:hi, :] <= seg_row[:, rows]
        q, g = q_ref[rows, :], g_ref[rows, :]
        dq_t = None
        for h, mask in enumerate(masks):
            qm = jnp.where(mask, q * scaling, 0).astype(BF16)
            gm = jnp.where(mask, g, 0).astype(BF16)
            near = lax.dot_general(k_ref[lo:hi, :], qm, NT, preferred_element_type=F32)
            near = jnp.where(visible, near, MASKED_SCORE)
            top = jnp.max(near, 0, keepdims=True)
            if i:
                far = lax.dot_general(k_ref[0:lo, :], qm, NT, preferred_element_type=F32)
                top = jnp.maximum(top, jnp.max(far, 0, keepdims=True))
            near = jnp.exp(near - top)
            total = jnp.sum(near, 0, keepdims=True)
            if i:
                far = jnp.exp(far - top)
                total = total + jnp.sum(far, 0, keepdims=True)
            inv = 1.0 / total
            near = near * inv
            near_g = lax.dot_general(v_ref[lo:hi, :], gm, NT, preferred_element_type=F32)
            inner = jnp.sum(near * near_g, 0, keepdims=True)
            if i:
                far = far * inv
                far_g = lax.dot_general(v_ref[0:lo, :], gm, NT, preferred_element_type=F32)
                inner = inner + jnp.sum(far * far_g, 0, keepdims=True)
            near_s = (near * (near_g - inner)).astype(BF16)
            dv_ref[lo:hi, :] += dot32(near.astype(BF16), gm)
            dk_ref[lo:hi, :] += dot32(near_s, qm)
            dq = dot32(key_t[:, lo:hi], near_s)
            if i:
                far_s = (far * (far_g - inner)).astype(BF16)
                dv_ref[0:lo, :] += dot32(far.astype(BF16), gm)
                dk_ref[0:lo, :] += dot32(far_s, qm)
                dq = dq + dot32(key_t[:, 0:lo], far_s)
            dq_t = dq if dq_t is None else jnp.where(half == h, dq, dq_t)
        lanes = pl.ds(pl.multiple_of(pair * LANES, LANES), LANES)
        o_ref[rows, lanes] = (jnp.transpose(dq_t) * scaling).astype(BF16)
    for c, ref in ((1, dk_ref), (2, dv_ref)):
        lanes = pl.ds(pl.multiple_of(c * width + pair * LANES, LANES), LANES)
        o_ref[:, lanes] = ref[...].astype(BF16)


def attend_back(qkv, seg_col, seg_row, grad_mixed, scaling):
    length, width = qkv.shape[0], qkv.shape[1] // 3
    pairs = width // LANES

    def part(c):
        return pl.BlockSpec((length, LANES), lambda j, c=c: (0, c * pairs + j))

    return pl.pallas_call(
        functools.partial(attend_back_kernel, length=length, scaling=scaling, width=width),
        grid=(pairs,),
        out_shape=jax.ShapeDtypeStruct((length, 3 * width), BF16),
        in_specs=[
            pl.BlockSpec((length, 1), lambda j: (0, 0)),
            pl.BlockSpec((1, length), lambda j: (0, 0)),
            part(0),
            part(1),
            part(2),
            pl.BlockSpec((length, LANES), lambda j: (0, j)),
        ],
        out_specs=pl.BlockSpec((length, 3 * width), lambda j: (0, 0)),
        scratch_shapes=[pltpu.VMEM((length, LANES), F32)] * 2,
        compiler_params=pltpu.CompilerParams(vmem_limit_bytes=VMEM_LIMIT),
        cost_estimate=busy(18),
        name="attend_back",
    )(seg_col, seg_row, qkv, qkv, qkv, grad_mixed)


def residual_kernel(m_ref, w_ref, t_ref, g_ref, b_ref, s_ref, n_ref, *, groups):
    acc = t_ref[...].astype(F32)
    depth = m_ref.shape[2]
    for t in range(groups):
        acc = acc + dot32(m_ref[t], w_ref[t * depth : (t + 1) * depth, :])
    s_ref[...] = acc
    hat, unused = norm_parts(acc)
    n_ref[...] = (hat * g_ref[...] + b_ref[...]).astype(BF16)


def residual_norm(mixed_all, weight, tokens_all, gain, bias):
    groups, length, depth = mixed_all.shape
    width = weight.shape[1]
    rows = BLOCK
    return pl.pallas_call(
        functools.partial(residual_kernel, groups=groups),
        grid=(length // rows,),
        out_shape=(
            jax.ShapeDtypeStruct((length, width), F32),
            jax.ShapeDtypeStruct((length, width), BF16),
        ),
        in_specs=[
            pl.BlockSpec((groups, rows, depth), lambda i: (0, i, 0)),
            pl.BlockSpec((groups * depth, width), lambda i: (0, 0)),
            pl.BlockSpec((rows, width), lambda i: (i, 0)),
            pl.BlockSpec((1, width), lambda i: (0, 0)),
            pl.BlockSpec((1, width), lambda i: (0, 0)),
        ],
        out_specs=(
            pl.BlockSpec((rows, width), lambda i: (i, 0)),
            pl.BlockSpec((rows, width), lambda i: (i, 0)),
        ),
        compiler_params=pltpu.CompilerParams(vmem_limit_bytes=VMEM_LIMIT),
        cost_estimate=busy(7.5),
        name="residual_norm",
    )(mixed_all, weight, tokens_all, gain[None], bias[None])


def spread_kernel(d_ref, x_ref, o_ref):
    rows = o_ref.shape[0]
    slot = lax.broadcasted_iota(jnp.int32, (rows, d_ref.shape[1]), 0) + pl.program_id(0) * rows
    pick = jnp.where(slot == d_ref[...], 1.0, 0.0).astype(BF16)
    o_ref[...] = dot32(pick, x_ref[...]).astype(BF16)


def spread(dest_row, rows_in, slots):
    length, width = rows_in.shape
    block = 2 * BLOCK
    return pl.pallas_call(
        spread_kernel,
        grid=(slots // block,),
        out_shape=jax.ShapeDtypeStruct((slots, width), BF16),
        in_specs=[
            pl.BlockSpec((1, length), lambda i: (0, 0)),
            pl.BlockSpec((length, width), lambda i: (0, 0)),
        ],
        out_specs=pl.BlockSpec((block, width), lambda i: (i, 0)),
        compiler_params=pltpu.CompilerParams(vmem_limit_bytes=VMEM_LIMIT),
        cost_estimate=busy(6.4),
        name="spread",
    )(dest_row, rows_in)


def pick_kernel(d_ref, x_ref, o_ref):
    rows, slots = o_ref.shape[0], x_ref.shape[0]
    slot = lax.broadcasted_iota(jnp.int32, (rows, slots), 1)
    pick = jnp.where(slot == d_ref[...], 1.0, 0.0).astype(BF16)
    o_ref[...] = dot32(pick, x_ref[...]).astype(BF16)


def pick_rows(dest_col, rows_in, length):
    slots, width = rows_in.shape
    return pl.pallas_call(
        pick_kernel,
        grid=(length // BLOCK,),
        out_shape=jax.ShapeDtypeStruct((length, width), BF16),
        in_specs=[
            pl.BlockSpec((BLOCK, 1), lambda i: (i, 0)),
            pl.BlockSpec((slots, width), lambda i: (0, 0)),
        ],
        out_specs=pl.BlockSpec((BLOCK, width), lambda i: (i, 0)),
        compiler_params=pltpu.CompilerParams(vmem_limit_bytes=VMEM_LIMIT),
        cost_estimate=busy(7),
        name="pick_rows",
    )(dest_col, rows_in)


ROOT = 0.7978845608028654
CUBE = 0.044715


def expert_kernel(x_ref, u_ref, w_ref, o_ref, h_ref, s_ref, *, chunk):
    x = x_ref[...].reshape(-1, x_ref.shape[-1])
    rows, ffn = x.shape[0], u_ref.shape[2]
    acc = None
    for c in range(ffn // chunk):
        part = slice(c * chunk, (c + 1) * chunk)
        up = dot32(x, u_ref[0, :, part])
        square = up * up
        tanh = jnp.tanh(ROOT * (up + CUBE * (square * up)))
        half = 0.5 * (1.0 + tanh)
        hidden = (up * half).astype(BF16)
        slope = half + (0.5 * ROOT) * up * (1.0 - tanh * tanh) * (1.0 + (3.0 * CUBE) * square)
        h_ref[0, :, part] = hidden
        s_ref[0, :, part] = slope.astype(BF16)
        out = dot32(hidden, w_ref[0, part, :])
        acc = out if acc is None else acc + out
    o_ref[...] = acc.astype(BF16).reshape(o_ref.shape)


def expert_forward(received, w_up, w_down):
    sources, experts, capacity, width = received.shape
    rows, ffn = sources * capacity, w_up.shape[2]
    tile = pl.BlockSpec((sources, 1, capacity, width), lambda e: (0, e, 0, 0))
    flat = pl.BlockSpec((1, rows, ffn), lambda e: (e, 0, 0))
    return pl.pallas_call(
        functools.partial(expert_kernel, chunk=256),
        grid=(experts,),
        out_shape=(
            jax.ShapeDtypeStruct(received.shape, BF16),
            jax.ShapeDtypeStruct((experts, rows, ffn), BF16),
            jax.ShapeDtypeStruct((experts, rows, ffn), BF16),
        ),
        in_specs=[
            tile,
            pl.BlockSpec((1, width, ffn), lambda e: (e, 0, 0)),
            pl.BlockSpec((1, ffn, width), lambda e: (e, 0, 0)),
        ],
        out_specs=(tile, flat, flat),
        compiler_params=pltpu.CompilerParams(vmem_limit_bytes=VMEM_LIMIT),
        cost_estimate=busy(16),
        name="expert_forward",
    )(received, w_up, w_down)


def expert_back_kernel(x_ref, c_ref, r_ref, u_ref, w_ref, s_ref, o_ref, g_ref, e_ref, *, chunk, experts):
    first = lax.axis_index("dp") * experts + pl.program_id(0)
    x = x_ref[...].reshape(-1, x_ref.shape[-1])
    logits = dot32(x, r_ref[...])
    weights = exp_rows(logits)
    lane = lax.broadcasted_iota(jnp.int32, logits.shape, 1)
    chosen = jnp.sum(jnp.where(lane == first, weights, 0.0), -1, keepdims=True)
    gate = chosen / jnp.sum(weights, -1, keepdims=True)
    grad = (c_ref[...].reshape(x.shape).astype(F32) * gate).astype(BF16)
    e_ref[0] = grad
    acc = None
    for c in range(u_ref.shape[2] // chunk):
        part = slice(c * chunk, (c + 1) * chunk)
        hidden = lax.dot_general(grad, w_ref[0, part, :], NT, preferred_element_type=F32)
        upact = (hidden * s_ref[0, :, part].astype(F32)).astype(BF16)
        g_ref[0, :, part] = upact
        out = lax.dot_general(upact, u_ref[0, :, part], NT, preferred_element_type=F32)
        acc = out if acc is None else acc + out
    o_ref[...] = acc.astype(BF16).reshape(o_ref.shape)


def expert_backward(received, cot_received, router, w_up, w_down, slope):
    sources, experts, capacity, width = received.shape
    rows, ffn = sources * capacity, w_up.shape[2]
    tile = pl.BlockSpec((sources, 1, capacity, width), lambda e: (0, e, 0, 0))
    flat = pl.BlockSpec((1, rows, ffn), lambda e: (e, 0, 0))
    return pl.pallas_call(
        functools.partial(expert_back_kernel, chunk=256, experts=experts),
        grid=(experts,),
        out_shape=(
            jax.ShapeDtypeStruct(received.shape, BF16),
            jax.ShapeDtypeStruct((experts, rows, ffn), BF16),
            jax.ShapeDtypeStruct((experts, rows, width), BF16),
        ),
        in_specs=[
            tile,
            tile,
            pl.BlockSpec(router.shape, lambda e: (0, 0)),
            pl.BlockSpec((1, width, ffn), lambda e: (e, 0, 0)),
            pl.BlockSpec((1, ffn, width), lambda e: (e, 0, 0)),
            flat,
        ],
        out_specs=(tile, flat, pl.BlockSpec((1, rows, width), lambda e: (e, 0, 0))),
        compiler_params=pltpu.CompilerParams(vmem_limit_bytes=VMEM_LIMIT),
        cost_estimate=busy(17.5),
        name="expert_backward",
    )(received, cot_received, router, w_up, w_down, slope)


def weight_grad_kernel(*refs, count, chunk):
    lefts, rights, o_ref = refs[:count], refs[count : 2 * count], refs[2 * count]
    outs = o_ref.shape[1]

    @pl.loop(0, outs // chunk)
    def _(c):
        part = pl.ds(pl.multiple_of(c * chunk, chunk), chunk)
        acc = None
        for a_ref, b_ref in zip(lefts, rights):
            if len(a_ref.shape) == 4:
                a = a_ref[:, :, :, part].reshape(-1, chunk)
            else:
                a = a_ref[0, :, part]
            out = lax.dot_general(a, b_ref[0], TN, preferred_element_type=F32)
            acc = out if acc is None else acc + out
        o_ref[0, part, :] = acc


def weight_grads(lefts, rights):
    experts, rows, ncols = rights[0].shape
    mrows = lefts[0].shape[-1]

    def spec(a):
        if a.ndim == 4:
            return pl.BlockSpec((a.shape[0], 1, a.shape[2], a.shape[3]), lambda e: (0, e, 0, 0))
        return pl.BlockSpec((1,) + a.shape[1:], lambda e: (e, 0, 0))

    return pl.pallas_call(
        functools.partial(weight_grad_kernel, count=len(lefts), chunk=256),
        grid=(experts,),
        out_shape=jax.ShapeDtypeStruct((experts, mrows, ncols), F32),
        in_specs=[spec(a) for a in lefts] + [spec(b) for b in rights],
        out_specs=pl.BlockSpec((1, mrows, ncols), lambda e: (e, 0, 0)),
        compiler_params=pltpu.CompilerParams(vmem_limit_bytes=VMEM_LIMIT),
        cost_estimate=busy(16.4),
        name="weight_grads",
    )(*lefts, *rights)


def mid_kernel(t_ref, e_ref, h_ref, i_ref, c_ref, g_ref, w_ref, m_ref, s_ref, a_ref, k_ref):
    grad = t_ref[...].astype(F32) + e_ref[...]
    hat = h_ref[...]
    k_ref[0:1, :] = jnp.sum(grad * hat, 0, keepdims=True)
    k_ref[1:2, :] = jnp.sum(grad, 0, keepdims=True)
    stream = c_ref[...].astype(F32) + norm_backward(grad, hat, i_ref[...], g_ref[...])
    s_ref[...] = stream
    attn = stream.astype(BF16)
    a_ref[...] = attn
    width = m_ref.shape[2]
    for k in range(m_ref.shape[0]):
        part = w_ref[k * width : (k + 1) * width, :]
        m_ref[k] = lax.dot_general(attn, part, NT, preferred_element_type=F32).astype(BF16)


def middle_back(grad_two, extra, hat, inv, cot, gain, weight, groups):
    rows, width = grad_two.shape
    return pl.pallas_call(
        mid_kernel,
        out_shape=(
            jax.ShapeDtypeStruct((groups, rows, weight.shape[0] // groups), BF16),
            jax.ShapeDtypeStruct((rows, width), F32),
            jax.ShapeDtypeStruct((rows, width), BF16),
            jax.ShapeDtypeStruct((2, width), F32),
        ),
        compiler_params=pltpu.CompilerParams(vmem_limit_bytes=VMEM_LIMIT),
        cost_estimate=busy(5),
        name="middle_back",
    )(grad_two, extra, hat, inv, cot, gain[None], weight)


class Chain:
    def __init__(self, depth=1):
        self.depth, self.results = depth, []

    def run(self, step, operand, *more):
        more = more + tuple(self.results[: max(0, len(self.results) - self.depth + 1)][-1:])
        if more:
            operand, unused = lax.optimization_barrier((operand, more))
        result = step(operand)
        self.results.append(result)
        return result


def z_gather(rows):
    return lax.all_gather(rows, "tensor", axis=0, tiled=True)


def z_stack(rows):
    return lax.all_gather(rows, "tensor", axis=0, tiled=False)


def z_scatter(rows):
    return lax.psum_scatter(rows, "tensor", scatter_dimension=0, tiled=True)


def exchange(blocks, axis):
    return lax.all_to_all(blocks, axis, split_axis=0, concat_axis=0, tiled=True)


def dp_exchange(blocks):
    return exchange(blocks, "dp")


def gather_by_exchange(piece, axis):
    return exchange(jnp.broadcast_to(piece[None], (lax.axis_size(axis),) + piece.shape), axis)


def mesh_copy(src, dst, send, recv, axis, peer):
    return pltpu.make_async_remote_copy(
        src_ref=src,
        dst_ref=dst,
        send_sem=send,
        recv_sem=recv,
        device_id={axis: peer},
        device_id_type=pl.DeviceIdType.MESH,
    )


def greet(peers):
    barrier = pltpu.get_barrier_semaphore()
    for axis, peer in peers:
        pl.semaphore_signal(
            barrier, inc=1, device_id={axis: peer}, device_id_type=pl.DeviceIdType.MESH
        )
    pl.semaphore_wait(barrier, len(peers))


def other_peers(axis, count):
    me = lax.axis_index(axis)
    return [lax.rem(me + k, count) for k in range(1, count)]


def z_swap_kernel(x_ref, o_ref, send, recv, *, count):
    me = lax.axis_index("tensor")
    peers = other_peers("tensor", count)
    greet([("tensor", p) for p in peers])
    copies = [
        mesh_copy(x_ref.at[p], o_ref.at[me], send.at[k], recv.at[k], "tensor", p)
        for k, p in enumerate(peers)
    ]
    for copy in copies:
        copy.start()
    o_ref[me] = x_ref[me]
    for copy in copies:
        copy.wait()


def z_swap(blocks, number=1, micros=14):
    count = blocks.shape[0]
    whole = pl.BlockSpec(memory_space=pltpu.VMEM)
    return pl.pallas_call(
        functools.partial(z_swap_kernel, count=count),
        out_shape=jax.ShapeDtypeStruct(blocks.shape, blocks.dtype),
        in_specs=[whole],
        out_specs=whole,
        scratch_shapes=[pltpu.SemaphoreType.DMA((count - 1,))] * 2,
        compiler_params=pltpu.CompilerParams(collective_id=number, has_side_effects=True),
        cost_estimate=busy(micros),
        name="z_swap",
    )(blocks)


def out_swap(blocks):
    return z_swap(blocks, 4, 3)


def tree_sum(ref, count):
    total = ref[0]
    for k in range(1, count):
        total = total + ref[k]
    return total


def table_sum_kernel(x_ref, o_ref, zin, mid, din, zs, zr, ds, dr, es, er, fs, fr, *, zn, dn):
    z, d = lax.axis_index("tensor"), lax.axis_index("dp")
    zp, dp = other_peers("tensor", zn), other_peers("dp", dn)
    greet([("tensor", p) for p in zp] + [("dp", p) for p in dp])

    def run(copies):
        for copy in copies:
            copy.start()
        return copies

    def settle(copies):
        for copy in copies:
            copy.wait()

    first = run(
        [mesh_copy(x_ref.at[p], zin.at[z], zs.at[k], zr.at[k], "tensor", p) for k, p in enumerate(zp)]
    )
    zin[z] = x_ref[z]
    settle(first)
    mid[...] = tree_sum(zin, zn)
    second = run(
        [mesh_copy(mid.at[p], din.at[d], ds.at[k], dr.at[k], "dp", p) for k, p in enumerate(dp)]
    )
    din[d] = mid[d]
    settle(second)
    o_ref[z, d] = tree_sum(din, dn)
    third = run(
        [
            mesh_copy(o_ref.at[z, d], o_ref.at[z, d], es.at[k], er.at[k], "dp", p)
            for k, p in enumerate(dp)
        ]
    )
    settle(third)
    fourth = run(
        [mesh_copy(o_ref.at[z], o_ref.at[z], fs.at[k], fr.at[k], "tensor", p) for k, p in enumerate(zp)]
    )
    settle(fourth)


def table_sum(values):
    zn, dn = lax.axis_size("tensor"), lax.axis_size("dp")
    rows, width = values.shape
    depth = -(-values.size // (zn * dn * LANES))
    flat = jnp.pad(values.reshape(-1), (0, zn * dn * depth * LANES - values.size))
    shape = (zn, dn, depth, LANES)
    whole = pl.BlockSpec(memory_space=pltpu.VMEM)
    sems = [pltpu.SemaphoreType.DMA((n - 1,)) for n in (zn, zn, dn, dn, dn, dn, zn, zn)]
    return pl.pallas_call(
        functools.partial(table_sum_kernel, zn=zn, dn=dn),
        out_shape=jax.ShapeDtypeStruct(shape, F32),
        in_specs=[whole],
        out_specs=whole,
        scratch_shapes=[
            pltpu.VMEM(shape, F32),
            pltpu.VMEM(shape[1:], F32),
            pltpu.VMEM(shape[1:], F32),
        ]
        + sems,
        compiler_params=pltpu.CompilerParams(collective_id=2, has_side_effects=True),
        cost_estimate=busy(15),
        name="table_sum",
    )(flat.reshape(shape)).reshape(-1)[: values.size].reshape(rows, width)


def shards(
    tokens,
    block_ids,
    routes,
    cotangent,
    ln1_gain,
    ln1_bias,
    w_qkv,
    w_out,
    ln2_gain,
    ln2_bias,
    router,
    w_up,
    w_down,
):
    micro_count, unused, rows_dev, model_width = tokens.shape
    length = routes.shape[2]
    local_experts = w_up.shape[0]
    experts_all = router.shape[1]
    dp_count = lax.axis_size("dp")
    tensor_count = lax.axis_size("tensor")
    capacity = -(-(3 * length // (2 * experts_all)) // 16) * 16
    slots = experts_all * capacity
    scaling = HEAD_DIM ** (-0.5)
    local_width = w_qkv.shape[2]
    first_row = lax.axis_index("tensor") * rows_dev
    expert_range = jnp.arange(experts_all, dtype=jnp.int32)
    micros = range(micro_count)

    def own(rows):
        return lax.dynamic_slice_in_dim(rows, first_row, rows_dev)

    zc, tc, xc = Chain(), Chain(), Chain()
    qkv_flat = xc.run(lambda v: gather_by_exchange(v, "dp"), w_qkv.reshape(-1, 3 * local_width))
    qkv_flat = qkv_flat.reshape(model_width, 3 * local_width)
    out_parts = xc.run(lambda v: gather_by_exchange(v, "tensor"), w_out)
    out_parts = xc.run(lambda v: gather_by_exchange(v, "dp"), out_parts)
    out_matrix = out_parts.transpose(1, 2, 0, 3).reshape(model_width, model_width)

    dest_rows, dest_cols, seg_rows, seg_cols = [], [], [], []
    before = (
        jnp.arange(length, dtype=jnp.int32)[:, None] > jnp.arange(length, dtype=jnp.int32)[None, :]
    ).astype(BF16)
    for m in micros:
        ids = routes[m, 0]
        onehot = (ids == expert_range[None, :]).astype(BF16)
        place = jnp.sum(dot32(before, onehot) * onehot.astype(F32), 1).astype(jnp.int32)
        dest = ids[:, 0] * capacity + place
        dest_rows.append(dest[None, :])
        dest_cols.append(dest[:, None])
        seg_rows.append(block_ids[m])
        seg_cols.append(block_ids[m, 0][:, None])

    def to_blocks(rows):
        return rows.reshape(dp_count, local_experts, capacity, model_width)

    tokens_all, cot_all, whole_one, qkv, mixed = {}, {}, {}, {}, {}
    mixed_all, stream_all, whole_two = {}, {}, {}
    cot_received, received, hidden, slope, upact, grad_expert = {}, {}, {}, {}, {}, {}
    returned, grad_back, expert_out, grad_two = {}, {}, {}, {}
    partial, grad_in = {}, {}
    grad_stream, grad_mixed, grad_one, final_rows, grad_rows = {}, {}, {}, {}, {}
    routers, gain_two, outs_acc, qkv_acc, gain_acc = {}, {}, {}, {}, {}

    def attention(m, *after):
        def step(rows):
            whole = (norm_parts(rows.astype(F32))[0] * ln1_gain + ln1_bias).astype(BF16)
            act = dot32(whole, qkv_flat).astype(BF16)
            return attend(act, seg_cols[m], seg_rows[m], scaling), whole, act

        mixed[m], whole_one[m], qkv[m] = tc.run(step, tokens_all[m], *after)

    def send_cotangent(m):
        blocks = tc.run(lambda v: to_blocks(spread(dest_rows[m], v, slots)), cot_all[m])
        cot_received[m] = xc.run(dp_exchange, blocks)

    def send_tokens(m):
        def step(v):
            stream, whole = residual_norm(v, out_matrix, tokens_all[m], ln2_gain, ln2_bias)
            return to_blocks(spread(dest_rows[m], whole, slots)), stream, whole

        blocks, stream_all[m], whole_two[m] = tc.run(step, mixed_all[m])
        received[m] = xc.run(dp_exchange, blocks)

    def experts_forward(m):
        partial[m], hidden[m], slope[m] = tc.run(
            lambda v: expert_forward(v, w_up, w_down), received[m]
        )

    def experts_backward(m):
        grad_in[m], upact[m], grad_expert[m] = tc.run(
            lambda v: expert_backward(v[0], v[1], router, w_up, w_down, v[2]),
            (received[m], cot_received[m], slope[m]),
        )

    def send_back(m, source, target):
        target[m] = xc.run(dp_exchange, source[m]).reshape(slots, model_width)

    def combine(m, source):
        return tc.run(lambda v: pick_rows(dest_cols[m], v, length), source[m])

    extra, hats, invs = {}, {}, {}

    def gates(m):
        def step(v):
            eo, stream, whole = v
            stream_one = own(stream)
            hat_two, inv_two = norm_parts(stream_one)
            normed_two = own(whole)
            logits = dot32(normed_two, router)
            weights = exp_rows(logits)
            probs = weights / jnp.sum(weights, -1, keepdims=True)
            pick_table = (own(routes[m, 0]) == expert_range[None, :]).astype(F32)
            gate = jnp.sum(probs * pick_table, -1, keepdims=True)
            eo = eo.astype(F32)
            final = (stream_one + gate * eo).astype(BF16)
            grad_gate = jnp.sum(cotangent[m, 0].astype(F32) * eo, -1, keepdims=True)
            grad_logits = (gate * grad_gate * (pick_table - probs)).astype(BF16)
            more = lax.dot_general(grad_logits, router, NT, preferred_element_type=F32)
            grad_router = lax.dot_general(grad_logits, normed_two, TN, preferred_element_type=F32)
            return more, final, grad_router, hat_two, inv_two

        extra[m], final_rows[m], routers[m], hats[m], invs[m] = tc.run(
            step, (expert_out[m], stream_all[m], whole_two[m])
        )

    def middle(m):
        def step(v):
            return middle_back(
                v, extra[m], hats[m], invs[m], cotangent[m, 0], ln2_gain, out_matrix, tensor_count
            )

        gm, grad_stream[m], grad_attn, gain_two[m] = tc.run(step, grad_two[m])
        grad_mixed[m] = tc.run(z_swap, gm).reshape(length, local_width)

        def sums(v):
            mixed_own = lax.dynamic_slice_in_dim(v[0], first_row, rows_dev, axis=1)
            return jnp.einsum("trf,rd->tfd", mixed_own, v[1], preferred_element_type=F32)

        outs_acc[m] = tc.run(sums, (mixed_all[m], grad_attn))

    def attention_back(m):
        act = tc.run(
            lambda v: attend_back(qkv[m], seg_cols[m], seg_rows[m], v, scaling), grad_mixed[m]
        )

        def push(*after):
            return tc.run(
                lambda v: lax.dot_general(v, qkv_flat, NT, preferred_element_type=F32).astype(BF16),
                act,
                *after,
            )

        def sums(v):
            rows, cols, tok = v
            rows = rows.astype(F32)
            hat_one = norm_parts(tok.astype(F32))[0]
            gains = jnp.stack([jnp.sum(rows * hat_one, 0), jnp.sum(rows, 0)])
            return gains, lax.dot_general(whole_one[m], cols, TN, preferred_element_type=F32)

        return push, lambda part: tc.run(sums, (part, act, tokens_all[m]))

    def finish(m):
        grad = grad_one[m].astype(F32)
        hat_one, inv_one = norm_parts(tokens[m, 0].astype(F32))
        grad_rows[m] = grad_stream[m] + norm_backward(grad, hat_one, inv_one, ln1_gain)

    tokens_all[0] = zc.run(z_gather, tokens[0, 0])
    attention(0)
    mixed_all[0] = zc.run(z_stack, mixed[0])
    cot_all[0] = zc.run(z_gather, cotangent[0, 0])
    tokens_all[1] = zc.run(z_gather, tokens[1, 0])
    send_tokens(0)
    send_cotangent(0)
    experts_forward(0)
    send_back(0, partial, returned)
    attention(1, cot_received[0])
    mixed_all[1] = zc.run(z_stack, mixed[1])
    cot_all[1] = zc.run(z_gather, cotangent[1, 0])
    experts_backward(0)
    send_back(0, grad_in, grad_back)
    picked = combine(0, returned)
    send_tokens(1)
    picked_grad = combine(0, grad_back)
    send_cotangent(1)
    expert_out[0] = zc.run(z_scatter, picked)
    experts_forward(1)
    send_back(1, partial, returned)
    grad_two[0] = zc.run(z_scatter, picked_grad)
    experts_backward(1)
    send_back(1, grad_in, grad_back)
    acc_up = tc.run(
        lambda v: weight_grads([v[0], v[1]], [v[2], v[3]]),
        (received[0], received[1], upact[0], upact[1]),
    )
    gates(0)
    expert_out[1] = zc.run(z_scatter, combine(1, returned))
    middle(0)
    grad_two[1] = zc.run(z_scatter, combine(1, grad_back))
    push, sums = attention_back(0)
    part = push()
    grad_one[0] = zc.run(z_scatter, part)
    gates(1)
    gain_acc[0], qkv_acc[0] = sums(part)
    acc_down = tc.run(
        lambda v: weight_grads([v[0], v[1]], [v[2], v[3]]),
        (hidden[0], hidden[1], grad_expert[0], grad_expert[1]),
    )
    middle(1)
    acc_out = (outs_acc[0] + outs_acc[1]).astype(BF16)
    acc_out = acc_out.reshape(model_width, dp_count, -1).transpose(1, 0, 2)
    acc_out = xc.run(dp_exchange, acc_out)
    push, sums = attention_back(1)
    part = push()
    grad_one[1] = zc.run(z_scatter, part)
    gain_acc[1], qkv_acc[1] = sums(part)
    acc_qkv = (qkv_acc[0] + qkv_acc[1]).astype(BF16)
    gains = jnp.concatenate([gain_two[0] + gain_two[1], gain_acc[0] + gain_acc[1]])
    table = jnp.concatenate([routers[0] + routers[1], gains])
    table = tc.run(table_sum, table)
    acc_qkv = xc.run(dp_exchange, acc_qkv.reshape(dp_count, -1, 3 * local_width), table)
    acc_out = tc.run(
        lambda v: jnp.sum(v.astype(F32), 0).astype(BF16).reshape((tensor_count,) + w_out.shape),
        acc_out,
    )
    grad_out_shard = jnp.sum(tc.run(out_swap, acc_out).astype(F32), 0)
    finish(0)
    router_sum, gain_sum = table[:experts_all], table[experts_all:]
    grad_qkv_shard = jnp.sum(acc_qkv.astype(F32), 0).reshape(w_qkv.shape)
    finish(1)
    return (
        jnp.stack([final_rows[m] for m in micros])[:, None],
        jnp.stack([grad_rows[m] for m in micros])[:, None],
        gain_sum[2],
        gain_sum[3],
        grad_qkv_shard,
        grad_out_shard,
        gain_sum[0],
        gain_sum[1],
        router_sum.T,
        acc_up,
        acc_down,
    )


def solution(mesh):
    return jax.shard_map(
        shards,
        mesh=mesh,
        in_specs=(
            P(None, "dp", "tensor", None),
            P(None, "dp", None),
            P(None, "dp", None, None),
            P(None, "dp", "tensor", None),
            P(),
            P(),
            P("dp", None, "tensor"),
            P("tensor", "dp"),
            P(),
            P(),
            P(),
            P("dp", None, "tensor"),
            P("dp", "tensor", None),
        ),
        out_specs=(
            P(None, "dp", "tensor", None),
            P(None, "dp", "tensor", None),
            P(),
            P(),
            P("dp", None, "tensor"),
            P("tensor", "dp"),
            P(),
            P(),
            P(),
            P("dp", None, "tensor"),
            P("dp", "tensor", None),
        ),
        check_vma=False,
    )
```

```python
import functools

import jax
import jax.numpy as jnp
from jax import lax
from jax.experimental import pallas as pl
from jax.experimental.pallas import tpu as pltpu
from jax.sharding import PartitionSpec as P

HEAD_DIM = 64
LANES = 128
BLOCK = 256
EPSILON = 1e-05
MASKED_SCORE = -1e30
F32 = jnp.float32
BF16 = jnp.bfloat16
NT = (((1,), (1,)), ((), ()))
TN = (((0,), (0,)), ((), ()))
BUSY = 1.15e9
VMEM_LIMIT = 60 * 1024 * 1024


def busy(micros):
    return pl.CostEstimate(flops=int(micros * BUSY), bytes_accessed=1024, transcendentals=0)


def norm_parts(stream):
    centre = stream - jnp.mean(stream, -1, keepdims=True)
    inv_std = lax.rsqrt(jnp.mean(centre * centre, -1, keepdims=True) + EPSILON)
    return centre * inv_std, inv_std


def norm_backward(grad_normed, normed, inv_std, gain_vec):
    grad_hat = grad_normed * gain_vec
    mean_grad = jnp.mean(grad_hat, -1, keepdims=True)
    mean_cross = jnp.mean(grad_hat * normed, -1, keepdims=True)
    return inv_std * (grad_hat - mean_grad - normed * mean_cross)


def dot32(a, b):
    return jnp.dot(a, b, preferred_element_type=F32)


def head_masks(rows):
    lane = lax.broadcasted_iota(jnp.int32, (rows, LANES), 1)
    return [(lane // HEAD_DIM) == h for h in range(LANES // HEAD_DIM)]


def exp_rows(scores):
    row_max = jnp.max(scores, -1, keepdims=True)
    return jnp.exp(scores - row_max)


def attend_kernel(seg_col, seg_row, q_ref, k_ref, v_ref, o_ref, *, length, scaling):
    masks = head_masks(BLOCK)
    for i in range(length // BLOCK):
        lo, hi = i * BLOCK, min(length, (i + 2) * BLOCK)
        rows = pl.ds(lo, BLOCK)
        visible = seg_row[:, lo:hi] <= seg_col[rows, :]
        q = q_ref[rows, :]
        outs = []
        for mask in masks:
            qm = jnp.where(mask, q * scaling, 0).astype(BF16)
            near = lax.dot_general(qm, k_ref[lo:hi, :], NT, preferred_element_type=F32)
            near = jnp.where(visible, near, MASKED_SCORE)
            top = jnp.max(near, -1, keepdims=True)
            if i:
                far = lax.dot_general(qm, k_ref[0:lo, :], NT, preferred_element_type=F32)
                top = jnp.maximum(top, jnp.max(far, -1, keepdims=True))
            near = jnp.exp(near - top)
            total = jnp.sum(near, -1, keepdims=True)
            if i:
                far = jnp.exp(far - top)
                total = total + jnp.sum(far, -1, keepdims=True)
            inv = 1.0 / total
            out = dot32((near * inv).astype(BF16), v_ref[lo:hi, :])
            if i:
                out = out + dot32((far * inv).astype(BF16), v_ref[0:lo, :])
            outs.append(out)
        acc = outs[0]
        for mask, out in zip(masks[1:], outs[1:]):
            acc = jnp.where(mask, out, acc)
        o_ref[rows, :] = acc.astype(BF16)


def attend(qkv, seg_col, seg_row, scaling):
    length, width = qkv.shape[0], qkv.shape[1] // 3
    pairs = width // LANES

    def part(c):
        return pl.BlockSpec((length, LANES), lambda j, c=c: (0, c * pairs + j))

    return pl.pallas_call(
        functools.partial(attend_kernel, length=length, scaling=scaling),
        grid=(pairs,),
        out_shape=jax.ShapeDtypeStruct((length, width), BF16),
        in_specs=[
            pl.BlockSpec((length, 1), lambda j: (0, 0)),
            pl.BlockSpec((1, length), lambda j: (0, 0)),
            part(0),
            part(1),
            part(2),
        ],
        out_specs=pl.BlockSpec((length, LANES), lambda j: (0, j)),
        compiler_params=pltpu.CompilerParams(vmem_limit_bytes=VMEM_LIMIT),
        cost_estimate=busy(11),
        name="attend",
    )(seg_col, seg_row, qkv, qkv, qkv)


def attend_back_kernel(
    seg_col, seg_row, q_ref, k_ref, v_ref, g_ref, o_ref, dk_ref, dv_ref, *, length, scaling, width
):
    pair = pl.program_id(0)
    masks = head_masks(BLOCK)
    key_t = jnp.transpose(k_ref[...])
    dk_ref[...] = jnp.zeros_like(dk_ref)
    dv_ref[...] = jnp.zeros_like(dv_ref)
    half = lax.broadcasted_iota(jnp.int32, (LANES, BLOCK), 0) // HEAD_DIM
    for i in range(length // BLOCK):
        lo, hi = i * BLOCK, min(length, (i + 2) * BLOCK)
        rows = pl.ds(lo, BLOCK)
        visible = seg_col[lo:hi, :] <= seg_row[:, rows]
        q, g = q_ref[rows, :], g_ref[rows, :]
        dq_t = None
        for h, mask in enumerate(masks):
            qm = jnp.where(mask, q * scaling, 0).astype(BF16)
            gm = jnp.where(mask, g, 0).astype(BF16)
            near = lax.dot_general(k_ref[lo:hi, :], qm, NT, preferred_element_type=F32)
            near = jnp.where(visible, near, MASKED_SCORE)
            top = jnp.max(near, 0, keepdims=True)
            if i:
                far = lax.dot_general(k_ref[0:lo, :], qm, NT, preferred_element_type=F32)
                top = jnp.maximum(top, jnp.max(far, 0, keepdims=True))
            near = jnp.exp(near - top)
            total = jnp.sum(near, 0, keepdims=True)
            if i:
                far = jnp.exp(far - top)
                total = total + jnp.sum(far, 0, keepdims=True)
            inv = 1.0 / total
            near = near * inv
            near_g = lax.dot_general(v_ref[lo:hi, :], gm, NT, preferred_element_type=F32)
            inner = jnp.sum(near * near_g, 0, keepdims=True)
            if i:
                far = far * inv
                far_g = lax.dot_general(v_ref[0:lo, :], gm, NT, preferred_element_type=F32)
                inner = inner + jnp.sum(far * far_g, 0, keepdims=True)
            near_s = (near * (near_g - inner)).astype(BF16)
            dv_ref[lo:hi, :] += dot32(near.astype(BF16), gm)
            dk_ref[lo:hi, :] += dot32(near_s, qm)
            dq = dot32(key_t[:, lo:hi], near_s)
            if i:
                far_s = (far * (far_g - inner)).astype(BF16)
                dv_ref[0:lo, :] += dot32(far.astype(BF16), gm)
                dk_ref[0:lo, :] += dot32(far_s, qm)
                dq = dq + dot32(key_t[:, 0:lo], far_s)
            dq_t = dq if dq_t is None else jnp.where(half == h, dq, dq_t)
        lanes = pl.ds(pl.multiple_of(pair * LANES, LANES), LANES)
        o_ref[rows, lanes] = (jnp.transpose(dq_t) * scaling).astype(BF16)
    for c, ref in ((1, dk_ref), (2, dv_ref)):
        lanes = pl.ds(pl.multiple_of(c * width + pair * LANES, LANES), LANES)
        o_ref[:, lanes] = ref[...].astype(BF16)


def attend_back(qkv, seg_col, seg_row, grad_mixed, scaling):
    length, width = qkv.shape[0], qkv.shape[1] // 3
    pairs = width // LANES

    def part(c):
        return pl.BlockSpec((length, LANES), lambda j, c=c: (0, c * pairs + j))

    return pl.pallas_call(
        functools.partial(attend_back_kernel, length=length, scaling=scaling, width=width),
        grid=(pairs,),
        out_shape=jax.ShapeDtypeStruct((length, 3 * width), BF16),
        in_specs=[
            pl.BlockSpec((length, 1), lambda j: (0, 0)),
            pl.BlockSpec((1, length), lambda j: (0, 0)),
            part(0),
            part(1),
            part(2),
            pl.BlockSpec((length, LANES), lambda j: (0, j)),
        ],
        out_specs=pl.BlockSpec((length, 3 * width), lambda j: (0, 0)),
        scratch_shapes=[pltpu.VMEM((length, LANES), F32)] * 2,
        compiler_params=pltpu.CompilerParams(vmem_limit_bytes=VMEM_LIMIT),
        cost_estimate=busy(18),
        name="attend_back",
    )(seg_col, seg_row, qkv, qkv, qkv, grad_mixed)


def residual_kernel(m_ref, w_ref, t_ref, g_ref, b_ref, s_ref, n_ref, *, groups):
    acc = t_ref[...].astype(F32)
    depth = m_ref.shape[2]
    for t in range(groups):
        acc = acc + dot32(m_ref[t], w_ref[t * depth : (t + 1) * depth, :])
    s_ref[...] = acc
    hat, unused = norm_parts(acc)
    n_ref[...] = (hat * g_ref[...] + b_ref[...]).astype(BF16)


def residual_norm(mixed_all, weight, tokens_all, gain, bias):
    groups, length, depth = mixed_all.shape
    width = weight.shape[1]
    rows = BLOCK
    return pl.pallas_call(
        functools.partial(residual_kernel, groups=groups),
        grid=(length // rows,),
        out_shape=(
            jax.ShapeDtypeStruct((length, width), F32),
            jax.ShapeDtypeStruct((length, width), BF16),
        ),
        in_specs=[
            pl.BlockSpec((groups, rows, depth), lambda i: (0, i, 0)),
            pl.BlockSpec((groups * depth, width), lambda i: (0, 0)),
            pl.BlockSpec((rows, width), lambda i: (i, 0)),
            pl.BlockSpec((1, width), lambda i: (0, 0)),
            pl.BlockSpec((1, width), lambda i: (0, 0)),
        ],
        out_specs=(
            pl.BlockSpec((rows, width), lambda i: (i, 0)),
            pl.BlockSpec((rows, width), lambda i: (i, 0)),
        ),
        compiler_params=pltpu.CompilerParams(vmem_limit_bytes=VMEM_LIMIT),
        cost_estimate=busy(7.5),
        name="residual_norm",
    )(mixed_all, weight, tokens_all, gain[None], bias[None])


def spread_kernel(d_ref, x_ref, o_ref):
    rows = o_ref.shape[0]
    slot = lax.broadcasted_iota(jnp.int32, (rows, d_ref.shape[1]), 0) + pl.program_id(0) * rows
    pick = jnp.where(slot == d_ref[...], 1.0, 0.0).astype(BF16)
    o_ref[...] = dot32(pick, x_ref[...]).astype(BF16)


def spread(dest_row, rows_in, slots):
    length, width = rows_in.shape
    block = 2 * BLOCK
    return pl.pallas_call(
        spread_kernel,
        grid=(slots // block,),
        out_shape=jax.ShapeDtypeStruct((slots, width), BF16),
        in_specs=[
            pl.BlockSpec((1, length), lambda i: (0, 0)),
            pl.BlockSpec((length, width), lambda i: (0, 0)),
        ],
        out_specs=pl.BlockSpec((block, width), lambda i: (i, 0)),
        compiler_params=pltpu.CompilerParams(vmem_limit_bytes=VMEM_LIMIT),
        cost_estimate=busy(6.4),
        name="spread",
    )(dest_row, rows_in)


def pick_kernel(d_ref, x_ref, o_ref):
    rows, slots = o_ref.shape[0], x_ref.shape[0]
    slot = lax.broadcasted_iota(jnp.int32, (rows, slots), 1)
    pick = jnp.where(slot == d_ref[...], 1.0, 0.0).astype(BF16)
    o_ref[...] = dot32(pick, x_ref[...]).astype(BF16)


def pick_rows(dest_col, rows_in, length):
    slots, width = rows_in.shape
    return pl.pallas_call(
        pick_kernel,
        grid=(length // BLOCK,),
        out_shape=jax.ShapeDtypeStruct((length, width), BF16),
        in_specs=[
            pl.BlockSpec((BLOCK, 1), lambda i: (i, 0)),
            pl.BlockSpec((slots, width), lambda i: (0, 0)),
        ],
        out_specs=pl.BlockSpec((BLOCK, width), lambda i: (i, 0)),
        compiler_params=pltpu.CompilerParams(vmem_limit_bytes=VMEM_LIMIT),
        cost_estimate=busy(7),
        name="pick_rows",
    )(dest_col, rows_in)


ROOT = 0.7978845608028654
CUBE = 0.044715


def expert_kernel(x_ref, u_ref, w_ref, o_ref, h_ref, s_ref, *, chunk):
    x = x_ref[...].reshape(-1, x_ref.shape[-1])
    rows, ffn = x.shape[0], u_ref.shape[2]
    acc = None
    for c in range(ffn // chunk):
        part = slice(c * chunk, (c + 1) * chunk)
        up = dot32(x, u_ref[0, :, part])
        square = up * up
        tanh = jnp.tanh(ROOT * (up + CUBE * (square * up)))
        half = 0.5 * (1.0 + tanh)
        hidden = (up * half).astype(BF16)
        slope = half + (0.5 * ROOT) * up * (1.0 - tanh * tanh) * (1.0 + (3.0 * CUBE) * square)
        h_ref[0, :, part] = hidden
        s_ref[0, :, part] = slope.astype(BF16)
        out = dot32(hidden, w_ref[0, part, :])
        acc = out if acc is None else acc + out
    o_ref[...] = acc.astype(BF16).reshape(o_ref.shape)


def expert_forward(received, w_up, w_down):
    sources, experts, capacity, width = received.shape
    rows, ffn = sources * capacity, w_up.shape[2]
    tile = pl.BlockSpec((sources, 1, capacity, width), lambda e: (0, e, 0, 0))
    flat = pl.BlockSpec((1, rows, ffn), lambda e: (e, 0, 0))
    return pl.pallas_call(
        functools.partial(expert_kernel, chunk=256),
        grid=(experts,),
        out_shape=(
            jax.ShapeDtypeStruct(received.shape, BF16),
            jax.ShapeDtypeStruct((experts, rows, ffn), BF16),
            jax.ShapeDtypeStruct((experts, rows, ffn), BF16),
        ),
        in_specs=[
            tile,
            pl.BlockSpec((1, width, ffn), lambda e: (e, 0, 0)),
            pl.BlockSpec((1, ffn, width), lambda e: (e, 0, 0)),
        ],
        out_specs=(tile, flat, flat),
        compiler_params=pltpu.CompilerParams(vmem_limit_bytes=VMEM_LIMIT),
        cost_estimate=busy(16),
        name="expert_forward",
    )(received, w_up, w_down)


def expert_back_kernel(x_ref, c_ref, r_ref, u_ref, w_ref, s_ref, o_ref, g_ref, e_ref, *, chunk, experts):
    first = lax.axis_index("dp") * experts + pl.program_id(0)
    x = x_ref[...].reshape(-1, x_ref.shape[-1])
    logits = dot32(x, r_ref[...])
    weights = exp_rows(logits)
    lane = lax.broadcasted_iota(jnp.int32, logits.shape, 1)
    chosen = jnp.sum(jnp.where(lane == first, weights, 0.0), -1, keepdims=True)
    gate = chosen / jnp.sum(weights, -1, keepdims=True)
    grad = (c_ref[...].reshape(x.shape).astype(F32) * gate).astype(BF16)
    e_ref[0] = grad
    acc = None
    for c in range(u_ref.shape[2] // chunk):
        part = slice(c * chunk, (c + 1) * chunk)
        hidden = lax.dot_general(grad, w_ref[0, part, :], NT, preferred_element_type=F32)
        upact = (hidden * s_ref[0, :, part].astype(F32)).astype(BF16)
        g_ref[0, :, part] = upact
        out = lax.dot_general(upact, u_ref[0, :, part], NT, preferred_element_type=F32)
        acc = out if acc is None else acc + out
    o_ref[...] = acc.astype(BF16).reshape(o_ref.shape)


def expert_backward(received, cot_received, router, w_up, w_down, slope):
    sources, experts, capacity, width = received.shape
    rows, ffn = sources * capacity, w_up.shape[2]
    tile = pl.BlockSpec((sources, 1, capacity, width), lambda e: (0, e, 0, 0))
    flat = pl.BlockSpec((1, rows, ffn), lambda e: (e, 0, 0))
    return pl.pallas_call(
        functools.partial(expert_back_kernel, chunk=256, experts=experts),
        grid=(experts,),
        out_shape=(
            jax.ShapeDtypeStruct(received.shape, BF16),
            jax.ShapeDtypeStruct((experts, rows, ffn), BF16),
            jax.ShapeDtypeStruct((experts, rows, width), BF16),
        ),
        in_specs=[
            tile,
            tile,
            pl.BlockSpec(router.shape, lambda e: (0, 0)),
            pl.BlockSpec((1, width, ffn), lambda e: (e, 0, 0)),
            pl.BlockSpec((1, ffn, width), lambda e: (e, 0, 0)),
            flat,
        ],
        out_specs=(tile, flat, pl.BlockSpec((1, rows, width), lambda e: (e, 0, 0))),
        compiler_params=pltpu.CompilerParams(vmem_limit_bytes=VMEM_LIMIT),
        cost_estimate=busy(17.5),
        name="expert_backward",
    )(received, cot_received, router, w_up, w_down, slope)


def weight_grad_kernel(*refs, count, chunk):
    lefts, rights, o_ref = refs[:count], refs[count : 2 * count], refs[2 * count]
    outs = o_ref.shape[1]

    @pl.loop(0, outs // chunk)
    def _(c):
        part = pl.ds(pl.multiple_of(c * chunk, chunk), chunk)
        acc = None
        for a_ref, b_ref in zip(lefts, rights):
            if len(a_ref.shape) == 4:
                a = a_ref[:, :, :, part].reshape(-1, chunk)
            else:
                a = a_ref[0, :, part]
            out = lax.dot_general(a, b_ref[0], TN, preferred_element_type=F32)
            acc = out if acc is None else acc + out
        o_ref[0, part, :] = acc


def weight_grads(lefts, rights):
    experts, rows, ncols = rights[0].shape
    mrows = lefts[0].shape[-1]

    def spec(a):
        if a.ndim == 4:
            return pl.BlockSpec((a.shape[0], 1, a.shape[2], a.shape[3]), lambda e: (0, e, 0, 0))
        return pl.BlockSpec((1,) + a.shape[1:], lambda e: (e, 0, 0))

    return pl.pallas_call(
        functools.partial(weight_grad_kernel, count=len(lefts), chunk=256),
        grid=(experts,),
        out_shape=jax.ShapeDtypeStruct((experts, mrows, ncols), F32),
        in_specs=[spec(a) for a in lefts] + [spec(b) for b in rights],
        out_specs=pl.BlockSpec((1, mrows, ncols), lambda e: (e, 0, 0)),
        compiler_params=pltpu.CompilerParams(vmem_limit_bytes=VMEM_LIMIT),
        cost_estimate=busy(16.4),
        name="weight_grads",
    )(*lefts, *rights)


def mid_kernel(t_ref, e_ref, h_ref, i_ref, c_ref, g_ref, w_ref, m_ref, s_ref, a_ref, k_ref):
    grad = t_ref[...].astype(F32) + e_ref[...]
    hat = h_ref[...]
    k_ref[0:1, :] = jnp.sum(grad * hat, 0, keepdims=True)
    k_ref[1:2, :] = jnp.sum(grad, 0, keepdims=True)
    stream = c_ref[...].astype(F32) + norm_backward(grad, hat, i_ref[...], g_ref[...])
    s_ref[...] = stream
    attn = stream.astype(BF16)
    a_ref[...] = attn
    width = m_ref.shape[2]
    for k in range(m_ref.shape[0]):
        part = w_ref[k * width : (k + 1) * width, :]
        m_ref[k] = lax.dot_general(attn, part, NT, preferred_element_type=F32).astype(BF16)


def middle_back(grad_two, extra, hat, inv, cot, gain, weight, groups):
    rows, width = grad_two.shape
    return pl.pallas_call(
        mid_kernel,
        out_shape=(
            jax.ShapeDtypeStruct((groups, rows, weight.shape[0] // groups), BF16),
            jax.ShapeDtypeStruct((rows, width), F32),
            jax.ShapeDtypeStruct((rows, width), BF16),
            jax.ShapeDtypeStruct((2, width), F32),
        ),
        compiler_params=pltpu.CompilerParams(vmem_limit_bytes=VMEM_LIMIT),
        cost_estimate=busy(5),
        name="middle_back",
    )(grad_two, extra, hat, inv, cot, gain[None], weight)


class Chain:
    def __init__(self, depth=1):
        self.depth, self.results = depth, []

    def run(self, step, operand, *more):
        more = more + tuple(self.results[: max(0, len(self.results) - self.depth + 1)][-1:])
        if more:
            operand, unused = lax.optimization_barrier((operand, more))
        result = step(operand)
        self.results.append(result)
        return result


def z_gather(rows):
    return lax.all_gather(rows, "tensor", axis=0, tiled=True)


def z_stack(rows):
    return lax.all_gather(rows, "tensor", axis=0, tiled=False)


def z_scatter(rows):
    return lax.psum_scatter(rows, "tensor", scatter_dimension=0, tiled=True)


def exchange(blocks, axis):
    return lax.all_to_all(blocks, axis, split_axis=0, concat_axis=0, tiled=True)


def dp_exchange(blocks):
    return exchange(blocks, "dp")


def gather_by_exchange(piece, axis):
    return exchange(jnp.broadcast_to(piece[None], (lax.axis_size(axis),) + piece.shape), axis)


def mesh_copy(src, dst, send, recv, axis, peer):
    return pltpu.make_async_remote_copy(
        src_ref=src,
        dst_ref=dst,
        send_sem=send,
        recv_sem=recv,
        device_id={axis: peer},
        device_id_type=pl.DeviceIdType.MESH,
    )


def greet(peers):
    barrier = pltpu.get_barrier_semaphore()
    for axis, peer in peers:
        pl.semaphore_signal(
            barrier, inc=1, device_id={axis: peer}, device_id_type=pl.DeviceIdType.MESH
        )
    pl.semaphore_wait(barrier, len(peers))


def other_peers(axis, count):
    me = lax.axis_index(axis)
    return [lax.rem(me + k, count) for k in range(1, count)]


def z_swap_kernel(x_ref, o_ref, send, recv, *, count):
    me = lax.axis_index("tensor")
    peers = other_peers("tensor", count)
    greet([("tensor", p) for p in peers])
    copies = [
        mesh_copy(x_ref.at[p], o_ref.at[me], send.at[k], recv.at[k], "tensor", p)
        for k, p in enumerate(peers)
    ]
    for copy in copies:
        copy.start()
    o_ref[me] = x_ref[me]
    for copy in copies:
        copy.wait()


def z_swap(blocks, number=1, micros=14):
    count = blocks.shape[0]
    whole = pl.BlockSpec(memory_space=pltpu.VMEM)
    return pl.pallas_call(
        functools.partial(z_swap_kernel, count=count),
        out_shape=jax.ShapeDtypeStruct(blocks.shape, blocks.dtype),
        in_specs=[whole],
        out_specs=whole,
        scratch_shapes=[pltpu.SemaphoreType.DMA((count - 1,))] * 2,
        compiler_params=pltpu.CompilerParams(collective_id=number, has_side_effects=True),
        cost_estimate=busy(micros),
        name="z_swap",
    )(blocks)


def out_swap(blocks):
    return z_swap(blocks, 4, 3)


def tree_sum(ref, count):
    total = ref[0]
    for k in range(1, count):
        total = total + ref[k]
    return total


def table_sum_kernel(x_ref, o_ref, zin, mid, din, zs, zr, ds, dr, es, er, fs, fr, *, zn, dn):
    z, d = lax.axis_index("tensor"), lax.axis_index("dp")
    zp, dp = other_peers("tensor", zn), other_peers("dp", dn)
    greet([("tensor", p) for p in zp] + [("dp", p) for p in dp])

    def run(copies):
        for copy in copies:
            copy.start()
        return copies

    def settle(copies):
        for copy in copies:
            copy.wait()

    first = run(
        [mesh_copy(x_ref.at[p], zin.at[z], zs.at[k], zr.at[k], "tensor", p) for k, p in enumerate(zp)]
    )
    zin[z] = x_ref[z]
    settle(first)
    mid[...] = tree_sum(zin, zn)
    second = run(
        [mesh_copy(mid.at[p], din.at[d], ds.at[k], dr.at[k], "dp", p) for k, p in enumerate(dp)]
    )
    din[d] = mid[d]
    settle(second)
    o_ref[z, d] = tree_sum(din, dn)
    third = run(
        [
            mesh_copy(o_ref.at[z, d], o_ref.at[z, d], es.at[k], er.at[k], "dp", p)
            for k, p in enumerate(dp)
        ]
    )
    settle(third)
    fourth = run(
        [mesh_copy(o_ref.at[z], o_ref.at[z], fs.at[k], fr.at[k], "tensor", p) for k, p in enumerate(zp)]
    )
    settle(fourth)


def table_sum(values):
    zn, dn = lax.axis_size("tensor"), lax.axis_size("dp")
    rows, width = values.shape
    depth = -(-values.size // (zn * dn * LANES))
    flat = jnp.pad(values.reshape(-1), (0, zn * dn * depth * LANES - values.size))
    shape = (zn, dn, depth, LANES)
    whole = pl.BlockSpec(memory_space=pltpu.VMEM)
    sems = [pltpu.SemaphoreType.DMA((n - 1,)) for n in (zn, zn, dn, dn, dn, dn, zn, zn)]
    return pl.pallas_call(
        functools.partial(table_sum_kernel, zn=zn, dn=dn),
        out_shape=jax.ShapeDtypeStruct(shape, F32),
        in_specs=[whole],
        out_specs=whole,
        scratch_shapes=[
            pltpu.VMEM(shape, F32),
            pltpu.VMEM(shape[1:], F32),
            pltpu.VMEM(shape[1:], F32),
        ]
        + sems,
        compiler_params=pltpu.CompilerParams(collective_id=2, has_side_effects=True),
        cost_estimate=busy(15),
        name="table_sum",
    )(flat.reshape(shape)).reshape(-1)[: values.size].reshape(rows, width)


def shards(
    tokens,
    block_ids,
    routes,
    cotangent,
    ln1_gain,
    ln1_bias,
    w_qkv,
    w_out,
    ln2_gain,
    ln2_bias,
    router,
    w_up,
    w_down,
):
    micro_count, unused, rows_dev, model_width = tokens.shape
    length = routes.shape[2]
    local_experts = w_up.shape[0]
    experts_all = router.shape[1]
    dp_count = lax.axis_size("dp")
    tensor_count = lax.axis_size("tensor")
    capacity = -(-(3 * length // (2 * experts_all)) // 16) * 16
    slots = experts_all * capacity
    scaling = HEAD_DIM ** (-0.5)
    local_width = w_qkv.shape[2]
    first_row = lax.axis_index("tensor") * rows_dev
    expert_range = jnp.arange(experts_all, dtype=jnp.int32)
    micros = range(micro_count)

    def own(rows):
        return lax.dynamic_slice_in_dim(rows, first_row, rows_dev)

    zc, tc, xc = Chain(), Chain(), Chain()
    qkv_flat = xc.run(lambda v: gather_by_exchange(v, "dp"), w_qkv.reshape(-1, 3 * local_width))
    qkv_flat = qkv_flat.reshape(model_width, 3 * local_width)
    out_parts = xc.run(lambda v: gather_by_exchange(v, "tensor"), w_out)
    out_parts = xc.run(lambda v: gather_by_exchange(v, "dp"), out_parts)
    out_matrix = out_parts.transpose(1, 2, 0, 3).reshape(model_width, model_width)

    dest_rows, dest_cols, seg_rows, seg_cols = [], [], [], []
    before = (
        jnp.arange(length, dtype=jnp.int32)[:, None] > jnp.arange(length, dtype=jnp.int32)[None, :]
    ).astype(BF16)
    for m in micros:
        ids = routes[m, 0]
        onehot = (ids == expert_range[None, :]).astype(BF16)
        place = jnp.sum(dot32(before, onehot) * onehot.astype(F32), 1).astype(jnp.int32)
        dest = ids[:, 0] * capacity + place
        dest_rows.append(dest[None, :])
        dest_cols.append(dest[:, None])
        seg_rows.append(block_ids[m])
        seg_cols.append(block_ids[m, 0][:, None])

    def to_blocks(rows):
        return rows.reshape(dp_count, local_experts, capacity, model_width)

    tokens_all, cot_all, whole_one, qkv, mixed = {}, {}, {}, {}, {}
    mixed_all, stream_all, whole_two = {}, {}, {}
    cot_received, received, hidden, slope, upact, grad_expert = {}, {}, {}, {}, {}, {}
    returned, grad_back, expert_out, grad_two = {}, {}, {}, {}
    partial, grad_in = {}, {}
    grad_stream, grad_mixed, grad_one, final_rows, grad_rows = {}, {}, {}, {}, {}
    routers, gain_two, outs_acc, qkv_acc, gain_acc = {}, {}, {}, {}, {}

    def attention(m, *after):
        def step(rows):
            whole = (norm_parts(rows.astype(F32))[0] * ln1_gain + ln1_bias).astype(BF16)
            act = dot32(whole, qkv_flat).astype(BF16)
            return attend(act, seg_cols[m], seg_rows[m], scaling), whole, act

        mixed[m], whole_one[m], qkv[m] = tc.run(step, tokens_all[m], *after)

    def spread_rows(m):
        return tc.run(lambda v: to_blocks(spread(dest_rows[m], v, slots)), cot_all[m])

    def send_cotangent(m):
        cot_received[m] = xc.run(dp_exchange, spread_rows(m))

    def send_tokens(m):
        def step(v):
            stream, whole = residual_norm(v, out_matrix, tokens_all[m], ln2_gain, ln2_bias)
            return to_blocks(spread(dest_rows[m], whole, slots)), stream, whole

        blocks, stream_all[m], whole_two[m] = tc.run(step, mixed_all[m])
        received[m] = xc.run(dp_exchange, blocks)

    def experts_forward(m):
        partial[m], hidden[m], slope[m] = tc.run(
            lambda v: expert_forward(v, w_up, w_down), received[m]
        )

    def experts_backward(m):
        grad_in[m], upact[m], grad_expert[m] = tc.run(
            lambda v: expert_backward(v[0], v[1], router, w_up, w_down, v[2]),
            (received[m], cot_received[m], slope[m]),
        )

    def send_back(m, source, target, *after):
        target[m] = xc.run(dp_exchange, source[m], *after).reshape(slots, model_width)

    def combine(m, source):
        return tc.run(lambda v: pick_rows(dest_cols[m], v, length), source[m])

    extra, hats, invs = {}, {}, {}

    def gates(m):
        def step(v):
            eo, stream, whole = v
            stream_one = own(stream)
            hat_two, inv_two = norm_parts(stream_one)
            normed_two = own(whole)
            logits = dot32(normed_two, router)
            weights = exp_rows(logits)
            probs = weights / jnp.sum(weights, -1, keepdims=True)
            pick_table = (own(routes[m, 0]) == expert_range[None, :]).astype(F32)
            gate = jnp.sum(probs * pick_table, -1, keepdims=True)
            eo = eo.astype(F32)
            final = (stream_one + gate * eo).astype(BF16)
            grad_gate = jnp.sum(cotangent[m, 0].astype(F32) * eo, -1, keepdims=True)
            grad_logits = (gate * grad_gate * (pick_table - probs)).astype(BF16)
            more = lax.dot_general(grad_logits, router, NT, preferred_element_type=F32)
            grad_router = lax.dot_general(grad_logits, normed_two, TN, preferred_element_type=F32)
            return more, final, grad_router, hat_two, inv_two

        extra[m], final_rows[m], routers[m], hats[m], invs[m] = tc.run(
            step, (expert_out[m], stream_all[m], whole_two[m])
        )

    def middle(m):
        def step(v):
            return middle_back(
                v, extra[m], hats[m], invs[m], cotangent[m, 0], ln2_gain, out_matrix, tensor_count
            )

        gm, grad_stream[m], grad_attn, gain_two[m] = tc.run(step, grad_two[m])
        grad_mixed[m] = tc.run(z_swap, gm).reshape(length, local_width)

        def sums(v):
            mixed_own = lax.dynamic_slice_in_dim(v[0], first_row, rows_dev, axis=1)
            return jnp.einsum("trf,rd->tfd", mixed_own, v[1], preferred_element_type=F32)

        outs_acc[m] = tc.run(sums, (mixed_all[m], grad_attn))

    def attention_back(m):
        act = tc.run(
            lambda v: attend_back(qkv[m], seg_cols[m], seg_rows[m], v, scaling), grad_mixed[m]
        )

        def push(*after):
            return tc.run(
                lambda v: lax.dot_general(v, qkv_flat, NT, preferred_element_type=F32).astype(BF16),
                act,
                *after,
            )

        def sums(v):
            rows, cols, tok = v
            rows = rows.astype(F32)
            hat_one = norm_parts(tok.astype(F32))[0]
            gains = jnp.stack([jnp.sum(rows * hat_one, 0), jnp.sum(rows, 0)])
            return gains, lax.dot_general(whole_one[m], cols, TN, preferred_element_type=F32)

        return push, lambda part: tc.run(sums, (part, act, tokens_all[m]))

    def finish(m):
        grad = grad_one[m].astype(F32)
        hat_one, inv_one = norm_parts(tokens[m, 0].astype(F32))
        grad_rows[m] = grad_stream[m] + norm_backward(grad, hat_one, inv_one, ln1_gain)

    tokens_all[0] = zc.run(z_gather, tokens[0, 0])
    attention(0)
    mixed_all[0] = zc.run(z_stack, mixed[0])
    cot_all[0] = zc.run(z_gather, cotangent[0, 0])
    tokens_all[1] = zc.run(z_gather, tokens[1, 0])
    send_tokens(0)
    send_cotangent(0)
    experts_forward(0)
    send_back(0, partial, returned)
    cot_all[1] = zc.run(z_gather, cotangent[1, 0])
    attention(1, cot_received[0])
    mixed_all[1] = zc.run(z_stack, mixed[1])
    experts_backward(0)
    send_back(0, grad_in, grad_back)
    picked = combine(0, returned)
    expert_out[0] = zc.run(z_scatter, picked)
    spread_cotangent = spread_rows(1)
    send_tokens(1)
    picked = combine(0, grad_back)
    grad_two[0] = zc.run(z_scatter, picked)
    cot_received[1] = xc.run(dp_exchange, spread_cotangent, picked)
    experts_forward(1)
    send_back(1, partial, returned)
    gates(0)
    experts_backward(1)
    middle(0)
    send_back(1, grad_in, grad_back, grad_mixed[0])
    expert_out[1] = zc.run(z_scatter, combine(1, returned))
    push, sums = attention_back(0)
    part = push()
    acc_up = tc.run(
        lambda v: weight_grads([v[0], v[1]], [v[2], v[3]]),
        (received[0], received[1], upact[0], upact[1]),
    )
    grad_two[1] = zc.run(z_scatter, combine(1, grad_back))
    grad_one[0] = zc.run(z_scatter, part)
    gates(1)
    gain_acc[0], qkv_acc[0] = sums(part)
    acc_down = tc.run(
        lambda v: weight_grads([v[0], v[1]], [v[2], v[3]]),
        (hidden[0], hidden[1], grad_expert[0], grad_expert[1]),
    )
    middle(1)
    acc_out = (outs_acc[0] + outs_acc[1]).astype(BF16)
    acc_out = acc_out.reshape(model_width, dp_count, -1).transpose(1, 0, 2)
    acc_out = xc.run(dp_exchange, acc_out)
    push, sums = attention_back(1)
    part = push()
    grad_one[1] = zc.run(z_scatter, part)
    gain_acc[1], qkv_acc[1] = sums(part)
    acc_qkv = (qkv_acc[0] + qkv_acc[1]).astype(BF16)
    gains = jnp.concatenate([gain_two[0] + gain_two[1], gain_acc[0] + gain_acc[1]])
    table = jnp.concatenate([routers[0] + routers[1], gains])
    table = tc.run(table_sum, table)
    acc_qkv = xc.run(dp_exchange, acc_qkv.reshape(dp_count, -1, 3 * local_width), table)
    acc_out = tc.run(
        lambda v: jnp.sum(v.astype(F32), 0).astype(BF16).reshape((tensor_count,) + w_out.shape),
        acc_out,
    )
    grad_out_shard = jnp.sum(tc.run(out_swap, acc_out).astype(F32), 0)
    finish(0)
    router_sum, gain_sum = table[:experts_all], table[experts_all:]
    grad_qkv_shard = jnp.sum(acc_qkv.astype(F32), 0).reshape(w_qkv.shape)
    finish(1)
    return (
        jnp.stack([final_rows[m] for m in micros])[:, None],
        jnp.stack([grad_rows[m] for m in micros])[:, None],
        gain_sum[2],
        gain_sum[3],
        grad_qkv_shard,
        grad_out_shard,
        gain_sum[0],
        gain_sum[1],
        router_sum.T,
        acc_up,
        acc_down,
    )


def solution(mesh):
    return jax.shard_map(
        shards,
        mesh=mesh,
        in_specs=(
            P(None, "dp", "tensor", None),
            P(None, "dp", None),
            P(None, "dp", None, None),
            P(None, "dp", "tensor", None),
            P(),
            P(),
            P("dp", None, "tensor"),
            P("tensor", "dp"),
            P(),
            P(),
            P(),
            P("dp", None, "tensor"),
            P("dp", "tensor", None),
        ),
        out_specs=(
            P(None, "dp", "tensor", None),
            P(None, "dp", "tensor", None),
            P(),
            P(),
            P("dp", None, "tensor"),
            P("tensor", "dp"),
            P(),
            P(),
            P(),
            P("dp", None, "tensor"),
            P("dp", "tensor", None),
        ),
        check_vma=False,
    )
```

```python
import functools

import jax
import jax.numpy as jnp
from jax import lax
from jax.experimental import pallas as pl
from jax.experimental.pallas import tpu as pltpu
from jax.sharding import PartitionSpec as P

HEAD_DIM = 64
LANES = 128
BLOCK = 256
EPSILON = 1e-05
MASKED_SCORE = -1e30
F32 = jnp.float32
BF16 = jnp.bfloat16
NT = (((1,), (1,)), ((), ()))
TN = (((0,), (0,)), ((), ()))
BUSY = 1.15e9
VMEM_LIMIT = 60 * 1024 * 1024


def busy(micros):
    return pl.CostEstimate(flops=int(micros * BUSY), bytes_accessed=1024, transcendentals=0)


def norm_parts(stream):
    centre = stream - jnp.mean(stream, -1, keepdims=True)
    inv_std = lax.rsqrt(jnp.mean(centre * centre, -1, keepdims=True) + EPSILON)
    return centre * inv_std, inv_std


def norm_backward(grad_normed, normed, inv_std, gain_vec):
    grad_hat = grad_normed * gain_vec
    mean_grad = jnp.mean(grad_hat, -1, keepdims=True)
    mean_cross = jnp.mean(grad_hat * normed, -1, keepdims=True)
    return inv_std * (grad_hat - mean_grad - normed * mean_cross)


def dot32(a, b):
    return jnp.dot(a, b, preferred_element_type=F32)


def head_masks(rows):
    lane = lax.broadcasted_iota(jnp.int32, (rows, LANES), 1)
    return [(lane // HEAD_DIM) == h for h in range(LANES // HEAD_DIM)]


def exp_rows(scores):
    row_max = jnp.max(scores, -1, keepdims=True)
    return jnp.exp(scores - row_max)


def attend_kernel(seg_col, seg_row, q_ref, k_ref, v_ref, o_ref, *, length, scaling):
    masks = head_masks(BLOCK)
    for i in range(length // BLOCK):
        lo, hi = i * BLOCK, min(length, (i + 2) * BLOCK)
        rows = pl.ds(lo, BLOCK)
        visible = seg_row[:, lo:hi] <= seg_col[rows, :]
        q = q_ref[rows, :]
        outs = []
        for mask in masks:
            qm = jnp.where(mask, q * scaling, 0).astype(BF16)
            near = lax.dot_general(qm, k_ref[lo:hi, :], NT, preferred_element_type=F32)
            near = jnp.where(visible, near, MASKED_SCORE)
            top = jnp.max(near, -1, keepdims=True)
            if i:
                far = lax.dot_general(qm, k_ref[0:lo, :], NT, preferred_element_type=F32)
                top = jnp.maximum(top, jnp.max(far, -1, keepdims=True))
            near = jnp.exp(near - top)
            total = jnp.sum(near, -1, keepdims=True)
            if i:
                far = jnp.exp(far - top)
                total = total + jnp.sum(far, -1, keepdims=True)
            inv = 1.0 / total
            out = dot32((near * inv).astype(BF16), v_ref[lo:hi, :])
            if i:
                out = out + dot32((far * inv).astype(BF16), v_ref[0:lo, :])
            outs.append(out)
        acc = outs[0]
        for mask, out in zip(masks[1:], outs[1:]):
            acc = jnp.where(mask, out, acc)
        o_ref[rows, :] = acc.astype(BF16)


def attend(qkv, seg_col, seg_row, scaling):
    length, width = qkv.shape[0], qkv.shape[1] // 3
    pairs = width // LANES

    def part(c):
        return pl.BlockSpec((length, LANES), lambda j, c=c: (0, c * pairs + j))

    return pl.pallas_call(
        functools.partial(attend_kernel, length=length, scaling=scaling),
        grid=(pairs,),
        out_shape=jax.ShapeDtypeStruct((length, width), BF16),
        in_specs=[
            pl.BlockSpec((length, 1), lambda j: (0, 0)),
            pl.BlockSpec((1, length), lambda j: (0, 0)),
            part(0),
            part(1),
            part(2),
        ],
        out_specs=pl.BlockSpec((length, LANES), lambda j: (0, j)),
        compiler_params=pltpu.CompilerParams(vmem_limit_bytes=VMEM_LIMIT),
        cost_estimate=busy(11),
        name="attend",
    )(seg_col, seg_row, qkv, qkv, qkv)


def attend_back_kernel(
    seg_col, seg_row, q_ref, k_ref, v_ref, g_ref, o_ref, dk_ref, dv_ref, *, length, scaling, width
):
    pair = pl.program_id(0)
    masks = head_masks(BLOCK)
    key_t = jnp.transpose(k_ref[...])
    dk_ref[...] = jnp.zeros_like(dk_ref)
    dv_ref[...] = jnp.zeros_like(dv_ref)
    half = lax.broadcasted_iota(jnp.int32, (LANES, BLOCK), 0) // HEAD_DIM
    for i in range(length // BLOCK):
        lo, hi = i * BLOCK, min(length, (i + 2) * BLOCK)
        rows = pl.ds(lo, BLOCK)
        visible = seg_col[lo:hi, :] <= seg_row[:, rows]
        q, g = q_ref[rows, :], g_ref[rows, :]
        dq_t = None
        for h, mask in enumerate(masks):
            qm = jnp.where(mask, q * scaling, 0).astype(BF16)
            gm = jnp.where(mask, g, 0).astype(BF16)
            near = lax.dot_general(k_ref[lo:hi, :], qm, NT, preferred_element_type=F32)
            near = jnp.where(visible, near, MASKED_SCORE)
            top = jnp.max(near, 0, keepdims=True)
            if i:
                far = lax.dot_general(k_ref[0:lo, :], qm, NT, preferred_element_type=F32)
                top = jnp.maximum(top, jnp.max(far, 0, keepdims=True))
            near = jnp.exp(near - top)
            total = jnp.sum(near, 0, keepdims=True)
            if i:
                far = jnp.exp(far - top)
                total = total + jnp.sum(far, 0, keepdims=True)
            inv = 1.0 / total
            near = near * inv
            near_g = lax.dot_general(v_ref[lo:hi, :], gm, NT, preferred_element_type=F32)
            inner = jnp.sum(near * near_g, 0, keepdims=True)
            if i:
                far = far * inv
                far_g = lax.dot_general(v_ref[0:lo, :], gm, NT, preferred_element_type=F32)
                inner = inner + jnp.sum(far * far_g, 0, keepdims=True)
            near_s = (near * (near_g - inner)).astype(BF16)
            dv_ref[lo:hi, :] += dot32(near.astype(BF16), gm)
            dk_ref[lo:hi, :] += dot32(near_s, qm)
            dq = dot32(key_t[:, lo:hi], near_s)
            if i:
                far_s = (far * (far_g - inner)).astype(BF16)
                dv_ref[0:lo, :] += dot32(far.astype(BF16), gm)
                dk_ref[0:lo, :] += dot32(far_s, qm)
                dq = dq + dot32(key_t[:, 0:lo], far_s)
            dq_t = dq if dq_t is None else jnp.where(half == h, dq, dq_t)
        lanes = pl.ds(pl.multiple_of(pair * LANES, LANES), LANES)
        o_ref[rows, lanes] = (jnp.transpose(dq_t) * scaling).astype(BF16)
    for c, ref in ((1, dk_ref), (2, dv_ref)):
        lanes = pl.ds(pl.multiple_of(c * width + pair * LANES, LANES), LANES)
        o_ref[:, lanes] = ref[...].astype(BF16)


def attend_back(qkv, seg_col, seg_row, grad_mixed, scaling):
    length, width = qkv.shape[0], qkv.shape[1] // 3
    pairs = width // LANES

    def part(c):
        return pl.BlockSpec((length, LANES), lambda j, c=c: (0, c * pairs + j))

    return pl.pallas_call(
        functools.partial(attend_back_kernel, length=length, scaling=scaling, width=width),
        grid=(pairs,),
        out_shape=jax.ShapeDtypeStruct((length, 3 * width), BF16),
        in_specs=[
            pl.BlockSpec((length, 1), lambda j: (0, 0)),
            pl.BlockSpec((1, length), lambda j: (0, 0)),
            part(0),
            part(1),
            part(2),
            pl.BlockSpec((length, LANES), lambda j: (0, j)),
        ],
        out_specs=pl.BlockSpec((length, 3 * width), lambda j: (0, 0)),
        scratch_shapes=[pltpu.VMEM((length, LANES), F32)] * 2,
        compiler_params=pltpu.CompilerParams(vmem_limit_bytes=VMEM_LIMIT),
        cost_estimate=busy(18),
        name="attend_back",
    )(seg_col, seg_row, qkv, qkv, qkv, grad_mixed)


def residual_kernel(m_ref, w_ref, t_ref, g_ref, b_ref, s_ref, n_ref, *, groups):
    acc = t_ref[...].astype(F32)
    depth = m_ref.shape[2]
    for t in range(groups):
        acc = acc + dot32(m_ref[t], w_ref[t * depth : (t + 1) * depth, :])
    s_ref[...] = acc
    hat, unused = norm_parts(acc)
    n_ref[...] = (hat * g_ref[...] + b_ref[...]).astype(BF16)


def residual_norm(mixed_all, weight, tokens_all, gain, bias):
    groups, length, depth = mixed_all.shape
    width = weight.shape[1]
    rows = BLOCK
    return pl.pallas_call(
        functools.partial(residual_kernel, groups=groups),
        grid=(length // rows,),
        out_shape=(
            jax.ShapeDtypeStruct((length, width), F32),
            jax.ShapeDtypeStruct((length, width), BF16),
        ),
        in_specs=[
            pl.BlockSpec((groups, rows, depth), lambda i: (0, i, 0)),
            pl.BlockSpec((groups * depth, width), lambda i: (0, 0)),
            pl.BlockSpec((rows, width), lambda i: (i, 0)),
            pl.BlockSpec((1, width), lambda i: (0, 0)),
            pl.BlockSpec((1, width), lambda i: (0, 0)),
        ],
        out_specs=(
            pl.BlockSpec((rows, width), lambda i: (i, 0)),
            pl.BlockSpec((rows, width), lambda i: (i, 0)),
        ),
        compiler_params=pltpu.CompilerParams(vmem_limit_bytes=VMEM_LIMIT),
        cost_estimate=busy(7.5),
        name="residual_norm",
    )(mixed_all, weight, tokens_all, gain[None], bias[None])


def spread_kernel(d_ref, x_ref, o_ref):
    rows = o_ref.shape[0]
    slot = lax.broadcasted_iota(jnp.int32, (rows, d_ref.shape[1]), 0) + pl.program_id(0) * rows
    pick = jnp.where(slot == d_ref[...], 1.0, 0.0).astype(BF16)
    o_ref[...] = dot32(pick, x_ref[...]).astype(BF16)


def spread(dest_row, rows_in, slots):
    length, width = rows_in.shape
    block = 2 * BLOCK
    return pl.pallas_call(
        spread_kernel,
        grid=(slots // block,),
        out_shape=jax.ShapeDtypeStruct((slots, width), BF16),
        in_specs=[
            pl.BlockSpec((1, length), lambda i: (0, 0)),
            pl.BlockSpec((length, width), lambda i: (0, 0)),
        ],
        out_specs=pl.BlockSpec((block, width), lambda i: (i, 0)),
        compiler_params=pltpu.CompilerParams(vmem_limit_bytes=VMEM_LIMIT),
        cost_estimate=busy(6.4),
        name="spread",
    )(dest_row, rows_in)


def pick_kernel(d_ref, x_ref, o_ref):
    rows, slots = o_ref.shape[0], x_ref.shape[0]
    slot = lax.broadcasted_iota(jnp.int32, (rows, slots), 1)
    pick = jnp.where(slot == d_ref[...], 1.0, 0.0).astype(BF16)
    o_ref[...] = dot32(pick, x_ref[...]).astype(BF16)


def pick_rows(dest_col, rows_in, length):
    slots, width = rows_in.shape
    return pl.pallas_call(
        pick_kernel,
        grid=(length // BLOCK,),
        out_shape=jax.ShapeDtypeStruct((length, width), BF16),
        in_specs=[
            pl.BlockSpec((BLOCK, 1), lambda i: (i, 0)),
            pl.BlockSpec((slots, width), lambda i: (0, 0)),
        ],
        out_specs=pl.BlockSpec((BLOCK, width), lambda i: (i, 0)),
        compiler_params=pltpu.CompilerParams(vmem_limit_bytes=VMEM_LIMIT),
        cost_estimate=busy(7),
        name="pick_rows",
    )(dest_col, rows_in)


ROOT = 0.7978845608028654
CUBE = 0.044715


def expert_kernel(x_ref, u_ref, w_ref, o_ref, h_ref, s_ref, *, chunk):
    x = x_ref[...].reshape(-1, x_ref.shape[-1])
    rows, ffn = x.shape[0], u_ref.shape[2]
    acc = None
    for c in range(ffn // chunk):
        part = slice(c * chunk, (c + 1) * chunk)
        up = dot32(x, u_ref[0, :, part])
        square = up * up
        tanh = jnp.tanh(ROOT * (up + CUBE * (square * up)))
        half = 0.5 * (1.0 + tanh)
        hidden = (up * half).astype(BF16)
        slope = half + (0.5 * ROOT) * up * (1.0 - tanh * tanh) * (1.0 + (3.0 * CUBE) * square)
        h_ref[0, :, part] = hidden
        s_ref[0, :, part] = slope.astype(BF16)
        out = dot32(hidden, w_ref[0, part, :])
        acc = out if acc is None else acc + out
    o_ref[...] = acc.astype(BF16).reshape(o_ref.shape)


def expert_forward(received, w_up, w_down):
    sources, experts, capacity, width = received.shape
    rows, ffn = sources * capacity, w_up.shape[2]
    tile = pl.BlockSpec((sources, 1, capacity, width), lambda e: (0, e, 0, 0))
    flat = pl.BlockSpec((1, rows, ffn), lambda e: (e, 0, 0))
    return pl.pallas_call(
        functools.partial(expert_kernel, chunk=256),
        grid=(experts,),
        out_shape=(
            jax.ShapeDtypeStruct(received.shape, BF16),
            jax.ShapeDtypeStruct((experts, rows, ffn), BF16),
            jax.ShapeDtypeStruct((experts, rows, ffn), BF16),
        ),
        in_specs=[
            tile,
            pl.BlockSpec((1, width, ffn), lambda e: (e, 0, 0)),
            pl.BlockSpec((1, ffn, width), lambda e: (e, 0, 0)),
        ],
        out_specs=(tile, flat, flat),
        compiler_params=pltpu.CompilerParams(vmem_limit_bytes=VMEM_LIMIT),
        cost_estimate=busy(16),
        name="expert_forward",
    )(received, w_up, w_down)


def expert_back_kernel(x_ref, c_ref, r_ref, u_ref, w_ref, s_ref, o_ref, g_ref, e_ref, *, chunk, experts):
    first = lax.axis_index("dp") * experts + pl.program_id(0)
    x = x_ref[...].reshape(-1, x_ref.shape[-1])
    logits = dot32(x, r_ref[...])
    weights = exp_rows(logits)
    lane = lax.broadcasted_iota(jnp.int32, logits.shape, 1)
    chosen = jnp.sum(jnp.where(lane == first, weights, 0.0), -1, keepdims=True)
    gate = chosen / jnp.sum(weights, -1, keepdims=True)
    grad = (c_ref[...].reshape(x.shape).astype(F32) * gate).astype(BF16)
    e_ref[0] = grad
    acc = None
    for c in range(u_ref.shape[2] // chunk):
        part = slice(c * chunk, (c + 1) * chunk)
        hidden = lax.dot_general(grad, w_ref[0, part, :], NT, preferred_element_type=F32)
        upact = (hidden * s_ref[0, :, part].astype(F32)).astype(BF16)
        g_ref[0, :, part] = upact
        out = lax.dot_general(upact, u_ref[0, :, part], NT, preferred_element_type=F32)
        acc = out if acc is None else acc + out
    o_ref[...] = acc.astype(BF16).reshape(o_ref.shape)


def expert_backward(received, cot_received, router, w_up, w_down, slope):
    sources, experts, capacity, width = received.shape
    rows, ffn = sources * capacity, w_up.shape[2]
    tile = pl.BlockSpec((sources, 1, capacity, width), lambda e: (0, e, 0, 0))
    flat = pl.BlockSpec((1, rows, ffn), lambda e: (e, 0, 0))
    return pl.pallas_call(
        functools.partial(expert_back_kernel, chunk=256, experts=experts),
        grid=(experts,),
        out_shape=(
            jax.ShapeDtypeStruct(received.shape, BF16),
            jax.ShapeDtypeStruct((experts, rows, ffn), BF16),
            jax.ShapeDtypeStruct((experts, rows, width), BF16),
        ),
        in_specs=[
            tile,
            tile,
            pl.BlockSpec(router.shape, lambda e: (0, 0)),
            pl.BlockSpec((1, width, ffn), lambda e: (e, 0, 0)),
            pl.BlockSpec((1, ffn, width), lambda e: (e, 0, 0)),
            flat,
        ],
        out_specs=(tile, flat, pl.BlockSpec((1, rows, width), lambda e: (e, 0, 0))),
        compiler_params=pltpu.CompilerParams(vmem_limit_bytes=VMEM_LIMIT),
        cost_estimate=busy(17.5),
        name="expert_backward",
    )(received, cot_received, router, w_up, w_down, slope)


def weight_grad_kernel(*refs, count, chunk):
    lefts, rights, o_ref = refs[:count], refs[count : 2 * count], refs[2 * count]
    outs = o_ref.shape[1]

    @pl.loop(0, outs // chunk)
    def _(c):
        part = pl.ds(pl.multiple_of(c * chunk, chunk), chunk)
        acc = None
        for a_ref, b_ref in zip(lefts, rights):
            if len(a_ref.shape) == 4:
                a = a_ref[:, :, :, part].reshape(-1, chunk)
            else:
                a = a_ref[0, :, part]
            out = lax.dot_general(a, b_ref[0], TN, preferred_element_type=F32)
            acc = out if acc is None else acc + out
        o_ref[0, part, :] = acc


def weight_grads(lefts, rights):
    experts, rows, ncols = rights[0].shape
    mrows = lefts[0].shape[-1]

    def spec(a):
        if a.ndim == 4:
            return pl.BlockSpec((a.shape[0], 1, a.shape[2], a.shape[3]), lambda e: (0, e, 0, 0))
        return pl.BlockSpec((1,) + a.shape[1:], lambda e: (e, 0, 0))

    return pl.pallas_call(
        functools.partial(weight_grad_kernel, count=len(lefts), chunk=256),
        grid=(experts,),
        out_shape=jax.ShapeDtypeStruct((experts, mrows, ncols), F32),
        in_specs=[spec(a) for a in lefts] + [spec(b) for b in rights],
        out_specs=pl.BlockSpec((1, mrows, ncols), lambda e: (e, 0, 0)),
        compiler_params=pltpu.CompilerParams(vmem_limit_bytes=VMEM_LIMIT),
        cost_estimate=busy(16.4),
        name="weight_grads",
    )(*lefts, *rights)


def mid_kernel(t_ref, e_ref, h_ref, i_ref, c_ref, g_ref, w_ref, m_ref, s_ref, a_ref, k_ref):
    grad = t_ref[...].astype(F32) + e_ref[...]
    hat = h_ref[...]
    k_ref[0:1, :] = jnp.sum(grad * hat, 0, keepdims=True)
    k_ref[1:2, :] = jnp.sum(grad, 0, keepdims=True)
    stream = c_ref[...].astype(F32) + norm_backward(grad, hat, i_ref[...], g_ref[...])
    s_ref[...] = stream
    attn = stream.astype(BF16)
    a_ref[...] = attn
    width = m_ref.shape[2]
    for k in range(m_ref.shape[0]):
        part = w_ref[k * width : (k + 1) * width, :]
        m_ref[k] = lax.dot_general(attn, part, NT, preferred_element_type=F32).astype(BF16)


def middle_back(grad_two, extra, hat, inv, cot, gain, weight, groups):
    rows, width = grad_two.shape
    return pl.pallas_call(
        mid_kernel,
        out_shape=(
            jax.ShapeDtypeStruct((groups, rows, weight.shape[0] // groups), BF16),
            jax.ShapeDtypeStruct((rows, width), F32),
            jax.ShapeDtypeStruct((rows, width), BF16),
            jax.ShapeDtypeStruct((2, width), F32),
        ),
        compiler_params=pltpu.CompilerParams(vmem_limit_bytes=VMEM_LIMIT),
        cost_estimate=busy(5),
        name="middle_back",
    )(grad_two, extra, hat, inv, cot, gain[None], weight)


class Chain:
    def __init__(self, depth=1):
        self.depth, self.results = depth, []

    def run(self, step, operand, *more):
        more = more + tuple(self.results[: max(0, len(self.results) - self.depth + 1)][-1:])
        if more:
            operand, unused = lax.optimization_barrier((operand, more))
        result = step(operand)
        self.results.append(result)
        return result


def z_gather(rows):
    return lax.all_gather(rows, "tensor", axis=0, tiled=True)


def z_stack(rows):
    return lax.all_gather(rows, "tensor", axis=0, tiled=False)


def z_scatter(rows):
    return lax.psum_scatter(rows, "tensor", scatter_dimension=0, tiled=True)


def exchange(blocks, axis):
    return lax.all_to_all(blocks, axis, split_axis=0, concat_axis=0, tiled=True)


def dp_exchange(blocks):
    return exchange(blocks, "dp")


def gather_by_exchange(piece, axis):
    return exchange(jnp.broadcast_to(piece[None], (lax.axis_size(axis),) + piece.shape), axis)


def mesh_copy(src, dst, send, recv, axis, peer):
    return pltpu.make_async_remote_copy(
        src_ref=src,
        dst_ref=dst,
        send_sem=send,
        recv_sem=recv,
        device_id={axis: peer},
        device_id_type=pl.DeviceIdType.MESH,
    )


def greet(peers):
    barrier = pltpu.get_barrier_semaphore()
    for axis, peer in peers:
        pl.semaphore_signal(
            barrier, inc=1, device_id={axis: peer}, device_id_type=pl.DeviceIdType.MESH
        )
    pl.semaphore_wait(barrier, len(peers))


def other_peers(axis, count):
    me = lax.axis_index(axis)
    return [lax.rem(me + k, count) for k in range(1, count)]


def z_swap_kernel(x_ref, o_ref, send, recv, *, count):
    me = lax.axis_index("tensor")
    peers = other_peers("tensor", count)
    greet([("tensor", p) for p in peers])
    copies = [
        mesh_copy(x_ref.at[p], o_ref.at[me], send.at[k], recv.at[k], "tensor", p)
        for k, p in enumerate(peers)
    ]
    for copy in copies:
        copy.start()
    o_ref[me] = x_ref[me]
    for copy in copies:
        copy.wait()


def z_swap(blocks, number=1, micros=14):
    count = blocks.shape[0]
    whole = pl.BlockSpec(memory_space=pltpu.VMEM)
    return pl.pallas_call(
        functools.partial(z_swap_kernel, count=count),
        out_shape=jax.ShapeDtypeStruct(blocks.shape, blocks.dtype),
        in_specs=[whole],
        out_specs=whole,
        scratch_shapes=[pltpu.SemaphoreType.DMA((count - 1,))] * 2,
        compiler_params=pltpu.CompilerParams(collective_id=number, has_side_effects=True),
        cost_estimate=busy(micros),
        name="z_swap",
    )(blocks)


def tree_sum(ref, count):
    total = ref[0]
    for k in range(1, count):
        total = total + ref[k]
    return total


def table_sum_kernel(
    x_ref, b_ref, o_ref, p_ref, zin, mid, din, zs, zr, ds, dr, es, er, fs, fr, bs, br, *, zn, dn
):
    z, d = lax.axis_index("tensor"), lax.axis_index("dp")
    zp, dp = other_peers("tensor", zn), other_peers("dp", dn)
    greet([("tensor", p) for p in zp] + [("dp", p) for p in dp])

    def run(copies):
        for copy in copies:
            copy.start()
        return copies

    def settle(copies):
        for copy in copies:
            copy.wait()

    first = run(
        [mesh_copy(x_ref.at[p], zin.at[z], zs.at[k], zr.at[k], "tensor", p) for k, p in enumerate(zp)]
    )
    blocks = run(
        [mesh_copy(b_ref.at[p], p_ref.at[z], bs.at[k], br.at[k], "tensor", p) for k, p in enumerate(zp)]
    )
    p_ref[z] = b_ref[z]
    zin[z] = x_ref[z]
    settle(first)
    mid[...] = tree_sum(zin, zn)
    second = run(
        [mesh_copy(mid.at[p], din.at[d], ds.at[k], dr.at[k], "dp", p) for k, p in enumerate(dp)]
    )
    din[d] = mid[d]
    settle(second)
    o_ref[z, d] = tree_sum(din, dn)
    third = run(
        [
            mesh_copy(o_ref.at[z, d], o_ref.at[z, d], es.at[k], er.at[k], "dp", p)
            for k, p in enumerate(dp)
        ]
    )
    settle(third)
    fourth = run(
        [mesh_copy(o_ref.at[z], o_ref.at[z], fs.at[k], fr.at[k], "tensor", p) for k, p in enumerate(zp)]
    )
    settle(fourth)
    settle(blocks)


def table_sum(values, blocks):
    zn, dn = lax.axis_size("tensor"), lax.axis_size("dp")
    rows, width = values.shape
    depth = -(-values.size // (zn * dn * LANES))
    flat = jnp.pad(values.reshape(-1), (0, zn * dn * depth * LANES - values.size))
    shape = (zn, dn, depth, LANES)
    whole = pl.BlockSpec(memory_space=pltpu.VMEM)
    sems = [pltpu.SemaphoreType.DMA((n - 1,)) for n in (zn, zn, dn, dn, dn, dn, zn, zn, zn, zn)]
    total, swapped = pl.pallas_call(
        functools.partial(table_sum_kernel, zn=zn, dn=dn),
        out_shape=(
            jax.ShapeDtypeStruct(shape, F32),
            jax.ShapeDtypeStruct(blocks.shape, blocks.dtype),
        ),
        in_specs=[whole, whole],
        out_specs=(whole, whole),
        scratch_shapes=[
            pltpu.VMEM(shape, F32),
            pltpu.VMEM(shape[1:], F32),
            pltpu.VMEM(shape[1:], F32),
        ]
        + sems,
        compiler_params=pltpu.CompilerParams(collective_id=2, has_side_effects=True),
        cost_estimate=busy(15),
        name="table_sum",
    )(flat.reshape(shape), blocks)
    return total.reshape(-1)[: values.size].reshape(rows, width), swapped


def shards(
    tokens,
    block_ids,
    routes,
    cotangent,
    ln1_gain,
    ln1_bias,
    w_qkv,
    w_out,
    ln2_gain,
    ln2_bias,
    router,
    w_up,
    w_down,
):
    micro_count, unused, rows_dev, model_width = tokens.shape
    length = routes.shape[2]
    local_experts = w_up.shape[0]
    experts_all = router.shape[1]
    dp_count = lax.axis_size("dp")
    tensor_count = lax.axis_size("tensor")
    capacity = -(-(3 * length // (2 * experts_all)) // 16) * 16
    slots = experts_all * capacity
    scaling = HEAD_DIM ** (-0.5)
    local_width = w_qkv.shape[2]
    first_row = lax.axis_index("tensor") * rows_dev
    expert_range = jnp.arange(experts_all, dtype=jnp.int32)
    micros = range(micro_count)

    def own(rows):
        return lax.dynamic_slice_in_dim(rows, first_row, rows_dev)

    zc, tc, xc = Chain(), Chain(), Chain()
    qkv_flat = xc.run(lambda v: gather_by_exchange(v, "dp"), w_qkv.reshape(-1, 3 * local_width))
    qkv_flat = qkv_flat.reshape(model_width, 3 * local_width)
    out_parts = xc.run(lambda v: gather_by_exchange(v, "tensor"), w_out)
    out_parts = xc.run(lambda v: gather_by_exchange(v, "dp"), out_parts)
    out_matrix = out_parts.transpose(1, 2, 0, 3).reshape(model_width, model_width)

    dest_rows, dest_cols, seg_rows, seg_cols = [], [], [], []
    before = (
        jnp.arange(length, dtype=jnp.int32)[:, None] > jnp.arange(length, dtype=jnp.int32)[None, :]
    ).astype(BF16)
    for m in micros:
        ids = routes[m, 0]
        onehot = (ids == expert_range[None, :]).astype(BF16)
        place = jnp.sum(dot32(before, onehot) * onehot.astype(F32), 1).astype(jnp.int32)
        dest = ids[:, 0] * capacity + place
        dest_rows.append(dest[None, :])
        dest_cols.append(dest[:, None])
        seg_rows.append(block_ids[m])
        seg_cols.append(block_ids[m, 0][:, None])

    def to_blocks(rows):
        return rows.reshape(dp_count, local_experts, capacity, model_width)

    tokens_all, cot_all, whole_one, qkv, mixed = {}, {}, {}, {}, {}
    mixed_all, stream_all, whole_two = {}, {}, {}
    cot_received, received, hidden, slope, upact, grad_expert = {}, {}, {}, {}, {}, {}
    returned, grad_back, expert_out, grad_two = {}, {}, {}, {}
    partial, grad_in = {}, {}
    grad_stream, grad_mixed, grad_one, final_rows, grad_rows = {}, {}, {}, {}, {}
    routers, gain_two, outs_acc, qkv_acc, gain_acc = {}, {}, {}, {}, {}

    def attention(m, *after):
        def step(rows):
            whole = (norm_parts(rows.astype(F32))[0] * ln1_gain + ln1_bias).astype(BF16)
            act = dot32(whole, qkv_flat).astype(BF16)
            return attend(act, seg_cols[m], seg_rows[m], scaling), whole, act

        mixed[m], whole_one[m], qkv[m] = tc.run(step, tokens_all[m], *after)

    def spread_rows(m):
        return tc.run(lambda v: to_blocks(spread(dest_rows[m], v, slots)), cot_all[m])

    def send_cotangent(m):
        cot_received[m] = xc.run(dp_exchange, spread_rows(m))

    def send_tokens(m):
        def step(v):
            stream, whole = residual_norm(v, out_matrix, tokens_all[m], ln2_gain, ln2_bias)
            return to_blocks(spread(dest_rows[m], whole, slots)), stream, whole

        blocks, stream_all[m], whole_two[m] = tc.run(step, mixed_all[m])
        received[m] = xc.run(dp_exchange, blocks)

    def experts_forward(m):
        partial[m], hidden[m], slope[m] = tc.run(
            lambda v: expert_forward(v, w_up, w_down), received[m]
        )

    def experts_backward(m):
        grad_in[m], upact[m], grad_expert[m] = tc.run(
            lambda v: expert_backward(v[0], v[1], router, w_up, w_down, v[2]),
            (received[m], cot_received[m], slope[m]),
        )

    def send_back(m, source, target, *after):
        target[m] = xc.run(dp_exchange, source[m], *after).reshape(slots, model_width)

    def combine(m, source):
        return tc.run(lambda v: pick_rows(dest_cols[m], v, length), source[m])

    extra, hats, invs = {}, {}, {}

    def gates(m):
        def step(v):
            eo, stream, whole = v
            stream_one = own(stream)
            hat_two, inv_two = norm_parts(stream_one)
            normed_two = own(whole)
            logits = dot32(normed_two, router)
            weights = exp_rows(logits)
            probs = weights / jnp.sum(weights, -1, keepdims=True)
            pick_table = (own(routes[m, 0]) == expert_range[None, :]).astype(F32)
            gate = jnp.sum(probs * pick_table, -1, keepdims=True)
            eo = eo.astype(F32)
            final = (stream_one + gate * eo).astype(BF16)
            grad_gate = jnp.sum(cotangent[m, 0].astype(F32) * eo, -1, keepdims=True)
            grad_logits = (gate * grad_gate * (pick_table - probs)).astype(BF16)
            more = lax.dot_general(grad_logits, router, NT, preferred_element_type=F32)
            grad_router = lax.dot_general(grad_logits, normed_two, TN, preferred_element_type=F32)
            return more, final, grad_router, hat_two, inv_two

        extra[m], final_rows[m], routers[m], hats[m], invs[m] = tc.run(
            step, (expert_out[m], stream_all[m], whole_two[m])
        )

    def middle(m):
        def step(v):
            return middle_back(
                v, extra[m], hats[m], invs[m], cotangent[m, 0], ln2_gain, out_matrix, tensor_count
            )

        gm, grad_stream[m], grad_attn, gain_two[m] = tc.run(step, grad_two[m])
        grad_mixed[m] = tc.run(z_swap, gm).reshape(length, local_width)

        def sums(v):
            mixed_own = lax.dynamic_slice_in_dim(v[0], first_row, rows_dev, axis=1)
            return jnp.einsum("trf,rd->tfd", mixed_own, v[1], preferred_element_type=F32)

        outs_acc[m] = tc.run(sums, (mixed_all[m], grad_attn))

    def attention_back(m):
        act = tc.run(
            lambda v: attend_back(qkv[m], seg_cols[m], seg_rows[m], v, scaling), grad_mixed[m]
        )

        def push(*after):
            return tc.run(
                lambda v: lax.dot_general(v, qkv_flat, NT, preferred_element_type=F32).astype(BF16),
                act,
                *after,
            )

        def sums(v):
            rows, cols, tok = v
            rows = rows.astype(F32)
            hat_one = norm_parts(tok.astype(F32))[0]
            gains = jnp.stack([jnp.sum(rows * hat_one, 0), jnp.sum(rows, 0)])
            return gains, lax.dot_general(whole_one[m], cols, TN, preferred_element_type=F32)

        return push, lambda part: tc.run(sums, (part, act, tokens_all[m]))

    def finish(m):
        grad = grad_one[m].astype(F32)
        hat_one, inv_one = norm_parts(tokens[m, 0].astype(F32))
        grad_rows[m] = grad_stream[m] + norm_backward(grad, hat_one, inv_one, ln1_gain)

    tokens_all[0] = zc.run(z_gather, tokens[0, 0])
    attention(0)
    mixed_all[0] = zc.run(z_stack, mixed[0])
    cot_all[0] = zc.run(z_gather, cotangent[0, 0])
    tokens_all[1] = zc.run(z_gather, tokens[1, 0])
    send_tokens(0)
    send_cotangent(0)
    experts_forward(0)
    send_back(0, partial, returned)
    cot_all[1] = zc.run(z_gather, cotangent[1, 0])
    attention(1, cot_received[0])
    mixed_all[1] = zc.run(z_stack, mixed[1])
    experts_backward(0)
    send_back(0, grad_in, grad_back)
    picked = combine(0, returned)
    expert_out[0] = zc.run(z_scatter, picked)
    spread_cotangent = spread_rows(1)
    send_tokens(1)
    picked = combine(0, grad_back)
    grad_two[0] = zc.run(z_scatter, picked)
    cot_received[1] = xc.run(dp_exchange, spread_cotangent, picked)
    experts_forward(1)
    send_back(1, partial, returned)
    gates(0)
    experts_backward(1)
    middle(0)
    send_back(1, grad_in, grad_back, grad_mixed[0])
    expert_out[1] = zc.run(z_scatter, combine(1, returned))
    push, sums = attention_back(0)
    part = push()
    acc_up = tc.run(
        lambda v: weight_grads([v[0], v[1]], [v[2], v[3]]),
        (received[0], received[1], upact[0], upact[1]),
    )
    grad_two[1] = zc.run(z_scatter, combine(1, grad_back))
    gates(1)
    gain_acc[0], qkv_acc[0] = sums(part)
    acc_down = tc.run(
        lambda v: weight_grads([v[0], v[1]], [v[2], v[3]]),
        (hidden[0], hidden[1], grad_expert[0], grad_expert[1]),
    )
    middle(1)
    grad_one[0] = zc.run(z_scatter, part, grad_mixed[1])
    acc_out = (outs_acc[0] + outs_acc[1]).astype(BF16)
    acc_out = acc_out.reshape(model_width, dp_count, -1).transpose(1, 0, 2)
    acc_out = xc.run(dp_exchange, acc_out)
    push, sums = attention_back(1)
    part = push(acc_out)
    grad_one[1] = zc.run(z_scatter, part)
    gain_acc[1], qkv_acc[1] = sums(part)
    acc_qkv = (qkv_acc[0] + qkv_acc[1]).astype(BF16)
    acc_qkv = xc.run(dp_exchange, acc_qkv.reshape(dp_count, -1, 3 * local_width))
    acc_out = tc.run(
        lambda v: jnp.sum(v.astype(F32), 0).astype(BF16).reshape((tensor_count,) + w_out.shape),
        acc_out,
    )
    gains = jnp.concatenate([gain_two[0] + gain_two[1], gain_acc[0] + gain_acc[1]])
    table = jnp.concatenate([routers[0] + routers[1], gains])
    table, acc_out = tc.run(lambda v: table_sum(v[0], v[1]), (table, acc_out))
    grad_out_shard = jnp.sum(acc_out.astype(F32), 0)
    finish(0)
    router_sum, gain_sum = table[:experts_all], table[experts_all:]
    grad_qkv_shard = jnp.sum(acc_qkv.astype(F32), 0).reshape(w_qkv.shape)
    finish(1)
    return (
        jnp.stack([final_rows[m] for m in micros])[:, None],
        jnp.stack([grad_rows[m] for m in micros])[:, None],
        gain_sum[2],
        gain_sum[3],
        grad_qkv_shard,
        grad_out_shard,
        gain_sum[0],
        gain_sum[1],
        router_sum.T,
        acc_up,
        acc_down,
    )


def solution(mesh):
    return jax.shard_map(
        shards,
        mesh=mesh,
        in_specs=(
            P(None, "dp", "tensor", None),
            P(None, "dp", None),
            P(None, "dp", None, None),
            P(None, "dp", "tensor", None),
            P(),
            P(),
            P("dp", None, "tensor"),
            P("tensor", "dp"),
            P(),
            P(),
            P(),
            P("dp", None, "tensor"),
            P("dp", "tensor", None),
        ),
        out_specs=(
            P(None, "dp", "tensor", None),
            P(None, "dp", "tensor", None),
            P(),
            P(),
            P("dp", None, "tensor"),
            P("tensor", "dp"),
            P(),
            P(),
            P(),
            P("dp", None, "tensor"),
            P("dp", "tensor", None),
        ),
        check_vma=False,
    )
```

```python
import functools

import jax
import jax.numpy as jnp
from jax import lax
from jax.experimental import pallas as pl
from jax.experimental.pallas import tpu as pltpu
from jax.sharding import PartitionSpec as P

HEAD_DIM = 64
LANES = 128
BLOCK = 256
EPSILON = 1e-05
MASKED_SCORE = -1e30
F32 = jnp.float32
BF16 = jnp.bfloat16
NT = (((1,), (1,)), ((), ()))
TN = (((0,), (0,)), ((), ()))
BUSY = 1.15e9
VMEM_LIMIT = 60 * 1024 * 1024


def busy(micros):
    return pl.CostEstimate(flops=int(micros * BUSY), bytes_accessed=1024, transcendentals=0)


def norm_parts(stream):
    centre = stream - jnp.mean(stream, -1, keepdims=True)
    inv_std = lax.rsqrt(jnp.mean(centre * centre, -1, keepdims=True) + EPSILON)
    return centre * inv_std, inv_std


def norm_backward(grad_normed, normed, inv_std, gain_vec):
    grad_hat = grad_normed * gain_vec
    mean_grad = jnp.mean(grad_hat, -1, keepdims=True)
    mean_cross = jnp.mean(grad_hat * normed, -1, keepdims=True)
    return inv_std * (grad_hat - mean_grad - normed * mean_cross)


def dot32(a, b):
    return jnp.dot(a, b, preferred_element_type=F32)


def head_masks(rows):
    lane = lax.broadcasted_iota(jnp.int32, (rows, LANES), 1)
    return [(lane // HEAD_DIM) == h for h in range(LANES // HEAD_DIM)]


def exp_rows(scores):
    row_max = jnp.max(scores, -1, keepdims=True)
    return jnp.exp(scores - row_max)


def attend_kernel(seg_col, seg_row, q_ref, k_ref, v_ref, o_ref, *, length, scaling):
    masks = head_masks(BLOCK)
    for i in range(length // BLOCK):
        lo, hi = i * BLOCK, min(length, (i + 2) * BLOCK)
        rows = pl.ds(lo, BLOCK)
        visible = seg_row[:, lo:hi] <= seg_col[rows, :]
        q = q_ref[rows, :]
        outs = []
        for mask in masks:
            qm = jnp.where(mask, q * scaling, 0).astype(BF16)
            near = lax.dot_general(qm, k_ref[lo:hi, :], NT, preferred_element_type=F32)
            near = jnp.where(visible, near, MASKED_SCORE)
            top = jnp.max(near, -1, keepdims=True)
            if i:
                far = lax.dot_general(qm, k_ref[0:lo, :], NT, preferred_element_type=F32)
                top = jnp.maximum(top, jnp.max(far, -1, keepdims=True))
            near = jnp.exp(near - top)
            total = jnp.sum(near, -1, keepdims=True)
            if i:
                far = jnp.exp(far - top)
                total = total + jnp.sum(far, -1, keepdims=True)
            inv = 1.0 / total
            out = dot32((near * inv).astype(BF16), v_ref[lo:hi, :])
            if i:
                out = out + dot32((far * inv).astype(BF16), v_ref[0:lo, :])
            outs.append(out)
        acc = outs[0]
        for mask, out in zip(masks[1:], outs[1:]):
            acc = jnp.where(mask, out, acc)
        o_ref[rows, :] = acc.astype(BF16)


def attend(qkv, seg_col, seg_row, scaling):
    length, width = qkv.shape[0], qkv.shape[1] // 3
    pairs = width // LANES

    def part(c):
        return pl.BlockSpec((length, LANES), lambda j, c=c: (0, c * pairs + j))

    return pl.pallas_call(
        functools.partial(attend_kernel, length=length, scaling=scaling),
        grid=(pairs,),
        out_shape=jax.ShapeDtypeStruct((length, width), BF16),
        in_specs=[
            pl.BlockSpec((length, 1), lambda j: (0, 0)),
            pl.BlockSpec((1, length), lambda j: (0, 0)),
            part(0),
            part(1),
            part(2),
        ],
        out_specs=pl.BlockSpec((length, LANES), lambda j: (0, j)),
        compiler_params=pltpu.CompilerParams(vmem_limit_bytes=VMEM_LIMIT),
        cost_estimate=busy(11),
        name="attend",
    )(seg_col, seg_row, qkv, qkv, qkv)


def attend_back_kernel(
    seg_col, seg_row, q_ref, k_ref, v_ref, g_ref, o_ref, dk_ref, dv_ref, *, length, scaling, width
):
    pair = pl.program_id(0)
    masks = head_masks(BLOCK)
    key_t = jnp.transpose(k_ref[...])
    dk_ref[...] = jnp.zeros_like(dk_ref)
    dv_ref[...] = jnp.zeros_like(dv_ref)
    half = lax.broadcasted_iota(jnp.int32, (LANES, BLOCK), 0) // HEAD_DIM
    for i in range(length // BLOCK):
        lo, hi = i * BLOCK, min(length, (i + 2) * BLOCK)
        rows = pl.ds(lo, BLOCK)
        visible = seg_col[lo:hi, :] <= seg_row[:, rows]
        q, g = q_ref[rows, :], g_ref[rows, :]
        dq_t = None
        for h, mask in enumerate(masks):
            qm = jnp.where(mask, q * scaling, 0).astype(BF16)
            gm = jnp.where(mask, g, 0).astype(BF16)
            near = lax.dot_general(k_ref[lo:hi, :], qm, NT, preferred_element_type=F32)
            near = jnp.where(visible, near, MASKED_SCORE)
            top = jnp.max(near, 0, keepdims=True)
            if i:
                far = lax.dot_general(k_ref[0:lo, :], qm, NT, preferred_element_type=F32)
                top = jnp.maximum(top, jnp.max(far, 0, keepdims=True))
            near = jnp.exp(near - top)
            total = jnp.sum(near, 0, keepdims=True)
            if i:
                far = jnp.exp(far - top)
                total = total + jnp.sum(far, 0, keepdims=True)
            inv = 1.0 / total
            near = near * inv
            near_g = lax.dot_general(v_ref[lo:hi, :], gm, NT, preferred_element_type=F32)
            inner = jnp.sum(near * near_g, 0, keepdims=True)
            if i:
                far = far * inv
                far_g = lax.dot_general(v_ref[0:lo, :], gm, NT, preferred_element_type=F32)
                inner = inner + jnp.sum(far * far_g, 0, keepdims=True)
            near_s = (near * (near_g - inner)).astype(BF16)
            dv_ref[lo:hi, :] += dot32(near.astype(BF16), gm)
            dk_ref[lo:hi, :] += dot32(near_s, qm)
            dq = dot32(key_t[:, lo:hi], near_s)
            if i:
                far_s = (far * (far_g - inner)).astype(BF16)
                dv_ref[0:lo, :] += dot32(far.astype(BF16), gm)
                dk_ref[0:lo, :] += dot32(far_s, qm)
                dq = dq + dot32(key_t[:, 0:lo], far_s)
            dq_t = dq if dq_t is None else jnp.where(half == h, dq, dq_t)
        lanes = pl.ds(pl.multiple_of(pair * LANES, LANES), LANES)
        o_ref[rows, lanes] = (jnp.transpose(dq_t) * scaling).astype(BF16)
    for c, ref in ((1, dk_ref), (2, dv_ref)):
        lanes = pl.ds(pl.multiple_of(c * width + pair * LANES, LANES), LANES)
        o_ref[:, lanes] = ref[...].astype(BF16)


def attend_back(qkv, seg_col, seg_row, grad_mixed, scaling):
    length, width = qkv.shape[0], qkv.shape[1] // 3
    pairs = width // LANES

    def part(c):
        return pl.BlockSpec((length, LANES), lambda j, c=c: (0, c * pairs + j))

    return pl.pallas_call(
        functools.partial(attend_back_kernel, length=length, scaling=scaling, width=width),
        grid=(pairs,),
        out_shape=jax.ShapeDtypeStruct((length, 3 * width), BF16),
        in_specs=[
            pl.BlockSpec((length, 1), lambda j: (0, 0)),
            pl.BlockSpec((1, length), lambda j: (0, 0)),
            part(0),
            part(1),
            part(2),
            pl.BlockSpec((length, LANES), lambda j: (0, j)),
        ],
        out_specs=pl.BlockSpec((length, 3 * width), lambda j: (0, 0)),
        scratch_shapes=[pltpu.VMEM((length, LANES), F32)] * 2,
        compiler_params=pltpu.CompilerParams(vmem_limit_bytes=VMEM_LIMIT),
        cost_estimate=busy(18),
        name="attend_back",
    )(seg_col, seg_row, qkv, qkv, qkv, grad_mixed)


def residual_kernel(m_ref, w_ref, t_ref, g_ref, b_ref, s_ref, n_ref, *, groups):
    acc = t_ref[...].astype(F32)
    depth = m_ref.shape[2]
    for t in range(groups):
        acc = acc + dot32(m_ref[t], w_ref[t * depth : (t + 1) * depth, :])
    s_ref[...] = acc
    hat, unused = norm_parts(acc)
    n_ref[...] = (hat * g_ref[...] + b_ref[...]).astype(BF16)


def residual_norm(mixed_all, weight, tokens_all, gain, bias):
    groups, length, depth = mixed_all.shape
    width = weight.shape[1]
    rows = BLOCK
    return pl.pallas_call(
        functools.partial(residual_kernel, groups=groups),
        grid=(length // rows,),
        out_shape=(
            jax.ShapeDtypeStruct((length, width), F32),
            jax.ShapeDtypeStruct((length, width), BF16),
        ),
        in_specs=[
            pl.BlockSpec((groups, rows, depth), lambda i: (0, i, 0)),
            pl.BlockSpec((groups * depth, width), lambda i: (0, 0)),
            pl.BlockSpec((rows, width), lambda i: (i, 0)),
            pl.BlockSpec((1, width), lambda i: (0, 0)),
            pl.BlockSpec((1, width), lambda i: (0, 0)),
        ],
        out_specs=(
            pl.BlockSpec((rows, width), lambda i: (i, 0)),
            pl.BlockSpec((rows, width), lambda i: (i, 0)),
        ),
        compiler_params=pltpu.CompilerParams(vmem_limit_bytes=VMEM_LIMIT),
        cost_estimate=busy(7.5),
        name="residual_norm",
    )(mixed_all, weight, tokens_all, gain[None], bias[None])


def spread_kernel(d_ref, x_ref, o_ref):
    rows = o_ref.shape[0]
    slot = lax.broadcasted_iota(jnp.int32, (rows, d_ref.shape[1]), 0) + pl.program_id(0) * rows
    pick = jnp.where(slot == d_ref[...], 1.0, 0.0).astype(BF16)
    o_ref[...] = dot32(pick, x_ref[...]).astype(BF16)


def spread(dest_row, rows_in, slots):
    length, width = rows_in.shape
    block = 2 * BLOCK
    return pl.pallas_call(
        spread_kernel,
        grid=(slots // block,),
        out_shape=jax.ShapeDtypeStruct((slots, width), BF16),
        in_specs=[
            pl.BlockSpec((1, length), lambda i: (0, 0)),
            pl.BlockSpec((length, width), lambda i: (0, 0)),
        ],
        out_specs=pl.BlockSpec((block, width), lambda i: (i, 0)),
        compiler_params=pltpu.CompilerParams(vmem_limit_bytes=VMEM_LIMIT),
        cost_estimate=busy(6.4),
        name="spread",
    )(dest_row, rows_in)


def pick_kernel(d_ref, x_ref, o_ref):
    rows, slots = o_ref.shape[0], x_ref.shape[0]
    slot = lax.broadcasted_iota(jnp.int32, (rows, slots), 1)
    pick = jnp.where(slot == d_ref[...], 1.0, 0.0).astype(BF16)
    o_ref[...] = dot32(pick, x_ref[...]).astype(BF16)


def pick_rows(dest_col, rows_in, length):
    slots, width = rows_in.shape
    return pl.pallas_call(
        pick_kernel,
        grid=(length // BLOCK,),
        out_shape=jax.ShapeDtypeStruct((length, width), BF16),
        in_specs=[
            pl.BlockSpec((BLOCK, 1), lambda i: (i, 0)),
            pl.BlockSpec((slots, width), lambda i: (0, 0)),
        ],
        out_specs=pl.BlockSpec((BLOCK, width), lambda i: (i, 0)),
        compiler_params=pltpu.CompilerParams(vmem_limit_bytes=VMEM_LIMIT),
        cost_estimate=busy(7),
        name="pick_rows",
    )(dest_col, rows_in)


ROOT = 0.7978845608028654
CUBE = 0.044715


def expert_kernel(x_ref, u_ref, w_ref, o_ref, h_ref, s_ref, *, chunk):
    x = x_ref[...].reshape(-1, x_ref.shape[-1])
    rows, ffn = x.shape[0], u_ref.shape[2]
    acc = None
    for c in range(ffn // chunk):
        part = slice(c * chunk, (c + 1) * chunk)
        up = dot32(x, u_ref[0, :, part])
        square = up * up
        tanh = jnp.tanh(ROOT * (up + CUBE * (square * up)))
        half = 0.5 * (1.0 + tanh)
        hidden = (up * half).astype(BF16)
        slope = half + (0.5 * ROOT) * up * (1.0 - tanh * tanh) * (1.0 + (3.0 * CUBE) * square)
        h_ref[0, :, part] = hidden
        s_ref[0, :, part] = slope.astype(BF16)
        out = dot32(hidden, w_ref[0, part, :])
        acc = out if acc is None else acc + out
    o_ref[...] = acc.astype(BF16).reshape(o_ref.shape)


def expert_forward(received, w_up, w_down):
    sources, experts, capacity, width = received.shape
    rows, ffn = sources * capacity, w_up.shape[2]
    tile = pl.BlockSpec((sources, 1, capacity, width), lambda e: (0, e, 0, 0))
    flat = pl.BlockSpec((1, rows, ffn), lambda e: (e, 0, 0))
    return pl.pallas_call(
        functools.partial(expert_kernel, chunk=256),
        grid=(experts,),
        out_shape=(
            jax.ShapeDtypeStruct(received.shape, BF16),
            jax.ShapeDtypeStruct((experts, rows, ffn), BF16),
            jax.ShapeDtypeStruct((experts, rows, ffn), BF16),
        ),
        in_specs=[
            tile,
            pl.BlockSpec((1, width, ffn), lambda e: (e, 0, 0)),
            pl.BlockSpec((1, ffn, width), lambda e: (e, 0, 0)),
        ],
        out_specs=(tile, flat, flat),
        compiler_params=pltpu.CompilerParams(vmem_limit_bytes=VMEM_LIMIT),
        cost_estimate=busy(16),
        name="expert_forward",
    )(received, w_up, w_down)


def expert_back_kernel(x_ref, c_ref, r_ref, u_ref, w_ref, s_ref, o_ref, g_ref, e_ref, *, chunk, experts):
    first = lax.axis_index("dp") * experts + pl.program_id(0)
    x = x_ref[...].reshape(-1, x_ref.shape[-1])
    logits = dot32(x, r_ref[...])
    weights = exp_rows(logits)
    lane = lax.broadcasted_iota(jnp.int32, logits.shape, 1)
    chosen = jnp.sum(jnp.where(lane == first, weights, 0.0), -1, keepdims=True)
    gate = chosen / jnp.sum(weights, -1, keepdims=True)
    grad = (c_ref[...].reshape(x.shape).astype(F32) * gate).astype(BF16)
    e_ref[0] = grad
    acc = None
    for c in range(u_ref.shape[2] // chunk):
        part = slice(c * chunk, (c + 1) * chunk)
        hidden = lax.dot_general(grad, w_ref[0, part, :], NT, preferred_element_type=F32)
        upact = (hidden * s_ref[0, :, part].astype(F32)).astype(BF16)
        g_ref[0, :, part] = upact
        out = lax.dot_general(upact, u_ref[0, :, part], NT, preferred_element_type=F32)
        acc = out if acc is None else acc + out
    o_ref[...] = acc.astype(BF16).reshape(o_ref.shape)


def expert_backward(received, cot_received, router, w_up, w_down, slope):
    sources, experts, capacity, width = received.shape
    rows, ffn = sources * capacity, w_up.shape[2]
    tile = pl.BlockSpec((sources, 1, capacity, width), lambda e: (0, e, 0, 0))
    flat = pl.BlockSpec((1, rows, ffn), lambda e: (e, 0, 0))
    return pl.pallas_call(
        functools.partial(expert_back_kernel, chunk=256, experts=experts),
        grid=(experts,),
        out_shape=(
            jax.ShapeDtypeStruct(received.shape, BF16),
            jax.ShapeDtypeStruct((experts, rows, ffn), BF16),
            jax.ShapeDtypeStruct((experts, rows, width), BF16),
        ),
        in_specs=[
            tile,
            tile,
            pl.BlockSpec(router.shape, lambda e: (0, 0)),
            pl.BlockSpec((1, width, ffn), lambda e: (e, 0, 0)),
            pl.BlockSpec((1, ffn, width), lambda e: (e, 0, 0)),
            flat,
        ],
        out_specs=(tile, flat, pl.BlockSpec((1, rows, width), lambda e: (e, 0, 0))),
        compiler_params=pltpu.CompilerParams(vmem_limit_bytes=VMEM_LIMIT),
        cost_estimate=busy(17.5),
        name="expert_backward",
    )(received, cot_received, router, w_up, w_down, slope)


def weight_grad_kernel(*refs, count, chunk):
    lefts, rights, o_ref = refs[:count], refs[count : 2 * count], refs[2 * count]
    outs = o_ref.shape[1]

    @pl.loop(0, outs // chunk)
    def _(c):
        part = pl.ds(pl.multiple_of(c * chunk, chunk), chunk)
        acc = None
        for a_ref, b_ref in zip(lefts, rights):
            if len(a_ref.shape) == 4:
                a = a_ref[:, :, :, part].reshape(-1, chunk)
            else:
                a = a_ref[0, :, part]
            out = lax.dot_general(a, b_ref[0], TN, preferred_element_type=F32)
            acc = out if acc is None else acc + out
        o_ref[0, part, :] = acc


def weight_grads(lefts, rights):
    experts, rows, ncols = rights[0].shape
    mrows = lefts[0].shape[-1]

    def spec(a):
        if a.ndim == 4:
            return pl.BlockSpec((a.shape[0], 1, a.shape[2], a.shape[3]), lambda e: (0, e, 0, 0))
        return pl.BlockSpec((1,) + a.shape[1:], lambda e: (e, 0, 0))

    return pl.pallas_call(
        functools.partial(weight_grad_kernel, count=len(lefts), chunk=256),
        grid=(experts,),
        out_shape=jax.ShapeDtypeStruct((experts, mrows, ncols), F32),
        in_specs=[spec(a) for a in lefts] + [spec(b) for b in rights],
        out_specs=pl.BlockSpec((1, mrows, ncols), lambda e: (e, 0, 0)),
        compiler_params=pltpu.CompilerParams(vmem_limit_bytes=VMEM_LIMIT),
        cost_estimate=busy(16.4),
        name="weight_grads",
    )(*lefts, *rights)


def mid_kernel(t_ref, e_ref, h_ref, i_ref, c_ref, g_ref, w_ref, m_ref, s_ref, a_ref, k_ref):
    grad = t_ref[...].astype(F32) + e_ref[...]
    hat = h_ref[...]
    k_ref[0:1, :] = jnp.sum(grad * hat, 0, keepdims=True)
    k_ref[1:2, :] = jnp.sum(grad, 0, keepdims=True)
    stream = c_ref[...].astype(F32) + norm_backward(grad, hat, i_ref[...], g_ref[...])
    s_ref[...] = stream
    attn = stream.astype(BF16)
    a_ref[...] = attn
    width = m_ref.shape[2]
    for k in range(m_ref.shape[0]):
        part = w_ref[k * width : (k + 1) * width, :]
        m_ref[k] = lax.dot_general(attn, part, NT, preferred_element_type=F32).astype(BF16)


def middle_back(grad_two, extra, hat, inv, cot, gain, weight, groups):
    rows, width = grad_two.shape
    return pl.pallas_call(
        mid_kernel,
        out_shape=(
            jax.ShapeDtypeStruct((groups, rows, weight.shape[0] // groups), BF16),
            jax.ShapeDtypeStruct((rows, width), F32),
            jax.ShapeDtypeStruct((rows, width), BF16),
            jax.ShapeDtypeStruct((2, width), F32),
        ),
        compiler_params=pltpu.CompilerParams(vmem_limit_bytes=VMEM_LIMIT),
        cost_estimate=busy(5),
        name="middle_back",
    )(grad_two, extra, hat, inv, cot, gain[None], weight)


class Chain:
    def __init__(self, depth=1):
        self.depth, self.results = depth, []

    def run(self, step, operand, *more):
        more = more + tuple(self.results[: max(0, len(self.results) - self.depth + 1)][-1:])
        if more:
            operand, unused = lax.optimization_barrier((operand, more))
        result = step(operand)
        self.results.append(result)
        return result


def z_gather(rows):
    return lax.all_gather(rows, "tensor", axis=0, tiled=True)


def z_stack(rows):
    return lax.all_gather(rows, "tensor", axis=0, tiled=False)


def z_scatter(rows):
    return lax.psum_scatter(rows, "tensor", scatter_dimension=0, tiled=True)


def exchange(blocks, axis):
    return lax.all_to_all(blocks, axis, split_axis=0, concat_axis=0, tiled=True)


def dp_exchange(blocks):
    return exchange(blocks, "dp")


def gather_by_exchange(piece, axis):
    return exchange(jnp.broadcast_to(piece[None], (lax.axis_size(axis),) + piece.shape), axis)


def mesh_copy(src, dst, send, recv, axis, peer):
    return pltpu.make_async_remote_copy(
        src_ref=src,
        dst_ref=dst,
        send_sem=send,
        recv_sem=recv,
        device_id={axis: peer},
        device_id_type=pl.DeviceIdType.MESH,
    )


def greet(peers):
    barrier = pltpu.get_barrier_semaphore()
    for axis, peer in peers:
        pl.semaphore_signal(
            barrier, inc=1, device_id={axis: peer}, device_id_type=pl.DeviceIdType.MESH
        )
    pl.semaphore_wait(barrier, len(peers))


def other_peers(axis, count):
    me = lax.axis_index(axis)
    return [lax.rem(me + k, count) for k in range(1, count)]


def z_swap_kernel(x_ref, o_ref, send, recv, *, count):
    me = lax.axis_index("tensor")
    peers = other_peers("tensor", count)
    greet([("tensor", p) for p in peers])
    copies = [
        mesh_copy(x_ref.at[p], o_ref.at[me], send.at[k], recv.at[k], "tensor", p)
        for k, p in enumerate(peers)
    ]
    for copy in copies:
        copy.start()
    o_ref[me] = x_ref[me]
    for copy in copies:
        copy.wait()


def z_swap(blocks, number=1, micros=14):
    count = blocks.shape[0]
    whole = pl.BlockSpec(memory_space=pltpu.VMEM)
    return pl.pallas_call(
        functools.partial(z_swap_kernel, count=count),
        out_shape=jax.ShapeDtypeStruct(blocks.shape, blocks.dtype),
        in_specs=[whole],
        out_specs=whole,
        scratch_shapes=[pltpu.SemaphoreType.DMA((count - 1,))] * 2,
        compiler_params=pltpu.CompilerParams(collective_id=number, has_side_effects=True),
        cost_estimate=busy(micros),
        name="z_swap",
    )(blocks)


def tree_sum(ref, count):
    total = ref[0]
    for k in range(1, count):
        total = total + ref[k]
    return total


def table_sum_kernel(
    x_ref, b_ref, o_ref, p_ref, zin, mid, din, zs, zr, ds, dr, es, er, fs, fr, bs, br, *, zn, dn
):
    z, d = lax.axis_index("tensor"), lax.axis_index("dp")
    zp, dp = other_peers("tensor", zn), other_peers("dp", dn)
    greet([("tensor", p) for p in zp] + [("dp", p) for p in dp])

    def run(copies):
        for copy in copies:
            copy.start()
        return copies

    def settle(copies):
        for copy in copies:
            copy.wait()

    first = run(
        [mesh_copy(x_ref.at[p], zin.at[z], zs.at[k], zr.at[k], "tensor", p) for k, p in enumerate(zp)]
    )
    blocks = run(
        [mesh_copy(b_ref.at[p], p_ref.at[z], bs.at[k], br.at[k], "tensor", p) for k, p in enumerate(zp)]
    )
    p_ref[z] = b_ref[z]
    zin[z] = x_ref[z]
    settle(first)
    mid[...] = tree_sum(zin, zn)
    second = run(
        [mesh_copy(mid.at[p], din.at[d], ds.at[k], dr.at[k], "dp", p) for k, p in enumerate(dp)]
    )
    din[d] = mid[d]
    settle(second)
    o_ref[z, d] = tree_sum(din, dn)
    third = run(
        [
            mesh_copy(o_ref.at[z, d], o_ref.at[z, d], es.at[k], er.at[k], "dp", p)
            for k, p in enumerate(dp)
        ]
    )
    settle(third)
    fourth = run(
        [mesh_copy(o_ref.at[z], o_ref.at[z], fs.at[k], fr.at[k], "tensor", p) for k, p in enumerate(zp)]
    )
    settle(fourth)
    settle(blocks)


def table_sum(values, blocks):
    zn, dn = lax.axis_size("tensor"), lax.axis_size("dp")
    rows, width = values.shape
    depth = -(-values.size // (zn * dn * LANES))
    flat = jnp.pad(values.reshape(-1), (0, zn * dn * depth * LANES - values.size))
    shape = (zn, dn, depth, LANES)
    whole = pl.BlockSpec(memory_space=pltpu.VMEM)
    sems = [pltpu.SemaphoreType.DMA((n - 1,)) for n in (zn, zn, dn, dn, dn, dn, zn, zn, zn, zn)]
    total, swapped = pl.pallas_call(
        functools.partial(table_sum_kernel, zn=zn, dn=dn),
        out_shape=(
            jax.ShapeDtypeStruct(shape, F32),
            jax.ShapeDtypeStruct(blocks.shape, blocks.dtype),
        ),
        in_specs=[whole, whole],
        out_specs=(whole, whole),
        scratch_shapes=[
            pltpu.VMEM(shape, F32),
            pltpu.VMEM(shape[1:], F32),
            pltpu.VMEM(shape[1:], F32),
        ]
        + sems,
        compiler_params=pltpu.CompilerParams(collective_id=2, has_side_effects=True),
        cost_estimate=busy(15),
        name="table_sum",
    )(flat.reshape(shape), blocks)
    return total.reshape(-1)[: values.size].reshape(rows, width), swapped


def shards(
    tokens,
    block_ids,
    routes,
    cotangent,
    ln1_gain,
    ln1_bias,
    w_qkv,
    w_out,
    ln2_gain,
    ln2_bias,
    router,
    w_up,
    w_down,
):
    micro_count, unused, rows_dev, model_width = tokens.shape
    length = routes.shape[2]
    local_experts = w_up.shape[0]
    experts_all = router.shape[1]
    dp_count = lax.axis_size("dp")
    tensor_count = lax.axis_size("tensor")
    capacity = -(-(3 * length // (2 * experts_all)) // 16) * 16
    slots = experts_all * capacity
    scaling = HEAD_DIM ** (-0.5)
    local_width = w_qkv.shape[2]
    first_row = lax.axis_index("tensor") * rows_dev
    expert_range = jnp.arange(experts_all, dtype=jnp.int32)
    micros = range(micro_count)

    def own(rows):
        return lax.dynamic_slice_in_dim(rows, first_row, rows_dev)

    zc, tc, xc = Chain(), Chain(), Chain()
    qkv_flat = xc.run(lambda v: gather_by_exchange(v, "dp"), w_qkv.reshape(-1, 3 * local_width))
    qkv_flat = qkv_flat.reshape(model_width, 3 * local_width)
    out_parts = xc.run(lambda v: gather_by_exchange(v, "tensor"), w_out)
    out_parts = xc.run(lambda v: gather_by_exchange(v, "dp"), out_parts)
    out_matrix = out_parts.transpose(1, 2, 0, 3).reshape(model_width, model_width)

    dest_rows, dest_cols, seg_rows, seg_cols = [], [], [], []
    before = (
        jnp.arange(length, dtype=jnp.int32)[:, None] > jnp.arange(length, dtype=jnp.int32)[None, :]
    ).astype(BF16)
    for m in micros:
        ids = routes[m, 0]
        onehot = (ids == expert_range[None, :]).astype(BF16)
        place = jnp.sum(dot32(before, onehot) * onehot.astype(F32), 1).astype(jnp.int32)
        dest = ids[:, 0] * capacity + place
        dest_rows.append(dest[None, :])
        dest_cols.append(dest[:, None])
        seg_rows.append(block_ids[m])
        seg_cols.append(block_ids[m, 0][:, None])

    def to_blocks(rows):
        return rows.reshape(dp_count, local_experts, capacity, model_width)

    tokens_all, cot_all, whole_one, qkv, mixed = {}, {}, {}, {}, {}
    mixed_all, stream_all, whole_two = {}, {}, {}
    cot_received, received, hidden, slope, upact, grad_expert = {}, {}, {}, {}, {}, {}
    returned, grad_back, expert_out, grad_two = {}, {}, {}, {}
    partial, grad_in = {}, {}
    grad_stream, grad_mixed, grad_one, final_rows, grad_rows = {}, {}, {}, {}, {}
    routers, gain_two, outs_acc, qkv_acc, gain_acc = {}, {}, {}, {}, {}

    def attention(m, *after):
        def step(rows):
            whole = (norm_parts(rows.astype(F32))[0] * ln1_gain + ln1_bias).astype(BF16)
            act = dot32(whole, qkv_flat).astype(BF16)
            return attend(act, seg_cols[m], seg_rows[m], scaling), whole, act

        mixed[m], whole_one[m], qkv[m] = tc.run(step, tokens_all[m], *after)

    def spread_rows(m):
        return tc.run(lambda v: to_blocks(spread(dest_rows[m], v, slots)), cot_all[m])

    def send_cotangent(m):
        cot_received[m] = xc.run(dp_exchange, spread_rows(m))

    def send_tokens(m):
        def step(v):
            stream, whole = residual_norm(v, out_matrix, tokens_all[m], ln2_gain, ln2_bias)
            return to_blocks(spread(dest_rows[m], whole, slots)), stream, whole

        blocks, stream_all[m], whole_two[m] = tc.run(step, mixed_all[m])
        received[m] = xc.run(dp_exchange, blocks)

    def experts_forward(m):
        partial[m], hidden[m], slope[m] = tc.run(
            lambda v: expert_forward(v, w_up, w_down), received[m]
        )

    def experts_backward(m):
        grad_in[m], upact[m], grad_expert[m] = tc.run(
            lambda v: expert_backward(v[0], v[1], router, w_up, w_down, v[2]),
            (received[m], cot_received[m], slope[m]),
        )

    def send_back(m, source, target, *after):
        target[m] = xc.run(dp_exchange, source[m], *after).reshape(slots, model_width)

    def combine(m, source):
        return tc.run(lambda v: pick_rows(dest_cols[m], v, length), source[m])

    extra, hats, invs = {}, {}, {}

    def gates(m):
        def step(v):
            eo, stream, whole = v
            stream_one = own(stream)
            hat_two, inv_two = norm_parts(stream_one)
            normed_two = own(whole)
            logits = dot32(normed_two, router)
            weights = exp_rows(logits)
            probs = weights / jnp.sum(weights, -1, keepdims=True)
            pick_table = (own(routes[m, 0]) == expert_range[None, :]).astype(F32)
            gate = jnp.sum(probs * pick_table, -1, keepdims=True)
            eo = eo.astype(F32)
            final = (stream_one + gate * eo).astype(BF16)
            grad_gate = jnp.sum(cotangent[m, 0].astype(F32) * eo, -1, keepdims=True)
            grad_logits = (gate * grad_gate * (pick_table - probs)).astype(BF16)
            more = lax.dot_general(grad_logits, router, NT, preferred_element_type=F32)
            grad_router = lax.dot_general(grad_logits, normed_two, TN, preferred_element_type=F32)
            return more, final, grad_router, hat_two, inv_two

        extra[m], final_rows[m], routers[m], hats[m], invs[m] = tc.run(
            step, (expert_out[m], stream_all[m], whole_two[m])
        )

    def middle(m):
        def step(v):
            return middle_back(
                v, extra[m], hats[m], invs[m], cotangent[m, 0], ln2_gain, out_matrix, tensor_count
            )

        gm, grad_stream[m], grad_attn, gain_two[m] = tc.run(step, grad_two[m])
        grad_mixed[m] = tc.run(z_swap, gm).reshape(length, local_width)

        def sums(v):
            mixed_own = lax.dynamic_slice_in_dim(v[0], first_row, rows_dev, axis=1)
            return jnp.einsum("trf,rd->tfd", mixed_own, v[1], preferred_element_type=F32)

        outs_acc[m] = tc.run(sums, (mixed_all[m], grad_attn))

    def attention_back(m):
        act = tc.run(
            lambda v: attend_back(qkv[m], seg_cols[m], seg_rows[m], v, scaling), grad_mixed[m]
        )

        def push(*after):
            return tc.run(
                lambda v: lax.dot_general(v, qkv_flat, NT, preferred_element_type=F32).astype(BF16),
                act,
                *after,
            )

        def sums(v):
            rows, cols, tok = v
            rows = rows.astype(F32)
            hat_one = norm_parts(tok.astype(F32))[0]
            gains = jnp.stack([jnp.sum(rows * hat_one, 0), jnp.sum(rows, 0)])
            return gains, lax.dot_general(whole_one[m], cols, TN, preferred_element_type=F32)

        return push, lambda part: tc.run(sums, (part, act, tokens_all[m]))

    def finish(m):
        grad = grad_one[m].astype(F32)
        hat_one, inv_one = norm_parts(tokens[m, 0].astype(F32))
        grad_rows[m] = grad_stream[m] + norm_backward(grad, hat_one, inv_one, ln1_gain)

    tokens_all[0] = zc.run(z_gather, tokens[0, 0])
    attention(0)
    mixed_all[0] = zc.run(z_stack, mixed[0])
    cot_all[0] = zc.run(z_gather, cotangent[0, 0], out_matrix)
    tokens_all[1] = zc.run(z_gather, tokens[1, 0])
    send_tokens(0)
    send_cotangent(0)
    experts_forward(0)
    send_back(0, partial, returned)
    cot_all[1] = zc.run(z_gather, cotangent[1, 0])
    attention(1, cot_received[0])
    mixed_all[1] = zc.run(z_stack, mixed[1])
    experts_backward(0)
    send_back(0, grad_in, grad_back)
    picked = combine(0, returned)
    expert_out[0] = zc.run(z_scatter, picked)
    spread_cotangent = spread_rows(1)
    send_tokens(1)
    picked = combine(0, grad_back)
    grad_two[0] = zc.run(z_scatter, picked)
    cot_received[1] = xc.run(dp_exchange, spread_cotangent, picked)
    experts_forward(1)
    send_back(1, partial, returned)
    gates(0)
    experts_backward(1)
    middle(0)
    send_back(1, grad_in, grad_back, grad_mixed[0])
    expert_out[1] = zc.run(z_scatter, combine(1, returned))
    push, sums = attention_back(0)
    part = push()
    acc_up = tc.run(
        lambda v: weight_grads([v[0], v[1]], [v[2], v[3]]),
        (received[0], received[1], upact[0], upact[1]),
    )
    grad_two[1] = zc.run(z_scatter, combine(1, grad_back))
    gates(1)
    gain_acc[0], qkv_acc[0] = sums(part)
    acc_down = tc.run(
        lambda v: weight_grads([v[0], v[1]], [v[2], v[3]]),
        (hidden[0], hidden[1], grad_expert[0], grad_expert[1]),
    )
    middle(1)
    grad_one[0] = zc.run(z_scatter, part, grad_mixed[1])
    acc_out = (outs_acc[0] + outs_acc[1]).astype(BF16)
    acc_out = acc_out.reshape(model_width, dp_count, -1).transpose(1, 0, 2)
    acc_out = xc.run(dp_exchange, acc_out)
    push, sums = attention_back(1)
    part = push(acc_out)
    grad_one[1] = zc.run(z_scatter, part)
    gain_acc[1], qkv_acc[1] = sums(part)
    acc_qkv = (qkv_acc[0] + qkv_acc[1]).astype(BF16)
    acc_qkv = xc.run(dp_exchange, acc_qkv.reshape(dp_count, -1, 3 * local_width))
    acc_out = tc.run(
        lambda v: jnp.sum(v.astype(F32), 0).astype(BF16).reshape((tensor_count,) + w_out.shape),
        acc_out,
    )
    gains = jnp.concatenate([gain_two[0] + gain_two[1], gain_acc[0] + gain_acc[1]])
    table = jnp.concatenate([routers[0] + routers[1], gains])
    table, acc_out = tc.run(lambda v: table_sum(v[0], v[1]), (table, acc_out))
    grad_out_shard = jnp.sum(acc_out.astype(F32), 0)
    finish(0)
    router_sum, gain_sum = table[:experts_all], table[experts_all:]
    grad_qkv_shard = jnp.sum(acc_qkv.astype(F32), 0).reshape(w_qkv.shape)
    finish(1)
    return (
        jnp.stack([final_rows[m] for m in micros])[:, None],
        jnp.stack([grad_rows[m] for m in micros])[:, None],
        gain_sum[2],
        gain_sum[3],
        grad_qkv_shard,
        grad_out_shard,
        gain_sum[0],
        gain_sum[1],
        router_sum.T,
        acc_up,
        acc_down,
    )


def solution(mesh):
    return jax.shard_map(
        shards,
        mesh=mesh,
        in_specs=(
            P(None, "dp", "tensor", None),
            P(None, "dp", None),
            P(None, "dp", None, None),
            P(None, "dp", "tensor", None),
            P(),
            P(),
            P("dp", None, "tensor"),
            P("tensor", "dp"),
            P(),
            P(),
            P(),
            P("dp", None, "tensor"),
            P("dp", "tensor", None),
        ),
        out_specs=(
            P(None, "dp", "tensor", None),
            P(None, "dp", "tensor", None),
            P(),
            P(),
            P("dp", None, "tensor"),
            P("tensor", "dp"),
            P(),
            P(),
            P(),
            P("dp", None, "tensor"),
            P("dp", "tensor", None),
        ),
        check_vma=False,
    )
```
